256 devices in a mesh: seq: 16 (over x, z_lo), mp: 4 (over y), dp: 4 (over z_hi, core).
Axes of the slice: x: 4, y: 4, z: 8 (z_hi: 2, z_lo: 4; z = z_hi * 4 + z_lo), core: 2. Of those that a mesh axis runs over, the one named last changes fastest.
Arguments:
- block_input: bfloat16 [4, 16384, 1280], P('dp', 'seq', 'mp'), may hold values from -6 to 6
- conv_weight: bfloat16 [5, 1280, 1536], P(None, None, 'mp'), as said below
- norm_gain: float32 [1536], P('mp'), may hold values from 0.1 to 1.9
- qkv_weight: bfloat16 [1536, 2560], P(None, 'mp'), may hold values from -0.15625 to 0.15625
- encoder_grad: bfloat16 [4, 8192, 1536], P('dp', 'seq', 'mp'), may hold values from -6 to 6
Outputs:
- qkv: bfloat16 [4, 8192, 2560], P('dp', 'seq', 'mp')
- conv_grad: float32 [1280, 5, 1536], P('seq', None, 'mp')
The draws below stay inside these ranges and needn't reach their ends.
Inputs may be any that keep to these rules, and one draw needn't show every extreme that they name: `conv_weight`: output channel o's kernel column carries a scale factor that varies with o; input channels differ in scale.
All inputs are finite; a program needn't handle non-finite values.
Results may differ from the reference program's by a relative error of at most 0.019.
Values may be sent and summed in bfloat16 or wider, within the bound.
A program may use at most 64 MiB of HBM per device.

```python
import jax
import jax.numpy as jnp
from jax import lax

CIN = 1280
COUT = 1536
KW = 5
QKVW = 2560
ROWS = 8192
LIN = 16384
BATCH = 4


def draw_conv_weight(key, part):
    k_base, k_rows, k_cols = jax.random.split(key, 3)
    base = jax.random.normal(k_base, (KW, CIN, COUT), jnp.float32)
    rows = jnp.exp(jax.random.uniform(k_rows, (1, CIN, 1), jnp.float32, 0.0, 2.302585))
    ramp = 3.0 ** (jnp.arange(COUT, dtype=jnp.float32) / COUT)
    cols = ramp.reshape(1, 1, COUT) * jnp.exp(jax.random.uniform(k_cols, (1, 1, COUT), jnp.float32, 0.0, 1.0986))
    weight = base * rows * cols / (5.0 * jnp.sqrt(jnp.float32(KW * CIN)))
    return weight.astype(jnp.bfloat16)


def shard_levels(rng, extent, pieces, least, high):
    gain, own = 1.0, jax.random.fold_in(rng, 6)
    for dim, parts in pieces:
        draws = jnp.exp(jax.random.uniform(jax.random.fold_in(own, dim), (parts,), jnp.float32, least / len(pieces), high / len(pieces)))
        gain = gain * jnp.repeat(draws, extent[dim] // parts).reshape([-1 if axis == dim else 1 for axis in range(len(extent))])
    return gain


def bell_draw(key, shape, scale, limit, cuts=(), held_as=jnp.bfloat16):
    values = scale * jax.random.normal(key, shape, jnp.float32)
    if cuts:
        values = values * shard_levels(key, shape, cuts, -0.22, 0.18)
    return jnp.clip(values, -limit, limit).astype(held_as)


def setup_inputs(seed: int = 0) -> dict:
    arg_keys = jax.random.split(jax.random.key(seed), 6)
    return {
        "block_input": bell_draw(arg_keys[0], (BATCH, LIN, CIN), 1.0, 6.0, ((0, 4), (1, 16), (2, 4))),
        "conv_weight": draw_conv_weight(jax.random.fold_in(arg_keys[5], 71), 0),
        "norm_gain": jnp.clip(1.0 + 0.18 * jax.random.normal(arg_keys[2], (COUT,), jnp.float32), 0.1, 1.9),
        "qkv_weight": bell_draw(arg_keys[3], (COUT, QKVW), COUT ** -0.5, 0.15625, ((1, 4),)),
        "encoder_grad": bell_draw(arg_keys[4], (BATCH, ROWS, COUT), 1.0, 6.0, ((0, 4), (1, 16), (2, 4))),
    }


def gelu_value(v):
    u = 0.7978845608 * (v + 0.044715 * v * v * v)
    return 0.5 * v * (1.0 + jnp.tanh(u))

def gelu_slope(v):
    u = 0.7978845608 * (v + 0.044715 * v * v * v)
    th = jnp.tanh(u)
    return 0.5 * (1.0 + th) + 0.5 * v * (1.0 - th * th) * 0.7978845608 * (1.0 + 0.134145 * v * v)

def one_sequence(inputs):
    seq_input, seq_grad, conv_weight, norm_gain, qkv_weight = inputs
    padded = jnp.pad(seq_input, ((2, 2), (0, 0)))
    length = seq_input.shape[0]
    pre = jnp.zeros((length, conv_weight.shape[2]), jnp.float32)
    for k in range(KW):
        pre = pre + jnp.dot(padded[k:k + length], conv_weight[k], preferred_element_type=jnp.float32)
    act = gelu_value(pre)
    encoded = (0.5 * (act[0::2] + act[1::2])).astype(jnp.bfloat16)
    values = encoded.astype(jnp.float32)
    mean = lax.optimization_barrier(jnp.sum(values, axis=1, keepdims=True)) / COUT
    meansq = lax.optimization_barrier(jnp.sum(values * values, axis=1, keepdims=True)) / COUT
    var = meansq - mean * mean
    normalized = ((values - mean) * lax.rsqrt(var + 1e-05) * norm_gain).astype(jnp.bfloat16)
    qkv = jnp.dot(normalized, qkv_weight, preferred_element_type=jnp.float32).astype(jnp.bfloat16)
    spread = jnp.repeat(seq_grad.astype(jnp.float32), 2, axis=0)
    pre_grad = (gelu_slope(pre) * 0.5 * spread).astype(jnp.bfloat16)
    terms = [lax.dot_general(padded[k:k + length], pre_grad, (((0,), (0,)), ((), ())), preferred_element_type=jnp.float32) for k in range(KW)]
    return (qkv, jnp.stack(terms, axis=1))

def reference(block_input, conv_weight, norm_gain, qkv_weight, encoder_grad):

    def step(carry, index):
        qkv, grad = one_sequence((block_input[index], encoder_grad[index], conv_weight, norm_gain, qkv_weight))
        return (carry + grad, qkv)
    start = jnp.zeros((CIN, KW, COUT), jnp.float32)
    conv_grad, qkv = lax.scan(step, start, jnp.arange(BATCH, dtype=jnp.int32))
    return (qkv, conv_grad)
```

```python
import jax
import jax.numpy as jnp
from jax import lax
from jax.experimental import pallas as pl
from jax.experimental.pallas import tpu as pltpu
from jax.sharding import PartitionSpec as P

MESH = pl.DeviceIdType.MESH
BF16, F32 = jnp.bfloat16, jnp.float32
KW = 5
T = 1024
R = 512
CB = 320
O = 384
OT = O // 128
C = 4 * CB
N = KW * O
W2 = 1024
Q = 640
TB = 256
NB = T // TB
XB = 320
ZB = 80
PIECE = 512
Y0 = 8

OWN_R, OWN_L, FWD_R, FWD_L = 0, 4, 8, 12
EDGE_UP, EDGE_DOWN, RIM, GAIN = 16, 17, 17, 20
ENC_R, ENC_L, EFWD_R, EFWD_L = 24, 26, 28, 29
SWAP = 30
X1R, X1L, X2R, X2L = 34, 35, 36, 38
ZUP, ZDN, DPG = 40, 44, 47
COPIES = 51


def kernel(
    xt_hbm, edge_hbm, w_hbm, gain_hbm, qw_hbm, eg_hbm, qkv_hbm, cg_hbm,
    xt, rim, wcat, gain, qw, eg, xrow, yb, pgb, pgcat, enc, norm, qout,
    psend, precv, gown, x1l, x1r, x2l, x2r, zb, zru, zrd, zsu, zsd, fin, cgo,
    lsem, ssem, rsem,
):
    seq, mp, dp = lax.axis_index("seq"), lax.axis_index("mp"), lax.axis_index("dp")
    x, zl = seq // 4, seq % 4
    zh, core = dp // 2, dp % 2
    z = zh * 4 + zl

    def at(s=None, m=None, d=None):
        return {"seq": seq if s is None else s, "mp": mp if m is None else m, "dp": dp if d is None else d}

    def z_at(zn):
        return at(s=x * 4 + zn % 4, d=(zn // 4) * 2 + core)

    y_right, y_left = at(m=(mp + 1) % 4), at(m=(mp + 3) % 4)
    s_up, s_down = at(s=(seq + 1) % 16), at(s=(seq + 15) % 16)
    x_right, x_left = at(s=(seq + 4) % 16), at(s=(seq + 12) % 16)
    z_up, z_down = z_at((z + 1) % 8), z_at((z + 7) % 8)
    partner = at(d=zh * 2 + 1 - core)
    far = [at(d=(1 - zh) * 2 + core), at(d=(1 - zh) * 2 + 1 - core)]

    local = []

    def load(src, dst):
        copy = pltpu.make_async_copy(src, dst, lsem.at[len(local)])
        copy.start()
        local.append(copy)
        return copy

    own_rows = pl.ds(pl.multiple_of(mp * CB, CB), CB)
    own_x = load(xt_hbm, xt.at[own_rows])
    loads = [load(w_hbm.at[k], wcat.at[:, pl.ds(k * O, O)]) for k in range(KW)]
    eg_load = load(eg_hbm, eg)
    gain_load = load(gain_hbm, gain.at[mp])
    qw_load = load(qw_hbm, qw)

    barrier = pltpu.get_barrier_semaphore()
    peers = [y_right, y_left, at(m=(mp + 2) % 4), s_up, s_down, x_right, x_left, z_up, z_down, partner] + far
    for peer in peers:
        pl.semaphore_signal(barrier, inc=1, device_id=peer, device_id_type=MESH)
    pl.semaphore_wait(barrier, len(peers))

    sent = []

    def remote(src, dst, i, peer):
        return pltpu.make_async_remote_copy(
            src_ref=src, dst_ref=dst, send_sem=ssem.at[i], recv_sem=rsem.at[i], device_id=peer, device_id_type=MESH
        )

    def send(src, dst, i, peer):
        copy = remote(src, dst, i, peer)
        copy.start()
        sent.append(copy)

    def arrived(dst, i):
        remote(dst, dst, i, y_right).wait_recv()

    def block(owner, half, tb):
        first = owner * CB + (0 if half is None else half * (CB // 2))
        size = CB if half is None else CB // 2
        return xt.at[pl.ds(pl.multiple_of(first, CB // 2), size), pl.ds(tb * TB, TB)]

    m_left, m_right, m_far = (mp + 3) % 4, (mp + 1) % 4, (mp + 2) % 4

    def send_own(tb):
        src = xt_hbm.at[:, pl.ds(tb * TB, TB)]
        send(src, block(mp, None, tb), OWN_R + tb, y_right)
        send(src, block(mp, None, tb), OWN_L + tb, y_left)

    def forward(tb):
        arrived(block(m_left, None, tb), OWN_R + tb)
        send(block(m_left, 0, tb), block(m_left, 0, tb), FWD_R + tb, y_right)
        arrived(block(m_right, None, tb), OWN_L + tb)
        send(block(m_right, 1, tb), block(m_right, 1, tb), FWD_L + tb, y_left)

    def complete(tb):
        arrived(block(m_far, 0, tb), FWD_R + tb)
        arrived(block(m_far, 1, tb), FWD_L + tb)

    send(edge_hbm, rim.at[mp, pl.ds(0, 16)], EDGE_UP, s_up)
    send(edge_hbm, rim.at[mp, pl.ds(16, 16)], EDGE_DOWN, s_down)
    send_own(0)
    for d in (1, 2, 3):
        send(gain_hbm, gain.at[mp], GAIN + d, at(m=(mp + d) % 4))
    send_own(1)
    arrived(rim.at[mp, pl.ds(0, 16)], EDGE_UP)
    arrived(rim.at[mp, pl.ds(16, 16)], EDGE_DOWN)
    for d in (1, 2, 3):
        send(rim.at[mp], rim.at[mp], RIM + d, at(m=(mp + d) % 4))
    own_x.wait()

    def tap_products(tb):
        xrow[...] = xt[:, tb * TB : (tb + 1) * TB].T

        def tile(n, carry):
            cols = pl.ds(pl.multiple_of(n * 256, 256), 256)
            y = jnp.dot(xrow[...], wcat[:, cols], preferred_element_type=F32)
            yb[2 * n, pl.ds(Y0 + tb * TB, TB), :] = y[:, :128]
            yb[2 * n + 1, pl.ds(Y0 + tb * TB, TB), :] = y[:, 128:]
            return carry

        lax.fori_loop(0, N // 256, tile, 0)
        y = jnp.dot(xrow[...], wcat[:, N - 128 :], preferred_element_type=F32)
        yb[N // 128 - 1, pl.ds(Y0 + tb * TB, TB), :] = y

    def rim_products():
        for d in (1, 2, 3):
            owner = (mp + 4 - d) % 4
            arrived(rim.at[owner], RIM + d)
        before = jnp.where(seq > 0, 1.0, 0.0).astype(F32)
        after = jnp.where(seq < 15, 1.0, 0.0).astype(F32)

        def tile(n, carry):
            cols = pl.ds(pl.multiple_of(n * 128, 128), 128)
            y = jnp.zeros((32, 128), F32)
            for m in range(4):
                y += jnp.dot(rim[m][:, :CB], wcat[m * CB : (m + 1) * CB, cols], preferred_element_type=F32)
            yb[n, pl.ds(0, 8), :] = y[0:8] * before
            yb[n, pl.ds(Y0 + T, 8), :] = y[16:24] * after
            return carry

        lax.fori_loop(0, N // 128, tile, 0)

    def gelu(v):
        v2 = v * v
        th = jnp.tanh(v * (0.7978845608 + (0.7978845608 * 0.044715) * v2))
        half = 0.5 + 0.5 * th
        slope = half + 0.5 * v * (1.0 - th * th) * (0.7978845608 + (0.7978845608 * 0.134145) * v2)
        return v * half, slope

    def pre(o, row, rows, stride):
        taps = [yb[k * OT + o, pl.ds(row + k - 2, rows, stride=stride), :] for k in range(KW)]
        return taps[0] + taps[1] + taps[2] + taps[3] + taps[4]

    STEP = 32

    def activations(first, count):
        def rows_of(i, carry):
            j = pl.multiple_of(first + i * STEP, STEP)
            for o in range(OT):
                lanes = pl.ds(o * 128, 128)
                act_e, slope_e = gelu(pre(o, Y0 + 2 * j, STEP, 2))
                act_o, slope_o = gelu(pre(o, Y0 + 2 * j + 1, STEP, 2))
                g = 0.5 * eg[pl.ds(j, STEP), lanes].astype(F32)
                enc[mp, pl.ds(j, STEP), lanes] = (0.5 * (act_e + act_o)).astype(BF16)
                pgb[o, pl.ds(Y0 + 2 * j, STEP, stride=2), :] = slope_e * g
                pgb[o, pl.ds(Y0 + 2 * j + 1, STEP, stride=2), :] = slope_o * g
            return carry

        lax.fori_loop(0, count // STEP, rows_of, 0)

    def rim_gradients():
        before = jnp.where(seq > 0, 0.5, 0.0).astype(F32)
        after = jnp.where(seq < 15, 0.5, 0.0).astype(F32)
        rims = rim[mp]
        for o in range(OT):
            lanes = slice(o * 128, (o + 1) * 128)
            for row, g in ((Y0 - 2, rims[9:10, lanes].astype(F32) * before), (Y0 + T, rims[24:25, lanes].astype(F32) * after)):
                for r in (row, row + 1):
                    slope = gelu(pre(o, r, 1, 1))[1]
                    pgb[o, pl.ds(r, 1), :] = slope * g

    PSTEP = 64

    def gradient_columns():
        def rows_of(i, carry):
            s = pl.multiple_of(i * PSTEP, PSTEP)
            for k in range(KW):
                for o in range(OT):
                    pgcat[pl.ds(s, PSTEP), (k * OT + o) * 128 : (k * OT + o + 1) * 128] = pgb[
                        o, pl.ds(Y0 + s + 2 - k, PSTEP), :
                    ].astype(BF16)
            pgcat[pl.ds(s, PSTEP), N:] = jnp.zeros((PSTEP, 128), BF16)
            return carry

        lax.fori_loop(0, T // PSTEP, rows_of, 0)

    for copy in loads:
        copy.wait()
    forward(0)
    send_own(2)
    complete(0)
    tap_products(0)
    forward(1)
    send_own(3)
    rim_products()
    eg_load.wait()
    complete(1)
    tap_products(1)
    activations(0, 224)
    forward(2)
    forward(3)
    complete(2)
    tap_products(2)
    activations(224, 128)
    complete(3)
    tap_products(3)
    activations(352, 160)
    rim_gradients()

    def half_rows(owner, e):
        return enc.at[owner, pl.ds(e * (R // 2), R // 2)]

    send(half_rows(mp, 0), half_rows(mp, 0), ENC_R, y_right)
    send(half_rows(mp, 1), half_rows(mp, 1), ENC_L + 1, y_left)
    send(half_rows(mp, 1), half_rows(mp, 1), ENC_R + 1, y_right)
    send(half_rows(mp, 0), half_rows(mp, 0), ENC_L, y_left)
    gradient_columns()

    def products(xb, column, write):
        rows = pl.ds(pl.multiple_of(xb * XB, XB), XB)

        def tile(n, carry):
            cols = pl.ds(pl.multiple_of(column + n * 256, 256), 256)
            write(n, jnp.dot(xt[rows, :], pgcat[:, cols], preferred_element_type=F32))
            return carry

        lax.fori_loop(0, W2 // 256, tile, 0)

    def theirs(step, xb):
        def write(n, value):
            psend[xb, :, pl.ds(pl.multiple_of(n * 256, 256), 256)] = value.astype(BF16)

        products(xb, (1 - core) * W2, write)
        send(psend.at[xb], precv.at[xb], SWAP + step, partner)

    def ours(step, xb):
        arrived(precv.at[xb], SWAP + step)

        def write(n, value):
            cols = pl.ds(pl.multiple_of(n * 256, 256), 256)
            gown[xb, :, cols] = (value + precv[xb, :, cols].astype(F32)).astype(BF16)

        products(xb, core * W2, write)

    top, bottom = pl.ds(0, XB // 2), pl.ds(XB // 2, XB // 2)
    xf, xr, xl = (x + 2) % 4, (x + 1) % 4, (x + 3) % 4

    def add_rows(dst, src, rows):
        for r in range(0, rows, 32):
            dst[pl.ds(r, 32), :] = (dst[pl.ds(r, 32), :].astype(F32) + src[pl.ds(r, 32), :].astype(F32)).astype(BF16)

    theirs(0, xf)
    theirs(1, xr)
    ours(0, xf)
    send(gown.at[xf, top], x1l, X1R, x_right)
    send(gown.at[xf, bottom], x1r, X1L, x_left)
    theirs(2, xl)
    ours(1, xr)
    send(gown.at[xr, bottom], x2l.at[bottom], X2R + 1, x_right)
    arrived(half_rows(m_left, 0), ENC_R)
    send(half_rows(m_left, 0), half_rows(m_left, 0), EFWD_R, y_right)
    arrived(half_rows(m_right, 1), ENC_L + 1)
    send(half_rows(m_right, 1), half_rows(m_right, 1), EFWD_L, y_left)
    theirs(3, x)
    ours(2, xl)
    send(gown.at[xl, top], x2r.at[top], X2L, x_left)
    arrived(x1l, X1R)
    add_rows(gown.at[xr, top], x1l, XB // 2)
    send(gown.at[xr, top], x2l.at[top], X2R, x_right)
    arrived(x1r, X1L)
    add_rows(gown.at[xl, bottom], x1r, XB // 2)
    send(gown.at[xl, bottom], x2r.at[bottom], X2L + 1, x_left)
    ours(3, x)

    arrived(half_rows(m_left, 1), ENC_R + 1)
    arrived(half_rows(m_right, 0), ENC_L)
    arrived(half_rows(m_far, 0), EFWD_R)
    arrived(half_rows(m_far, 1), EFWD_L)
    gain_load.wait()
    for d in (1, 2, 3):
        arrived(gain.at[(mp + 4 - d) % 4], GAIN + d)

    def normalize(i, carry):
        rows = pl.ds(pl.multiple_of(i * 32, 32), 32)
        values = [enc[m, rows, :].astype(F32) for m in range(4)]
        total = jnp.sum(values[0] + values[1] + values[2] + values[3], axis=1, keepdims=True)
        square = jnp.sum(sum(v * v for v in values), axis=1, keepdims=True)
        mean = total / (4 * O)
        scale = lax.rsqrt(square / (4 * O) - mean * mean + 1e-05)
        for m in range(4):
            norm[rows, m * O : (m + 1) * O] = ((values[m] - mean) * scale * gain[m]).astype(BF16)
        return carry

    lax.fori_loop(0, R // 32, normalize, 0)
    qw_load.wait()

    def project(i, carry):
        rows = pl.ds(pl.multiple_of(i * 128, 128), 128)
        qout[rows, :] = jnp.dot(norm[rows, :], qw[...], preferred_element_type=F32).astype(BF16)
        return carry

    lax.fori_loop(0, R // 128, project, 0)
    qkv_store = load(qout, qkv_hbm)

    for half, rows in ((0, top), (1, bottom)):
        arrived(x2l.at[rows], X2R + half)
        arrived(x2r.at[rows], X2L + half)
    for g in range(4):
        for r in range(0, ZB, 16):
            rows = pl.ds(g * ZB + r, 16)
            zb[g, pl.ds(r, 16), :] = (
                gown[x, rows, :].astype(F32) + x2l[rows, :].astype(F32) + x2r[rows, :].astype(F32)
            ).astype(BF16)

    def piece(zn, lane, width):
        return zb.at[zn % 4, :, pl.ds(pl.multiple_of((zn // 4) * PIECE + lane, 256), width)]

    def pass_on(step, zn, received, buffer, lane, i, peer):
        width = PIECE // 2 if step == 1 else PIECE
        src = piece(zn, 0, PIECE)
        if step == 1:
            arrived(received.at[0, :, pl.ds(lane, width)], i)
            other = PIECE // 2 - lane
            buffer[step, :, pl.ds(other, width)] = src[:, pl.ds(other, width)]
        else:
            lane = 0
            arrived(received.at[step - 1], i + step - 1)
        cols = pl.ds(lane, width)
        buffer[step, :, cols] = (src[:, cols].astype(F32) + received[step - 1, :, cols].astype(F32)).astype(BF16)
        send(buffer.at[step], received.at[step], i + step, peer)

    zf = (z + 4) % 8
    half = PIECE // 2
    send(piece(zf, 0, half), zru.at[0, :, pl.ds(0, half)], ZUP, z_up)
    send(piece(zf, half, half), zrd.at[0, :, pl.ds(half, half)], ZDN, z_down)
    for step in (1, 2, 3):
        pass_on(step, (z + 4 - step) % 8, zru, zsu, 0, ZUP, z_up)
        pass_on(step, (z + 4 + step) % 8, zrd, zsd, half, ZDN, z_down)
    arrived(zru.at[3], ZUP + 3)
    arrived(zrd.at[3], ZDN + 3)
    mine = piece(z, 0, PIECE)
    fin[dp] = (mine[...].astype(F32) + zru[3].astype(F32) + zrd[3].astype(F32)).astype(BF16)
    for i, peer in enumerate([partner] + far):
        send(fin.at[dp], fin.at[dp], DPG + 1 + i, peer)
    for i, d in enumerate((zh * 2 + 1 - core, (1 - zh) * 2 + core, (1 - zh) * 2 + 1 - core)):
        arrived(fin.at[d], DPG + 1 + i)
    for i in range(N // 128):
        owner = (i % 8) // 4 * 2 + i // 8
        lane = (i % 4) * 128
        cgo[i // OT, :, pl.ds((i % OT) * 128, 128)] = fin[owner, :, lane : lane + 128].astype(F32)
    cg_store = load(cgo, cg_hbm)
    for copy in sent:
        copy.wait_send()
    qkv_store.wait()
    cg_store.wait()


def on_device(block_input, conv_weight, norm_gain, qkv_weight, encoder_grad):
    xin, eg = block_input[0], encoder_grad[0]
    edge = jnp.concatenate(
        [
            jnp.pad(jnp.concatenate([xin[:4], xin[-4:]]), ((0, 0), (0, O - CB))),
            eg[:1],
            eg[-1:],
            jnp.zeros((6, O), BF16),
        ]
    )
    any_ = pl.BlockSpec(memory_space=pl.ANY)
    v = pltpu.VMEM
    qkv, grad = pl.pallas_call(
        kernel,
        name="block",
        out_shape=(jax.ShapeDtypeStruct((R, Q), BF16), jax.ShapeDtypeStruct((KW, ZB, O), F32)),
        in_specs=[any_] * 6,
        out_specs=(any_, any_),
        scratch_shapes=[
            v((C, T), BF16), v((4, 32, O), BF16), v((C, N), BF16), v((4, 1, O), F32), v((4 * O, Q), BF16), v((R, O), BF16),
            v((TB, C), BF16), v((N // 128, T + 16, 128), F32), v((OT, T + 16, 128), F32), v((T, 2 * W2), BF16),
            v((4, R, O), BF16), v((R, 4 * O), BF16), v((R, Q), BF16),
            v((4, XB, W2), BF16), v((4, XB, W2), BF16), v((4, XB, W2), BF16),
            v((XB // 2, W2), BF16), v((XB // 2, W2), BF16), v((XB, W2), BF16), v((XB, W2), BF16),
            v((4, ZB, W2), BF16), v((4, ZB, PIECE), BF16), v((4, ZB, PIECE), BF16), v((4, ZB, PIECE), BF16), v((4, ZB, PIECE), BF16),
            v((4, ZB, PIECE), BF16), v((KW, ZB, O), F32),
            pltpu.SemaphoreType.DMA((12,)), pltpu.SemaphoreType.DMA((COPIES,)), pltpu.SemaphoreType.DMA((COPIES,)),
        ],
        compiler_params=pltpu.CompilerParams(collective_id=0, has_side_effects=True, vmem_limit_bytes=60 * 2**20),
    )(xin.T, edge, conv_weight, norm_gain.reshape(1, O), qkv_weight, eg)
    return qkv[None], grad.transpose(1, 0, 2)


def solution(mesh):
    return jax.shard_map(
        on_device,
        mesh=mesh,
        in_specs=(
            P("dp", "seq", "mp"),
            P(None, None, "mp"),
            P("mp"),
            P(None, "mp"),
            P("dp", "seq", "mp"),
        ),
        out_specs=(P("dp", "seq", "mp"), P("seq", None, "mp")),
        check_vma=False,
    )
```

```python
import jax
import jax.numpy as jnp
from jax import lax
from jax.experimental import pallas as pl
from jax.experimental.pallas import tpu as pltpu
from jax.sharding import PartitionSpec as P

MESH = pl.DeviceIdType.MESH
BF16, F32 = jnp.bfloat16, jnp.float32
KW = 5
T = 1024
R = 512
CB = 320
O = 384
OT = O // 128
C = 4 * CB
N = KW * O
Q = 640
TB = 256
NB = T // TB
XB = 320
ZB = 80
COLS = (9 * 128, 6 * 128)
PIECE = (5 * 128, 3 * 128)
Y0 = 8

OWN_R, OWN_L, FWD_R, FWD_L = 0, 4, 8, 12
EDGE_UP, EDGE_DOWN, GRAD_UP, GRAD_DOWN, RIM, GAIN = 16, 17, 18, 19, 19, 22
ENC_R, ENC_L, EFWD_R, EFWD_L = 26, 28, 30, 31
SWAP = 32
X1R, X1L, X2R, X2L = 36, 37, 38, 40
ZUP, ZDN = 42, 46
DUP, DDN, DSW = 50, 51, 52
COPIES = 54


def kernel(
    xt_hbm, w_hbm, gain_hbm, qw_hbm, eg_hbm, qkv_hbm, cg_hbm,
    xt, ends, edge, rim, egrim, wcat, gain, qw, eg, xrow, yb, pgb, pgcat, enc, norm, qout,
    psend, precv, gown, x1l, x1r, x2l, x2r, zb, zru, zrd, zs, u1l, u1r, u2l, u2r, fin, cgo,
    lsem, ssem, rsem,
):
    seq, mp, dp = lax.axis_index("seq"), lax.axis_index("mp"), lax.axis_index("dp")
    x, zl = seq // 4, seq % 4
    zh, core = dp // 2, dp % 2
    z = zh * 4 + zl

    def at(s=None, m=None, d=None):
        return {"seq": seq if s is None else s, "mp": mp if m is None else m, "dp": dp if d is None else d}

    def z_at(zn):
        return at(s=x * 4 + zn % 4, d=(zn // 4) * 2 + core)

    y_right, y_left = at(m=(mp + 1) % 4), at(m=(mp + 3) % 4)
    s_up, s_down = at(s=(seq + 1) % 16), at(s=(seq + 15) % 16)
    x_right, x_left = at(s=(seq + 4) % 16), at(s=(seq + 12) % 16)
    z_up, z_down = z_at((z + 1) % 8), z_at((z + 7) % 8)
    partner = at(d=zh * 2 + 1 - core)
    z_up2, z_down2 = z_at((z + 2) % 8), z_at((z + 6) % 8)

    local = []

    def load(src, dst):
        copy = pltpu.make_async_copy(src, dst, lsem.at[len(local)])
        copy.start()
        local.append(copy)
        return copy

    own_rows = pl.ds(pl.multiple_of(mp * CB, CB), CB)
    end_loads = [load(xt_hbm.at[:, pl.ds(e * (T - 128), 128)], ends.at[e, pl.ds(0, CB)]) for e in (0, 1)]
    own_x = load(xt_hbm, xt.at[own_rows])
    loads = [load(w_hbm.at[k], wcat.at[:, pl.ds(k * O, O)]) for k in range(KW)]
    eg_load = load(eg_hbm, eg)
    gain_load = load(gain_hbm, gain.at[mp])
    qw_load = load(qw_hbm, qw)

    barrier = pltpu.get_barrier_semaphore()
    peers = [y_right, y_left, at(m=(mp + 2) % 4), s_up, s_down, x_right, x_left, z_up, z_down, z_up2, z_down2, partner]
    for peer in peers:
        pl.semaphore_signal(barrier, inc=1, device_id=peer, device_id_type=MESH)
    pl.semaphore_wait(barrier, len(peers))

    sent = []

    def remote(src, dst, i, peer):
        return pltpu.make_async_remote_copy(
            src_ref=src, dst_ref=dst, send_sem=ssem.at[i], recv_sem=rsem.at[i], device_id=peer, device_id_type=MESH
        )

    def send(src, dst, i, peer):
        copy = remote(src, dst, i, peer)
        copy.start()
        sent.append(copy)

    def arrived(dst, i):
        remote(dst, dst, i, y_right).wait_recv()

    def block(owner, half, tb):
        first = owner * CB + (0 if half is None else half * (CB // 2))
        size = CB if half is None else CB // 2
        return xt.at[pl.ds(pl.multiple_of(first, CB // 2), size), pl.ds(tb * TB, TB)]

    m_left, m_right, m_far = (mp + 3) % 4, (mp + 1) % 4, (mp + 2) % 4

    def send_own(tb):
        src = xt_hbm.at[:, pl.ds(tb * TB, TB)]
        send(src, block(mp, None, tb), OWN_R + tb, y_right)
        send(src, block(mp, None, tb), OWN_L + tb, y_left)

    def forward(tb):
        arrived(block(m_left, None, tb), OWN_R + tb)
        send(block(m_left, 0, tb), block(m_left, 0, tb), FWD_R + tb, y_right)
        arrived(block(m_right, None, tb), OWN_L + tb)
        send(block(m_right, 1, tb), block(m_right, 1, tb), FWD_L + tb, y_left)

    def complete(tb):
        arrived(block(m_far, 0, tb), FWD_R + tb)
        arrived(block(m_far, 1, tb), FWD_L + tb)

    send_own(0)
    send_own(1)
    for d in (1, 2, 3):
        send(gain_hbm, gain.at[mp], GAIN + d, at(m=(mp + d) % 4))
    send(eg_hbm.at[pl.ds(R - 16, 16)], egrim.at[0], GRAD_UP, s_up)
    send(eg_hbm.at[pl.ds(0, 16)], egrim.at[1], GRAD_DOWN, s_down)
    for copy in end_loads:
        copy.wait()
    for e in (0, 1):
        ends[e, CB:, :] = jnp.zeros((O - CB, 128), BF16)
        edge[e] = ends[e].T[112 * e : 112 * e + 16, :]
    send(edge.at[1], rim.at[mp, pl.ds(0, 16)], EDGE_UP, s_up)
    send(edge.at[0], rim.at[mp, pl.ds(16, 16)], EDGE_DOWN, s_down)
    own_x.wait()

    def tap_products(tb):
        xrow[...] = xt[:, tb * TB : (tb + 1) * TB].T

        def tile(n, carry):
            cols = pl.ds(pl.multiple_of(n * 256, 256), 256)
            y = jnp.dot(xrow[...], wcat[:, cols], preferred_element_type=F32)
            yb[2 * n, pl.ds(Y0 + tb * TB, TB), :] = y[:, :128]
            yb[2 * n + 1, pl.ds(Y0 + tb * TB, TB), :] = y[:, 128:]
            return carry

        lax.fori_loop(0, N // 256, tile, 0)
        y = jnp.dot(xrow[...], wcat[:, N - 128 :], preferred_element_type=F32)
        yb[N // 128 - 1, pl.ds(Y0 + tb * TB, TB), :] = y

    def rim_products():
        for d in (1, 2, 3):
            owner = (mp + 4 - d) % 4
            arrived(rim.at[owner], RIM + d)
        before = jnp.where(seq > 0, 1.0, 0.0).astype(F32)
        after = jnp.where(seq < 15, 1.0, 0.0).astype(F32)

        def tile(n, carry):
            cols = pl.ds(pl.multiple_of(n * 128, 128), 128)
            y = jnp.zeros((32, 128), F32)
            for m in range(4):
                y += jnp.dot(rim[m][:, :CB], wcat[m * CB : (m + 1) * CB, cols], preferred_element_type=F32)
            yb[n, pl.ds(0, 8), :] = y[8:16] * before
            yb[n, pl.ds(Y0 + T, 8), :] = y[16:24] * after
            return carry

        lax.fori_loop(0, N // 128, tile, 0)

    def gelu(v):
        v2 = v * v
        th = jnp.tanh(v * (0.7978845608 + (0.7978845608 * 0.044715) * v2))
        half = 0.5 + 0.5 * th
        slope = half + 0.5 * v * (1.0 - th * th) * (0.7978845608 + (0.7978845608 * 0.134145) * v2)
        return v * half, slope

    def pre(o, row, rows, stride):
        taps = [yb[k * OT + o, pl.ds(row + k - 2, rows, stride=stride), :] for k in range(KW)]
        return taps[0] + taps[1] + taps[2] + taps[3] + taps[4]

    STEP = 32

    def activations(first, count):
        def rows_of(i, carry):
            j = pl.multiple_of(first + i * STEP, STEP)
            for o in range(OT):
                lanes = pl.ds(o * 128, 128)
                act_e, slope_e = gelu(pre(o, Y0 + 2 * j, STEP, 2))
                act_o, slope_o = gelu(pre(o, Y0 + 2 * j + 1, STEP, 2))
                g = 0.5 * eg[pl.ds(j, STEP), lanes].astype(F32)
                enc[mp, pl.ds(j, STEP), lanes] = (0.5 * (act_e + act_o)).astype(BF16)
                pgb[o, pl.ds(Y0 + 2 * j, STEP, stride=2), :] = slope_e * g
                pgb[o, pl.ds(Y0 + 2 * j + 1, STEP, stride=2), :] = slope_o * g
            return carry

        lax.fori_loop(0, count // STEP, rows_of, 0)

    def rim_gradients():
        before = jnp.where(seq > 0, 0.5, 0.0).astype(F32)
        after = jnp.where(seq < 15, 0.5, 0.0).astype(F32)
        last, first = egrim[0, 8:16, :].astype(F32), egrim[1, 0:8, :].astype(F32)
        for o in range(OT):
            lanes = slice(o * 128, (o + 1) * 128)
            for row, g in ((Y0 - 2, last[7:8, lanes] * before), (Y0 + T, first[0:1, lanes] * after)):
                for r in (row, row + 1):
                    slope = gelu(pre(o, r, 1, 1))[1]
                    pgb[o, pl.ds(r, 1), :] = slope * g

    PSTEP = 64

    def gradient_columns():
        def rows_of(i, carry):
            s = pl.multiple_of(i * PSTEP, PSTEP)
            for k in range(KW):
                for o in range(OT):
                    pgcat[pl.ds(s, PSTEP), (k * OT + o) * 128 : (k * OT + o + 1) * 128] = pgb[
                        o, pl.ds(Y0 + s + 2 - k, PSTEP), :
                    ].astype(BF16)
            return carry

        lax.fori_loop(0, T // PSTEP, rows_of, 0)

    for copy in loads:
        copy.wait()
    forward(0)
    send_own(2)
    arrived(rim.at[mp, pl.ds(0, 16)], EDGE_UP)
    arrived(rim.at[mp, pl.ds(16, 16)], EDGE_DOWN)
    for d in (1, 2, 3):
        send(rim.at[mp], rim.at[mp], RIM + d, at(m=(mp + d) % 4))
    complete(0)
    tap_products(0)
    forward(1)
    send_own(3)
    rim_products()
    eg_load.wait()
    complete(1)
    tap_products(1)
    activations(0, 224)
    forward(2)
    forward(3)
    complete(2)
    tap_products(2)
    activations(224, 128)
    complete(3)
    tap_products(3)
    activations(352, 160)
    arrived(egrim.at[0], GRAD_UP)
    arrived(egrim.at[1], GRAD_DOWN)
    rim_gradients()

    def half_rows(owner, e):
        return enc.at[owner, pl.ds(e * (R // 2), R // 2)]

    send(half_rows(mp, 0), half_rows(mp, 0), ENC_R, y_right)
    send(half_rows(mp, 1), half_rows(mp, 1), ENC_L + 1, y_left)
    send(half_rows(mp, 1), half_rows(mp, 1), ENC_R + 1, y_right)
    send(half_rows(mp, 0), half_rows(mp, 0), ENC_L, y_left)
    gradient_columns()

    def rows_of_x(xb):
        return xt[pl.ds(pl.multiple_of(xb * XB, XB), XB), :]

    def rows_of_z(g):
        return jnp.concatenate(
            [xt[pl.ds(pl.multiple_of(xb * XB + g * ZB, ZB), ZB), :] for xb in range(4)], axis=0
        )

    def products(left, owner, write):
        first, width = owner * COLS[0], COLS[owner]

        def tile(n, carry):
            lane = pl.multiple_of(n * 256, 256)
            write(lane, 256, jnp.dot(left, pgcat[:, pl.ds(first + lane, 256)], preferred_element_type=F32))
            return carry

        lax.fori_loop(0, width // 256, tile, 0)
        if width % 256:
            lane = width // 256 * 256
            write(lane, 128, jnp.dot(left, pgcat[:, pl.ds(first + lane, 128)], preferred_element_type=F32))

    def theirs(other, step, b):
        def write(lane, width, value):
            psend[b, :, pl.ds(lane, width)] = value.astype(BF16)

        products((rows_of_z if other else rows_of_x)(b), other, write)
        cols = pl.ds(0, COLS[other])
        send(psend.at[b, :, cols], precv.at[b, :, cols], SWAP + step, partner)

    def ours(me, step, b):
        arrived(precv.at[b, :, pl.ds(0, COLS[me])], SWAP + step)

        def write(lane, width, value):
            cols = pl.ds(lane, width)
            gown[b, :, cols] = (value + precv[b, :, cols].astype(F32)).astype(BF16)

        products((rows_of_z if me else rows_of_x)(b), me, write)

    def add(dst, src):
        for r in range(0, dst.shape[0], 16):
            rows = pl.ds(r, 16)
            dst[rows, :] = (dst[rows, :].astype(F32) + src[rows, :].astype(F32)).astype(BF16)

    def add3(dst, a, b, c):
        for r in range(0, dst.shape[0], 16):
            rows = pl.ds(r, 16)
            dst[rows, :] = (a[rows, :].astype(F32) + b[rows, :].astype(F32) + c[rows, :].astype(F32)).astype(BF16)

    def forward_encoded():
        arrived(half_rows(m_left, 0), ENC_R)
        send(half_rows(m_left, 0), half_rows(m_left, 0), EFWD_R, y_right)
        arrived(half_rows(m_right, 1), ENC_L + 1)
        send(half_rows(m_right, 1), half_rows(m_right, 1), EFWD_L, y_left)

    def encoded_complete():
        arrived(half_rows(m_left, 1), ENC_R + 1)
        arrived(half_rows(m_right, 0), ENC_L)
        arrived(half_rows(m_far, 0), EFWD_R)
        arrived(half_rows(m_far, 1), EFWD_L)
        gain_load.wait()
        for d in (1, 2, 3):
            arrived(gain.at[(mp + 4 - d) % 4], GAIN + d)
        qw_load.wait()

    def heads(part):
        def normalize(i, carry):
            rows = pl.ds(pl.multiple_of(part * 128 + i * 32, 32), 32)
            values = [enc[m, rows, :].astype(F32) for m in range(4)]
            total = jnp.sum(values[0] + values[1] + values[2] + values[3], axis=1, keepdims=True)
            square = jnp.sum(sum(v * v for v in values), axis=1, keepdims=True)
            mean = total / (4 * O)
            scale = lax.rsqrt(square / (4 * O) - mean * mean + 1e-05)
            for m in range(4):
                norm[rows, m * O : (m + 1) * O] = ((values[m] - mean) * scale * gain[m]).astype(BF16)
            return carry

        lax.fori_loop(0, 4, normalize, 0)
        rows = pl.ds(part * 128, 128)
        qout[rows, :] = jnp.dot(norm[rows, :], qw[...], preferred_element_type=F32).astype(BF16)

    top, bottom = pl.ds(0, XB // 2), pl.ds(XB // 2, XB // 2)
    xf, xr, xl = (x + 2) % 4, (x + 1) % 4, (x + 3) % 4
    gf, gr, gl = (zl + 2) % 4, (zl + 1) % 4, (zl + 3) % 4

    def share(me, mine):
        cols = pl.ds(0, PIECE[me])
        send(mine, fin.at[me, zh, :, cols], DUP, z_up2)
        send(mine, fin.at[me, zh, :, cols], DDN, z_down2)
        lower, upper = (z + 6) % 8 // 4, (z + 2) % 8 // 4
        arrived(fin.at[me, lower, :, cols], DUP)
        send(fin.at[me, lower, :, cols], fin.at[me, lower, :, cols], DSW, partner)
        arrived(fin.at[me, upper, :, cols], DDN)
        send(fin.at[me, upper, :, cols], fin.at[me, upper, :, cols], DSW + 1, partner)
        cols = pl.ds(0, PIECE[1 - me])
        arrived(fin.at[1 - me, lower, :, cols], DSW)
        arrived(fin.at[1 - me, upper, :, cols], DSW + 1)

    shared = len(sent)

    @pl.when(core == 0)
    def _():
        theirs(1, 0, gf)
        theirs(1, 1, gr)
        theirs(1, 2, gl)
        ours(0, 0, xf)
        send(gown.at[xf, top], x1l, X1R, x_right)
        send(gown.at[xf, bottom], x1r, X1L, x_left)
        theirs(1, 3, zl)
        ours(0, 1, xr)
        send(gown.at[xr, bottom], x2l.at[bottom], X2R + 1, x_right)
        forward_encoded()
        ours(0, 2, xl)
        send(gown.at[xl, top], x2r.at[top], X2L, x_left)
        arrived(x1l, X1R)
        add(gown.at[xr, top], x1l)
        send(gown.at[xr, top], x2l.at[top], X2R, x_right)
        arrived(x1r, X1L)
        add(gown.at[xl, bottom], x1r)
        send(gown.at[xl, bottom], x2r.at[bottom], X2L + 1, x_left)
        ours(0, 3, x)
        encoded_complete()
        heads(0)
        for half, rows in ((0, top), (1, bottom)):
            arrived(x2l.at[rows], X2R + half)
            arrived(x2r.at[rows], X2L + half)
        for g in range(4):
            for h in range(2):
                rows, cols = pl.ds(g * ZB, ZB), pl.ds(h * 512, 640)
                add3(zb.at[g, h], gown.at[x, rows, cols], x2l.at[rows, cols], x2r.at[rows, cols])

        def piece(zo):
            return zb.at[(zo + 2) % 4, zo // 4]

        up, down = pl.ds(0, 384), pl.ds(384, 256)
        far = piece((z + 4) % 8)
        ru = [zru.at[s, pl.ds(0, ZB)] for s in range(4)]
        rd = [zrd.at[s, pl.ds(0, ZB)] for s in range(4)]
        send(far.at[:, up], ru[0].at[:, up], ZUP, z_up)
        send(far.at[:, down], rd[0].at[:, down], ZDN, z_down)
        for step in (1, 2, 3):
            heads(step)
            higher, lower = piece((z + 4 - step) % 8), piece((z + 4 + step) % 8)
            cu, cd = (up, down) if step == 1 else (pl.ds(0, 640),) * 2
            arrived(ru[step - 1].at[:, cu], ZUP + step - 1)
            add(higher.at[:, cu], ru[step - 1].at[:, cu])
            send(higher, ru[step], ZUP + step, z_up)
            arrived(rd[step - 1].at[:, cd], ZDN + step - 1)
            add(lower.at[:, cd], rd[step - 1].at[:, cd])
            send(lower, rd[step], ZDN + step, z_down)
        load(qout, qkv_hbm)
        arrived(ru[3], ZUP + 3)
        arrived(rd[3], ZDN + 3)
        mine = piece(z)
        add3(mine, mine, ru[3], rd[3])
        share(0, mine)
        for copy in sent:
            copy.wait_send()
        local[-1].wait()

    @pl.when(core == 1)
    def _():
        del sent[shared:]
        theirs(0, 0, xf)
        theirs(0, 1, xr)
        ours(1, 0, gf)

        def piece(zo):
            return gown.at[(zo + 2) % 4, :, pl.ds(pl.multiple_of(zo // 4 * PIECE[1], 128), PIECE[1])]

        ru = [zru.at[s, :, pl.ds(0, PIECE[1])] for s in range(4)]
        rd = [zrd.at[s, :, pl.ds(0, PIECE[1])] for s in range(4)]

        def up(step):
            dst = piece((z + 4 - step) % 8)
            rows = top if step == 1 else pl.ds(0, XB)
            arrived(ru[step - 1].at[rows], ZUP + step - 1)
            add(dst.at[rows], ru[step - 1].at[rows])
            send(dst, ru[step], ZUP + step, z_up)

        def down(step):
            dst = piece((z + 4 + step) % 8)
            rows = bottom if step == 1 else pl.ds(0, XB)
            arrived(rd[step - 1].at[rows], ZDN + step - 1)
            add(dst.at[rows], rd[step - 1].at[rows])
            send(dst, rd[step], ZDN + step, z_down)

        far = piece((z + 4) % 8)
        send(far.at[top], ru[0].at[top], ZUP, z_up)
        send(far.at[bottom], rd[0].at[bottom], ZDN, z_down)
        theirs(0, 2, xl)
        ours(1, 1, gr)
        up(1)
        ours(1, 2, gl)
        down(1)
        theirs(0, 3, x)
        forward_encoded()
        ours(1, 3, zl)
        up(2)
        down(2)
        up(3)
        down(3)
        encoded_complete()
        heads(0)
        heads(1)
        arrived(ru[3], ZUP + 3)
        arrived(rd[3], ZDN + 3)
        add3(zs, piece(z), ru[3], rd[3])

        def rows_at(xb, first, rows):
            return zs.at[pl.ds(pl.multiple_of(xb * ZB + first, 16), rows)]

        send(rows_at(xf, 0, 48), u1l, X1R, x_right)
        send(rows_at(xf, 48, 32), u1r, X1L, x_left)
        heads(2)
        arrived(u1l, X1R)
        add(rows_at(xr, 0, 48), u1l)
        send(rows_at(xr, 0, ZB), u2l, X2R, x_right)
        arrived(u1r, X1L)
        add(rows_at(xl, 48, 32), u1r)
        send(rows_at(xl, 0, ZB), u2r, X2L, x_left)
        heads(3)
        load(qout, qkv_hbm)
        arrived(u2l, X2R)
        arrived(u2r, X2L)
        mine = rows_at(x, 0, ZB)
        add3(mine, mine, u2l, u2r)
        share(1, mine)
        for copy in sent:
            copy.wait_send()
        local[-1].wait()

    for i in range(N // 128):
        if i < 9:
            src = fin.at[0, i // 5, :, pl.ds((i - i // 5 * 4) * 128, 128)]
        else:
            src = fin.at[1, (i - 9) // 3, :, pl.ds((i - 9) % 3 * 128, 128)]
        cgo[i // OT, :, pl.ds((i % OT) * 128, 128)] = src[...]
    load(cgo, cg_hbm).wait()


def finish(qkv_in, grad_in, qkv_out, grad_out, qkv, grad, wide, sem):
    first = pltpu.make_async_copy(grad_in, grad, sem.at[0])
    second = pltpu.make_async_copy(qkv_in, qkv, sem.at[1])
    first.start()
    second.start()
    first.wait()
    wide[...] = grad[...].astype(F32)
    third = pltpu.make_async_copy(wide, grad_out, sem.at[2])
    third.start()
    second.wait()
    fourth = pltpu.make_async_copy(qkv, qkv_out, sem.at[3])
    fourth.start()
    third.wait()
    fourth.wait()


def on_device(block_input, conv_weight, norm_gain, qkv_weight, encoder_grad):
    xin, eg = block_input[0], encoder_grad[0]
    any_ = pl.BlockSpec(memory_space=pl.ANY)
    v = pltpu.VMEM
    qkv, grad = pl.pallas_call(
        kernel,
        name="block",
        out_shape=(jax.ShapeDtypeStruct((R, Q), BF16), jax.ShapeDtypeStruct((KW, ZB, O), BF16)),
        in_specs=[any_] * 5,
        out_specs=(any_, any_),
        scratch_shapes=[
            v((C, T), BF16), v((2, O, 128), BF16), v((2, 16, O), BF16), v((4, 32, O), BF16), v((2, 16, O), BF16),
            v((C, N), BF16), v((4, O), F32), v((4 * O, Q), BF16), v((R, O), BF16),
            v((TB, C), BF16), v((N // 128, T + 16, 128), F32), v((OT, T + 16, 128), F32), v((T, N), BF16),
            v((4, R, O), BF16), v((R, 4 * O), BF16), v((R, Q), BF16),
            v((4, XB, COLS[0]), BF16), v((4, XB, COLS[0]), BF16), v((4, XB, COLS[0]), BF16),
            v((XB // 2, COLS[0]), BF16), v((XB // 2, COLS[0]), BF16), v((XB, COLS[0]), BF16), v((XB, COLS[0]), BF16),
            v((4, 2, ZB, PIECE[0]), BF16), v((4, XB, PIECE[0]), BF16), v((4, XB, PIECE[0]), BF16), v((XB, PIECE[1]), BF16),
            v((48, PIECE[1]), BF16), v((32, PIECE[1]), BF16), v((ZB, PIECE[1]), BF16), v((ZB, PIECE[1]), BF16),
            v((2, 2, ZB, PIECE[0]), BF16), v((KW, ZB, O), BF16),
            pltpu.SemaphoreType.DMA((16,)), pltpu.SemaphoreType.DMA((COPIES,)), pltpu.SemaphoreType.DMA((COPIES,)),
        ],
        compiler_params=pltpu.CompilerParams(collective_id=0, has_side_effects=True, vmem_limit_bytes=58 * 2**20),
    )(xin.T, conv_weight, norm_gain, qkv_weight, eg)
    qkv, grad = pl.pallas_call(
        finish,
        name="finish",
        out_shape=(jax.ShapeDtypeStruct((R, Q), BF16), jax.ShapeDtypeStruct((KW, ZB, O), F32)),
        in_specs=[any_] * 2,
        out_specs=(any_, any_),
        scratch_shapes=[v((R, Q), BF16), v((KW, ZB, O), BF16), v((KW, ZB, O), F32), pltpu.SemaphoreType.DMA((4,))],
    )(qkv, grad)
    return qkv[None], grad.transpose(1, 0, 2)


def solution(mesh):
    return jax.shard_map(
        on_device,
        mesh=mesh,
        in_specs=(
            P("dp", "seq", "mp"),
            P(None, None, "mp"),
            P("mp"),
            P(None, "mp"),
            P("dp", "seq", "mp"),
        ),
        out_specs=(P("dp", "seq", "mp"), P("seq", None, "mp")),
        check_vma=False,
    )
```

```python
import jax
import jax.numpy as jnp
from jax import lax
from jax.experimental import pallas as pl
from jax.experimental.pallas import tpu as pltpu
from jax.sharding import PartitionSpec as P

MESH = pl.DeviceIdType.MESH
BF16, F32 = jnp.bfloat16, jnp.float32
KW = 5
T = 1024
R = 512
CB = 320
O = 384
OT = O // 128
C = 4 * CB
N = KW * O
Q = 640
TB = 128
TC = 256
XB = 320
ZB = 80
COLS = (9 * 128, 6 * 128)
PIECE = 3 * 128
Y0 = 8

OWN_R, OWN_L, FWD_R, FWD_L = 0, 8, 16, 24
EDGE_UP, EDGE_DOWN, GRAD_UP, GRAD_DOWN, RIM, GAIN = 32, 33, 34, 35, 35, 38
ENC_R, ENC_L, EFWD_R, EFWD_L = 42, 44, 46, 47
SWAP = 48
X1R, X1L, X2R, X2L = 52, 53, 54, 56
ZUA, ZUB, ZDA, ZDB = 58, 62, 66, 70
DUP, DDN, DSW = 74, 75, 76
COPIES = 78


def kernel(
    xt_hbm, w_hbm, gain_hbm, qw_hbm, eg_hbm, qkv_hbm, cg_hbm,
    xt, ends, edge, rim, egrim, wcat, gain, qw, eg, xrow, yb, pgb, pgcat, enc, norm, qout,
    psend, precv, gown, x1l, x1r, x2l, x2r, zb, zr, zs, zr1, zs1, u1l, u1r, u2l, u2r, fin0, fin1, cgo,
    lsem, ssem, rsem,
):
    seq, mp, dp = lax.axis_index("seq"), lax.axis_index("mp"), lax.axis_index("dp")
    x, zl = seq // 4, seq % 4
    zh, core = dp // 2, dp % 2
    z = zh * 4 + zl

    def at(s=None, m=None, d=None):
        return {"seq": seq if s is None else s, "mp": mp if m is None else m, "dp": dp if d is None else d}

    def z_at(zn):
        return at(s=x * 4 + zn % 4, d=(zn // 4) * 2 + core)

    y_right, y_left = at(m=(mp + 1) % 4), at(m=(mp + 3) % 4)
    s_up, s_down = at(s=(seq + 1) % 16), at(s=(seq + 15) % 16)
    x_right, x_left = at(s=(seq + 4) % 16), at(s=(seq + 12) % 16)
    z_up, z_down = z_at((z + 1) % 8), z_at((z + 7) % 8)
    partner = at(d=zh * 2 + 1 - core)
    z_up2, z_down2 = z_at((z + 2) % 8), z_at((z + 6) % 8)

    local = []

    def load(src, dst):
        copy = pltpu.make_async_copy(src, dst, lsem.at[len(local)])
        copy.start()
        local.append(copy)
        return copy

    own_rows = pl.ds(pl.multiple_of(mp * CB, CB), CB)
    end_loads = [load(xt_hbm.at[:, pl.ds(e * (T - 128), 128)], ends.at[e, pl.ds(0, CB)]) for e in (0, 1)]
    own_x = load(xt_hbm, xt.at[own_rows])
    loads = [load(w_hbm.at[k], wcat.at[:, pl.ds(k * O, O)]) for k in range(KW)]
    eg_load = load(eg_hbm, eg)
    gain_load = load(gain_hbm, gain.at[mp])
    qw_load = load(qw_hbm, qw)

    barrier = pltpu.get_barrier_semaphore()
    peers = [y_right, y_left, at(m=(mp + 2) % 4), s_up, s_down, x_right, x_left, z_up, z_down, z_up2, z_down2, partner]
    for peer in peers:
        pl.semaphore_signal(barrier, inc=1, device_id=peer, device_id_type=MESH)
    pl.semaphore_wait(barrier, len(peers))

    sent = []

    def remote(src, dst, i, peer):
        return pltpu.make_async_remote_copy(
            src_ref=src, dst_ref=dst, send_sem=ssem.at[i], recv_sem=rsem.at[i], device_id=peer, device_id_type=MESH
        )

    def send(src, dst, i, peer):
        copy = remote(src, dst, i, peer)
        copy.start()
        sent.append(copy)

    def arrived(dst, i):
        remote(dst, dst, i, y_right).wait_recv()

    def block(owner, half, tb):
        first = owner * CB + (0 if half is None else half * (CB // 2))
        size = CB if half is None else CB // 2
        return xt.at[pl.ds(pl.multiple_of(first, CB // 2), size), pl.ds(tb * TB, TB)]

    m_left, m_right, m_far = (mp + 3) % 4, (mp + 1) % 4, (mp + 2) % 4

    def send_own(tb):
        src = xt_hbm.at[:, pl.ds(tb * TB, TB)]
        send(src, block(mp, None, tb), OWN_R + tb, y_right)
        send(src, block(mp, None, tb), OWN_L + tb, y_left)

    def forward(tb):
        arrived(block(m_left, None, tb), OWN_R + tb)
        send(block(m_left, 0, tb), block(m_left, 0, tb), FWD_R + tb, y_right)
        arrived(block(m_right, None, tb), OWN_L + tb)
        send(block(m_right, 1, tb), block(m_right, 1, tb), FWD_L + tb, y_left)

    def complete(tb):
        arrived(block(m_far, 0, tb), FWD_R + tb)
        arrived(block(m_far, 1, tb), FWD_L + tb)

    send_own(0)
    send_own(1)
    for d in (1, 2, 3):
        send(gain_hbm, gain.at[mp], GAIN + d, at(m=(mp + d) % 4))
    send(eg_hbm.at[pl.ds(R - 16, 16)], egrim.at[0], GRAD_UP, s_up)
    send(eg_hbm.at[pl.ds(0, 16)], egrim.at[1], GRAD_DOWN, s_down)
    for copy in end_loads:
        copy.wait()
    for e in (0, 1):
        ends[e, CB:, :] = jnp.zeros((O - CB, 128), BF16)
        edge[e] = ends[e].T[112 * e : 112 * e + 16, :]
    send(edge.at[1], rim.at[mp, pl.ds(0, 16)], EDGE_UP, s_up)
    send(edge.at[0], rim.at[mp, pl.ds(16, 16)], EDGE_DOWN, s_down)
    own_x.wait()

    def tap_products(g, half):
        if half == 0:
            xrow[...] = xt[:, g * TC : (g + 1) * TC].T

        def tile(n, carry):
            cols = pl.ds(pl.multiple_of(n * 256, 256), 256)
            y = jnp.dot(xrow[...], wcat[:, cols], preferred_element_type=F32)
            yb[2 * n, pl.ds(Y0 + g * TC, TC), :] = y[:, :128]
            yb[2 * n + 1, pl.ds(Y0 + g * TC, TC), :] = y[:, 128:]
            return carry

        if half == 0:
            lax.fori_loop(0, 4, tile, 0)
        else:
            lax.fori_loop(4, N // 256, tile, 0)
            y = jnp.dot(xrow[...], wcat[:, N - 128 :], preferred_element_type=F32)
            yb[N // 128 - 1, pl.ds(Y0 + g * TC, TC), :] = y

    def rim_products():
        for d in (1, 2, 3):
            owner = (mp + 4 - d) % 4
            arrived(rim.at[owner], RIM + d)
        before = jnp.where(seq > 0, 1.0, 0.0).astype(F32)
        after = jnp.where(seq < 15, 1.0, 0.0).astype(F32)

        def tile(n, carry):
            cols = pl.ds(pl.multiple_of(n * 128, 128), 128)
            y = jnp.zeros((32, 128), F32)
            for m in range(4):
                y += jnp.dot(rim[m][:, :CB], wcat[m * CB : (m + 1) * CB, cols], preferred_element_type=F32)
            yb[n, pl.ds(0, 8), :] = y[8:16] * before
            yb[n, pl.ds(Y0 + T, 8), :] = y[16:24] * after
            return carry

        lax.fori_loop(0, N // 128, tile, 0)

    def gelu(v):
        v2 = v * v
        th = jnp.tanh(v * (0.7978845608 + (0.7978845608 * 0.044715) * v2))
        half = 0.5 + 0.5 * th
        slope = half + 0.5 * v * (1.0 - th * th) * (0.7978845608 + (0.7978845608 * 0.134145) * v2)
        return v * half, slope

    def pre(o, row, rows, stride):
        taps = [yb[k * OT + o, pl.ds(row + k - 2, rows, stride=stride), :] for k in range(KW)]
        return taps[0] + taps[1] + taps[2] + taps[3] + taps[4]

    STEP = 32

    def activations(first, count):
        def rows_of(i, carry):
            j = pl.multiple_of(first + i * STEP, STEP)
            for o in range(OT):
                lanes = pl.ds(o * 128, 128)
                act_e, slope_e = gelu(pre(o, Y0 + 2 * j, STEP, 2))
                act_o, slope_o = gelu(pre(o, Y0 + 2 * j + 1, STEP, 2))
                g = 0.5 * eg[pl.ds(j, STEP), lanes].astype(F32)
                enc[mp, pl.ds(j, STEP), lanes] = (0.5 * (act_e + act_o)).astype(BF16)
                pgb[o, pl.ds(Y0 + 2 * j, STEP, stride=2), :] = slope_e * g
                pgb[o, pl.ds(Y0 + 2 * j + 1, STEP, stride=2), :] = slope_o * g
            return carry

        lax.fori_loop(0, count // STEP, rows_of, 0)

    def rim_gradients(side):
        before = jnp.where(seq > 0, 0.5, 0.0).astype(F32)
        after = jnp.where(seq < 15, 0.5, 0.0).astype(F32)
        last, first = egrim[0, 8:16, :].astype(F32), egrim[1, 0:8, :].astype(F32)
        for o in range(OT):
            lanes = slice(o * 128, (o + 1) * 128)
            row, g = ((Y0 - 2, last[7:8, lanes] * before), (Y0 + T, first[0:1, lanes] * after))[side]
            for r in (row, row + 1):
                slope = gelu(pre(o, r, 1, 1))[1]
                pgb[o, pl.ds(r, 1), :] = slope * g

    PSTEP = 64

    def gradient_columns(first, count):
        def rows_of(i, carry):
            s = pl.multiple_of(first + i * PSTEP, PSTEP)
            for k in range(KW):
                for o in range(OT):
                    pgcat[pl.ds(s, PSTEP), (k * OT + o) * 128 : (k * OT + o + 1) * 128] = pgb[
                        o, pl.ds(Y0 + s + 2 - k, PSTEP), :
                    ].astype(BF16)
            return carry

        lax.fori_loop(0, count // PSTEP, rows_of, 0)

    def serve(i):
        forward(i)
        if i + 2 < T // TB:
            send_own(i + 2)

    def group(g):
        complete(2 * g)
        complete(2 * g + 1)

    serve(0)
    arrived(rim.at[mp, pl.ds(0, 16)], EDGE_UP)
    arrived(rim.at[mp, pl.ds(16, 16)], EDGE_DOWN)
    for d in (1, 2, 3):
        send(rim.at[mp], rim.at[mp], RIM + d, at(m=(mp + d) % 4))
    serve(1)
    for copy in loads:
        copy.wait()
    serve(2)
    group(0)
    tap_products(0, 0)
    serve(3)
    tap_products(0, 1)
    rim_products()
    serve(4)
    group(1)
    tap_products(1, 0)
    serve(5)
    tap_products(1, 1)
    eg_load.wait()
    activations(0, 224)
    arrived(egrim.at[0], GRAD_UP)
    arrived(egrim.at[1], GRAD_DOWN)
    rim_gradients(0)
    serve(6)
    gradient_columns(0, 384)
    group(2)
    tap_products(2, 0)
    serve(7)
    tap_products(2, 1)
    activations(224, 128)
    group(3)
    tap_products(3, 0)
    tap_products(3, 1)
    activations(352, 160)
    rim_gradients(1)

    def half_rows(owner, e):
        return enc.at[owner, pl.ds(e * (R // 2), R // 2)]

    send(half_rows(mp, 0), half_rows(mp, 0), ENC_R, y_right)
    send(half_rows(mp, 1), half_rows(mp, 1), ENC_L + 1, y_left)
    send(half_rows(mp, 1), half_rows(mp, 1), ENC_R + 1, y_right)
    send(half_rows(mp, 0), half_rows(mp, 0), ENC_L, y_left)
    gradient_columns(384, 640)

    def rows_of_x(xb):
        return xt[pl.ds(pl.multiple_of(xb * XB, XB), XB), :]

    def rows_of_z(g):
        return jnp.concatenate(
            [xt[pl.ds(pl.multiple_of(xb * XB + g * ZB, ZB), ZB), :] for xb in range(4)], axis=0
        )

    def products(left, owner, write):
        first, width = owner * COLS[0], COLS[owner]

        def tile(n, carry):
            lane = pl.multiple_of(n * 256, 256)
            write(lane, 256, jnp.dot(left, pgcat[:, pl.ds(first + lane, 256)], preferred_element_type=F32))
            return carry

        lax.fori_loop(0, width // 256, tile, 0)
        if width % 256:
            lane = width // 256 * 256
            write(lane, 128, jnp.dot(left, pgcat[:, pl.ds(first + lane, 128)], preferred_element_type=F32))

    def theirs(other, step, b):
        def write(lane, width, value):
            psend[b, :, pl.ds(lane, width)] = value.astype(BF16)

        products((rows_of_z if other else rows_of_x)(b), other, write)
        cols = pl.ds(0, COLS[other])
        send(psend.at[b, :, cols], precv.at[b, :, cols], SWAP + step, partner)

    def ours(me, step, b):
        arrived(precv.at[b, :, pl.ds(0, COLS[me])], SWAP + step)

        def write(lane, width, value):
            cols = pl.ds(lane, width)
            gown[b, :, cols] = (value + precv[b, :, cols].astype(F32)).astype(BF16)

        products((rows_of_z if me else rows_of_x)(b), me, write)

    def add(dst, src):
        for r in range(0, dst.shape[0], 16):
            rows = pl.ds(r, 16)
            dst[rows, :] = (dst[rows, :].astype(F32) + src[rows, :].astype(F32)).astype(BF16)

    def add_to(dst, a, b):
        for r in range(0, dst.shape[0], 16):
            rows = pl.ds(r, 16)
            dst[rows, :] = (a[rows, :].astype(F32) + b[rows, :].astype(F32)).astype(BF16)

    def add3(dst, a, b, c):
        for r in range(0, dst.shape[0], 16):
            rows = pl.ds(r, 16)
            dst[rows, :] = (a[rows, :].astype(F32) + b[rows, :].astype(F32) + c[rows, :].astype(F32)).astype(BF16)

    def forward_encoded():
        arrived(half_rows(m_left, 0), ENC_R)
        send(half_rows(m_left, 0), half_rows(m_left, 0), EFWD_R, y_right)
        arrived(half_rows(m_right, 1), ENC_L + 1)
        send(half_rows(m_right, 1), half_rows(m_right, 1), EFWD_L, y_left)

    def encoded_complete():
        arrived(half_rows(m_left, 1), ENC_R + 1)
        arrived(half_rows(m_right, 0), ENC_L)
        arrived(half_rows(m_far, 0), EFWD_R)
        arrived(half_rows(m_far, 1), EFWD_L)
        gain_load.wait()
        for d in (1, 2, 3):
            arrived(gain.at[(mp + 4 - d) % 4], GAIN + d)
        qw_load.wait()

    def heads(part):
        def normalize(i, carry):
            rows = pl.ds(pl.multiple_of(part * 128 + i * 32, 32), 32)
            values = [enc[m, rows, :].astype(F32) for m in range(4)]
            total = jnp.sum(values[0] + values[1] + values[2] + values[3], axis=1, keepdims=True)
            square = jnp.sum(sum(v * v for v in values), axis=1, keepdims=True)
            mean = total / (4 * O)
            scale = lax.rsqrt(square / (4 * O) - mean * mean + 1e-05)
            for m in range(4):
                norm[rows, m * O : (m + 1) * O] = ((values[m] - mean) * scale * gain[m]).astype(BF16)
            return carry

        lax.fori_loop(0, 4, normalize, 0)
        rows = pl.ds(part * 128, 128)
        qout[rows, :] = jnp.dot(norm[rows, :], qw[...], preferred_element_type=F32).astype(BF16)

    top, bottom = pl.ds(0, XB // 2), pl.ds(XB // 2, XB // 2)
    xf, xr, xl = (x + 2) % 4, (x + 1) % 4, (x + 3) % 4
    gf, gr, gl = (zl + 2) % 4, (zl + 1) % 4, (zl + 3) % 4

    lower, upper = (z + 6) % 8 // 4, (z + 2) % 8 // 4

    def z_chain(step, part, base, received, staged):
        for sign, ids, peer in ((1, (ZUA, ZUB), z_up), (-1, (ZDA, ZDB), z_down)):
            z_hop(sign, step, part, base, received, staged, ids[part] + step - 1, peer)

    def z_hop(sign, step, part, base, received, staged, i, peer):
        src = base(sign, step, part)
        if step > 1 + part:
            arrived(received(sign, step - 1, part), i - 1)
            dst = staged(sign, step, part)
            add_to(dst, src, received(sign, step - 1, part))
            src = dst
        send(src, received(sign, step, part), i, peer)

    def z_last(received):
        for sign, ids in ((1, (ZUA, ZUB)), (-1, (ZDA, ZDB))):
            for part in (0, 1):
                arrived(received(sign, 4, part), ids[part] + 3)

    shared = len(sent)

    @pl.when(core == 0)
    def _():
        theirs(1, 0, gf)
        theirs(1, 1, gr)
        theirs(1, 2, gl)
        ours(0, 0, xf)
        send(gown.at[xf, top], x1l, X1R, x_right)
        send(gown.at[xf, bottom], x1r, X1L, x_left)
        theirs(1, 3, zl)
        ours(0, 1, xr)
        send(gown.at[xr, bottom], x2l.at[bottom], X2R + 1, x_right)
        forward_encoded()
        ours(0, 2, xl)
        send(gown.at[xl, top], x2r.at[top], X2L, x_left)
        arrived(x1l, X1R)
        add(gown.at[xr, top], x1l)
        send(gown.at[xr, top], x2l.at[top], X2R, x_right)
        arrived(x1r, X1L)
        add(gown.at[xl, bottom], x1r)
        send(gown.at[xl, bottom], x2r.at[bottom], X2L + 1, x_left)
        ours(0, 3, x)
        encoded_complete()
        heads(0)
        for half, rows in ((0, top), (1, bottom)):
            arrived(x2l.at[rows], X2R + half)
            arrived(x2r.at[rows], X2L + half)
        for g in range(4):
            rows = pl.ds(g * ZB, ZB)
            add3(zb.at[g], gown.at[x, rows], x2l.at[rows], x2r.at[rows])

        spans = (pl.ds(0, 640), pl.ds(640, 512))

        def cols(sign, part):
            return spans[part if sign == 1 else 1 - part]

        def way(sign):
            return 0 if sign == 1 else 1

        def base(sign, step, part):
            return zb.at[(zl + 5 - step if sign == 1 else zl + 3 + step) % 4, :, cols(sign, part)]

        def received(sign, step, part):
            return zr.at[way(sign), step - 1, :, cols(sign, part)]

        def staged(sign, step, part):
            return zs.at[way(sign), step - 2, :, cols(sign, part)]

        z_chain(1, 0, base, received, staged)
        z_chain(2, 1, base, received, staged)
        heads(1)
        z_chain(2, 0, base, received, staged)
        z_chain(3, 1, base, received, staged)
        heads(2)
        z_chain(3, 0, base, received, staged)
        z_chain(4, 1, base, received, staged)
        heads(3)
        load(qout, qkv_hbm)
        z_chain(4, 0, base, received, staged)
        z_last(received)
        add3(fin0, zb.at[zl], zr.at[0, 3], zr.at[1, 3])
        send(fin0, fin0, DSW, partner)
        arrived(fin1.at[lower], DSW)
        arrived(fin1.at[upper], DSW + 1)
        for copy in sent:
            copy.wait_send()
        local[-1].wait()

    @pl.when(core == 1)
    def _():
        del sent[shared:]
        theirs(0, 0, xf)
        theirs(0, 1, xr)
        ours(1, 0, gf)

        def piece(zo):
            return gown.at[(zo + 2) % 4, :, pl.ds(pl.multiple_of(zo // 4 * PIECE, 128), PIECE)]

        def half(ref, sign, part):
            return ref.at[top if (part == 0) == (sign == 1) else bottom]

        def base(sign, step, part):
            return half(piece((z + 5 - step if sign == 1 else z + 3 + step) % 8), sign, part)

        def received(sign, step, part):
            return half(zr1.at[0 if sign == 1 else 1, step - 1], sign, part)

        def hop(sign, step, part):
            i, peer = ((ZUA, ZUB)[part], z_up) if sign == 1 else ((ZDA, ZDB)[part], z_down)
            z_hop(sign, step, part, base, received, base, i + step - 1, peer)

        z_chain(1, 0, base, received, base)
        theirs(0, 2, xl)
        ours(1, 1, gr)
        hop(1, 2, 1)
        hop(1, 2, 0)
        ours(1, 2, gl)
        hop(-1, 2, 1)
        hop(-1, 2, 0)
        theirs(0, 3, x)
        ours(1, 3, zl)
        z_chain(3, 1, base, received, base)
        z_chain(3, 0, base, received, base)
        forward_encoded()
        z_chain(4, 1, base, received, base)
        z_chain(4, 0, base, received, base)
        encoded_complete()
        heads(0)
        z_last(received)
        add3(zs1, piece(z), zr1.at[0, 3], zr1.at[1, 3])

        def rows_at(xb, first, rows):
            return zs1.at[pl.ds(pl.multiple_of(xb * ZB + first, 16), rows)]

        send(rows_at(xf, 0, 48), u1l, X1R, x_right)
        send(rows_at(xf, 48, 32), u1r, X1L, x_left)
        heads(1)
        arrived(u1l, X1R)
        add(rows_at(xr, 0, 48), u1l)
        send(rows_at(xr, 0, ZB), u2l, X2R, x_right)
        arrived(u1r, X1L)
        add(rows_at(xl, 48, 32), u1r)
        send(rows_at(xl, 0, ZB), u2r, X2L, x_left)
        heads(2)
        arrived(u2l, X2R)
        arrived(u2r, X2L)
        mine = rows_at(x, 0, ZB)
        add3(mine, mine, u2l, u2r)
        send(mine, fin1.at[zh], DUP, z_up2)
        send(mine, fin1.at[zh], DDN, z_down2)
        heads(3)
        load(qout, qkv_hbm)
        arrived(fin1.at[lower], DUP)
        send(fin1.at[lower], fin1.at[lower], DSW, partner)
        arrived(fin1.at[upper], DDN)
        send(fin1.at[upper], fin1.at[upper], DSW + 1, partner)
        arrived(fin0, DSW)
        for copy in sent:
            copy.wait_send()
        local[-1].wait()

    for i in range(N // 128):
        if i < 9:
            src = fin0.at[:, pl.ds(i * 128, 128)]
        else:
            src = fin1.at[(i - 9) // 3, :, pl.ds((i - 9) % 3 * 128, 128)]
        cgo[i // OT, :, pl.ds((i % OT) * 128, 128)] = src[...]
    load(cgo, cg_hbm).wait()


def finish(qkv_in, grad_in, qkv_out, grad_out, qkv, grad, wide, sem):
    first = pltpu.make_async_copy(grad_in, grad, sem.at[0])
    second = pltpu.make_async_copy(qkv_in, qkv, sem.at[1])
    first.start()
    second.start()
    first.wait()
    wide[...] = grad[...].astype(F32)
    third = pltpu.make_async_copy(wide, grad_out, sem.at[2])
    third.start()
    second.wait()
    fourth = pltpu.make_async_copy(qkv, qkv_out, sem.at[3])
    fourth.start()
    third.wait()
    fourth.wait()


def on_device(block_input, conv_weight, norm_gain, qkv_weight, encoder_grad):
    xin, eg = block_input[0], encoder_grad[0]
    any_ = pl.BlockSpec(memory_space=pl.ANY)
    v = pltpu.VMEM
    qkv, grad = pl.pallas_call(
        kernel,
        name="block",
        out_shape=(jax.ShapeDtypeStruct((R, Q), BF16), jax.ShapeDtypeStruct((KW, ZB, O), BF16)),
        in_specs=[any_] * 5,
        out_specs=(any_, any_),
        scratch_shapes=[
            v((C, T), BF16), v((2, O, 128), BF16), v((2, 16, O), BF16), v((4, 32, O), BF16), v((2, 16, O), BF16),
            v((C, N), BF16), v((4, O), F32), v((4 * O, Q), BF16), v((R, O), BF16),
            v((TC, C), BF16), v((N // 128, T + 16, 128), F32), v((OT, T + 16, 128), F32), v((T, N), BF16),
            v((4, R, O), BF16), v((R, 4 * O), BF16), v((R, Q), BF16),
            v((4, XB, COLS[0]), BF16), v((4, XB, COLS[0]), BF16), v((4, XB, COLS[0]), BF16),
            v((XB // 2, COLS[0]), BF16), v((XB // 2, COLS[0]), BF16), v((XB, COLS[0]), BF16), v((XB, COLS[0]), BF16),
            v((4, ZB, COLS[0]), BF16), v((2, 4, ZB, COLS[0]), BF16), v((2, 3, ZB, COLS[0]), BF16),
            v((2, 4, XB, PIECE), BF16), v((XB, PIECE), BF16),
            v((48, PIECE), BF16), v((32, PIECE), BF16), v((ZB, PIECE), BF16), v((ZB, PIECE), BF16),
            v((ZB, COLS[0]), BF16), v((2, ZB, PIECE), BF16), v((KW, ZB, O), BF16),
            pltpu.SemaphoreType.DMA((16,)), pltpu.SemaphoreType.DMA((COPIES,)), pltpu.SemaphoreType.DMA((COPIES,)),
        ],
        compiler_params=pltpu.CompilerParams(collective_id=0, has_side_effects=True, vmem_limit_bytes=58 * 2**20),
    )(xin.T, conv_weight, norm_gain, qkv_weight, eg)
    qkv, grad = pl.pallas_call(
        finish,
        name="finish",
        out_shape=(jax.ShapeDtypeStruct((R, Q), BF16), jax.ShapeDtypeStruct((KW, ZB, O), F32)),
        in_specs=[any_] * 2,
        out_specs=(any_, any_),
        scratch_shapes=[v((R, Q), BF16), v((KW, ZB, O), BF16), v((KW, ZB, O), F32), pltpu.SemaphoreType.DMA((4,))],
    )(qkv, grad)
    return qkv[None], grad.transpose(1, 0, 2)


def solution(mesh):
    return jax.shard_map(
        on_device,
        mesh=mesh,
        in_specs=(
            P("dp", "seq", "mp"),
            P(None, None, "mp"),
            P("mp"),
            P(None, "mp"),
            P("dp", "seq", "mp"),
        ),
        out_specs=(P("dp", "seq", "mp"), P("seq", None, "mp")),
        check_vma=False,
    )
```

```python
import jax
import jax.numpy as jnp
from jax import lax
from jax.experimental import pallas as pl
from jax.experimental.pallas import tpu as pltpu
from jax.sharding import PartitionSpec as P

MESH = pl.DeviceIdType.MESH
BF16, F32 = jnp.bfloat16, jnp.float32
KW = 5
T = 1024
R = 512
CB = 320
O = 384
OT = O // 128
C = 4 * CB
N = KW * O
Q = 640
TB = 128
TC = 256
XB = 320
ZB = 80
COLS = (9 * 128, 6 * 128)
PIECE = 3 * 128
Y0 = 8

OWN_R, OWN_L, FWD_R, FWD_L = 0, 8, 16, 24
EDGE_UP, EDGE_DOWN, GRAD_UP, GRAD_DOWN, RIM, GAIN = 32, 33, 34, 35, 35, 38
ENC_R, ENC_L, EFWD_R, EFWD_L = 42, 44, 46, 47
SWAP = 48
SPLIT = (0, 4)
X1R, X1L, X2R, X2L = 53, 54, 55, 57
ZUA, ZUB, ZDA, ZDB = 59, 63, 67, 71
DUP, DDN, DSW = 75, 76, 77
COPIES = 79


def kernel(
    xt_hbm, w_hbm, gain_hbm, qw_hbm, eg_hbm, qout, cgo,
    xt, ends, edge, rim, egrim, wcat, gain, qw, eg, xrow, yb, pgb, pgcat, enc, norm,
    psend, precv, gown, x1l, x1r, x2l, x2r, zb, zr, zs, zr1, zs1, u1l, u1r, u2l, u2r, fin0, fin1,
    lsem, ssem, rsem,
):
    seq, mp, dp = lax.axis_index("seq"), lax.axis_index("mp"), lax.axis_index("dp")
    x, zl = seq // 4, seq % 4
    zh, core = dp // 2, dp % 2
    z = zh * 4 + zl

    def at(s=None, m=None, d=None):
        return {"seq": seq if s is None else s, "mp": mp if m is None else m, "dp": dp if d is None else d}

    def z_at(zn):
        return at(s=x * 4 + zn % 4, d=(zn // 4) * 2 + core)

    y_right, y_left = at(m=(mp + 1) % 4), at(m=(mp + 3) % 4)
    s_up, s_down = at(s=(seq + 1) % 16), at(s=(seq + 15) % 16)
    x_right, x_left = at(s=(seq + 4) % 16), at(s=(seq + 12) % 16)
    z_up, z_down = z_at((z + 1) % 8), z_at((z + 7) % 8)
    partner = at(d=zh * 2 + 1 - core)
    z_up2, z_down2 = z_at((z + 2) % 8), z_at((z + 6) % 8)

    local = []

    def load(src, dst):
        copy = pltpu.make_async_copy(src, dst, lsem.at[len(local)])
        copy.start()
        local.append(copy)
        return copy

    own_rows = pl.ds(pl.multiple_of(mp * CB, CB), CB)
    end_loads = [load(xt_hbm.at[:, pl.ds(e * (T - 128), 128)], ends.at[e, pl.ds(0, CB)]) for e in (0, 1)]
    own_x = load(xt_hbm, xt.at[own_rows])
    loads = [load(w_hbm.at[k], wcat.at[:, pl.ds(k * O, O)]) for k in range(KW)]
    eg_load = load(eg_hbm, eg)
    gain_load = load(gain_hbm, gain.at[mp])
    qw_load = load(qw_hbm, qw)

    barrier = pltpu.get_barrier_semaphore()
    peers = [y_right, y_left, at(m=(mp + 2) % 4), s_up, s_down, x_right, x_left, z_up, z_down, z_up2, z_down2, partner]
    for peer in peers:
        pl.semaphore_signal(barrier, inc=1, device_id=peer, device_id_type=MESH)
    pl.semaphore_wait(barrier, len(peers))

    sent = []

    def remote(src, dst, i, peer):
        return pltpu.make_async_remote_copy(
            src_ref=src, dst_ref=dst, send_sem=ssem.at[i], recv_sem=rsem.at[i], device_id=peer, device_id_type=MESH
        )

    def send(src, dst, i, peer):
        copy = remote(src, dst, i, peer)
        copy.start()
        sent.append(copy)

    def arrived(dst, i):
        remote(dst, dst, i, y_right).wait_recv()

    def block(owner, half, tb):
        first = owner * CB + (0 if half is None else half * (CB // 2))
        size = CB if half is None else CB // 2
        return xt.at[pl.ds(pl.multiple_of(first, CB // 2), size), pl.ds(tb * TB, TB)]

    m_left, m_right, m_far = (mp + 3) % 4, (mp + 1) % 4, (mp + 2) % 4

    def send_own(tb):
        src = xt_hbm.at[:, pl.ds(tb * TB, TB)]
        send(src, block(mp, None, tb), OWN_R + tb, y_right)
        send(src, block(mp, None, tb), OWN_L + tb, y_left)

    def forward(tb):
        arrived(block(m_left, None, tb), OWN_R + tb)
        send(block(m_left, 0, tb), block(m_left, 0, tb), FWD_R + tb, y_right)
        arrived(block(m_right, None, tb), OWN_L + tb)
        send(block(m_right, 1, tb), block(m_right, 1, tb), FWD_L + tb, y_left)

    def complete(tb):
        arrived(block(m_far, 0, tb), FWD_R + tb)
        arrived(block(m_far, 1, tb), FWD_L + tb)

    send_own(0)
    send_own(1)
    for d in (1, 2, 3):
        send(gain_hbm, gain.at[mp], GAIN + d, at(m=(mp + d) % 4))
    send(eg_hbm.at[pl.ds(R - 16, 16)], egrim.at[0], GRAD_UP, s_up)
    send(eg_hbm.at[pl.ds(0, 16)], egrim.at[1], GRAD_DOWN, s_down)
    for copy in end_loads:
        copy.wait()
    for e in (0, 1):
        ends[e, CB:, :] = jnp.zeros((O - CB, 128), BF16)
        edge[e] = ends[e].T[112 * e : 112 * e + 16, :]
    send(edge.at[1], rim.at[mp, pl.ds(0, 16)], EDGE_UP, s_up)
    send(edge.at[0], rim.at[mp, pl.ds(16, 16)], EDGE_DOWN, s_down)
    own_x.wait()

    def tap_products(g, half):
        if half == 0:
            xrow[...] = xt[:, g * TC : (g + 1) * TC].T

        def tile(n, carry):
            cols = pl.ds(pl.multiple_of(n * 256, 256), 256)
            y = jnp.dot(xrow[...], wcat[:, cols], preferred_element_type=F32)
            yb[2 * n, pl.ds(Y0 + g * TC, TC), :] = y[:, :128]
            yb[2 * n + 1, pl.ds(Y0 + g * TC, TC), :] = y[:, 128:]
            return carry

        if half == 0:
            lax.fori_loop(0, 4, tile, 0)
        else:
            lax.fori_loop(4, N // 256, tile, 0)
            y = jnp.dot(xrow[...], wcat[:, N - 128 :], preferred_element_type=F32)
            yb[N // 128 - 1, pl.ds(Y0 + g * TC, TC), :] = y

    def rim_products():
        for d in (1, 2, 3):
            owner = (mp + 4 - d) % 4
            arrived(rim.at[owner], RIM + d)
        before = jnp.where(seq > 0, 1.0, 0.0).astype(F32)
        after = jnp.where(seq < 15, 1.0, 0.0).astype(F32)

        def tile(n, carry):
            cols = pl.ds(pl.multiple_of(n * 128, 128), 128)
            y = jnp.zeros((32, 128), F32)
            for m in range(4):
                y += jnp.dot(rim[m][:, :CB], wcat[m * CB : (m + 1) * CB, cols], preferred_element_type=F32)
            yb[n, pl.ds(0, 8), :] = y[8:16] * before
            yb[n, pl.ds(Y0 + T, 8), :] = y[16:24] * after
            return carry

        lax.fori_loop(0, N // 128, tile, 0)

    def gelu(v):
        v2 = v * v
        th = jnp.tanh(v * (0.7978845608 + (0.7978845608 * 0.044715) * v2))
        half = 0.5 + 0.5 * th
        slope = half + 0.5 * v * (1.0 - th * th) * (0.7978845608 + (0.7978845608 * 0.134145) * v2)
        return v * half, slope

    def pre(o, row, rows, stride):
        taps = [yb[k * OT + o, pl.ds(row + k - 2, rows, stride=stride), :] for k in range(KW)]
        return taps[0] + taps[1] + taps[2] + taps[3] + taps[4]

    STEP = 32

    def activations(first, count):
        def rows_of(i, carry):
            j = pl.multiple_of(first + i * STEP, STEP)
            for o in range(OT):
                lanes = pl.ds(o * 128, 128)
                act_e, slope_e = gelu(pre(o, Y0 + 2 * j, STEP, 2))
                act_o, slope_o = gelu(pre(o, Y0 + 2 * j + 1, STEP, 2))
                g = 0.5 * eg[pl.ds(j, STEP), lanes].astype(F32)
                enc[mp, pl.ds(j, STEP), lanes] = (0.5 * (act_e + act_o)).astype(BF16)
                pgb[o, pl.ds(Y0 + 2 * j, STEP, stride=2), :] = slope_e * g
                pgb[o, pl.ds(Y0 + 2 * j + 1, STEP, stride=2), :] = slope_o * g
            return carry

        lax.fori_loop(0, count // STEP, rows_of, 0)

    def rim_gradients(side):
        before = jnp.where(seq > 0, 0.5, 0.0).astype(F32)
        after = jnp.where(seq < 15, 0.5, 0.0).astype(F32)
        last, first = egrim[0, 8:16, :].astype(F32), egrim[1, 0:8, :].astype(F32)
        for o in range(OT):
            lanes = slice(o * 128, (o + 1) * 128)
            row, g = ((Y0 - 2, last[7:8, lanes] * before), (Y0 + T, first[0:1, lanes] * after))[side]
            for r in (row, row + 1):
                slope = gelu(pre(o, r, 1, 1))[1]
                pgb[o, pl.ds(r, 1), :] = slope * g

    PSTEP = 64

    def gradient_columns(first, count):
        def rows_of(i, carry):
            s = pl.multiple_of(first + i * PSTEP, PSTEP)
            for k in range(KW):
                for o in range(OT):
                    pgcat[pl.ds(s, PSTEP), (k * OT + o) * 128 : (k * OT + o + 1) * 128] = pgb[
                        o, pl.ds(Y0 + s + 2 - k, PSTEP), :
                    ].astype(BF16)
            return carry

        lax.fori_loop(0, count // PSTEP, rows_of, 0)

    def serve(i):
        forward(i)
        if i + 2 < T // TB:
            send_own(i + 2)

    def group(g):
        complete(2 * g)
        complete(2 * g + 1)

    serve(0)
    arrived(rim.at[mp, pl.ds(0, 16)], EDGE_UP)
    arrived(rim.at[mp, pl.ds(16, 16)], EDGE_DOWN)
    for d in (1, 2, 3):
        send(rim.at[mp], rim.at[mp], RIM + d, at(m=(mp + d) % 4))
    serve(1)
    for copy in loads:
        copy.wait()
    serve(2)
    group(0)
    tap_products(0, 0)
    serve(3)
    tap_products(0, 1)
    rim_products()
    serve(4)
    group(1)
    tap_products(1, 0)
    serve(5)
    tap_products(1, 1)
    eg_load.wait()
    activations(0, 224)
    arrived(egrim.at[0], GRAD_UP)
    arrived(egrim.at[1], GRAD_DOWN)
    rim_gradients(0)
    serve(6)
    gradient_columns(0, 384)
    group(2)
    tap_products(2, 0)
    serve(7)
    tap_products(2, 1)
    activations(224, 128)
    group(3)
    tap_products(3, 0)
    tap_products(3, 1)
    activations(352, 160)
    rim_gradients(1)

    def half_rows(owner, e):
        return enc.at[owner, pl.ds(e * (R // 2), R // 2)]

    send(half_rows(mp, 0), half_rows(mp, 0), ENC_R, y_right)
    send(half_rows(mp, 1), half_rows(mp, 1), ENC_L + 1, y_left)
    send(half_rows(mp, 1), half_rows(mp, 1), ENC_R + 1, y_right)
    send(half_rows(mp, 0), half_rows(mp, 0), ENC_L, y_left)
    gradient_columns(384, 640)

    def rows_of_z(g):
        return jnp.concatenate(
            [xt[pl.ds(pl.multiple_of(xb * XB + g * ZB, ZB), ZB), :] for xb in range(4)], axis=0
        )

    def products(left, owner, write):
        first, width = owner * COLS[0], COLS[owner]

        def tile(n, carry):
            lane = pl.multiple_of(n * 256, 256)
            write(lane, 256, jnp.dot(left, pgcat[:, pl.ds(first + lane, 256)], preferred_element_type=F32))
            return carry

        lax.fori_loop(0, width // 256, tile, 0)
        if width % 256:
            lane = width // 256 * 256
            write(lane, 128, jnp.dot(left, pgcat[:, pl.ds(first + lane, 128)], preferred_element_type=F32))

    def left_rows(kind, b, half):
        if kind:
            return rows_of_z(b)
        first, rows = (0, XB) if half is None else (half * (XB // 2), XB // 2)
        return xt[pl.ds(pl.multiple_of(b * XB + first, XB // 2), rows), :]

    def span(half):
        return pl.ds(0, XB) if half is None else pl.ds(half * (XB // 2), XB // 2)

    def theirs(other, step, b, half=None):
        rows = span(half)

        def write(lane, width, value):
            psend[b, rows, pl.ds(lane, width)] = value.astype(BF16)

        products(left_rows(other, b, half), other, write)
        cols = pl.ds(0, COLS[other])
        send(psend.at[b, rows, cols], precv.at[b, rows, cols], SWAP + step, partner)

    def ours(me, step, b, half=None, waits=True):
        rows = span(half)
        if waits:
            arrived(precv.at[b, span(half if me == 0 and step in SPLIT else None), pl.ds(0, COLS[me])], SWAP + step)

        def write(lane, width, value):
            cols = pl.ds(lane, width)
            gown[b, rows, cols] = (value + precv[b, rows, cols].astype(F32)).astype(BF16)

        products(left_rows(me, b, half), me, write)

    def add(dst, src):
        for r in range(0, dst.shape[0], 16):
            rows = pl.ds(r, 16)
            dst[rows, :] = (dst[rows, :].astype(F32) + src[rows, :].astype(F32)).astype(BF16)

    def add_to(dst, a, b):
        for r in range(0, dst.shape[0], 16):
            rows = pl.ds(r, 16)
            dst[rows, :] = (a[rows, :].astype(F32) + b[rows, :].astype(F32)).astype(BF16)

    def add3(dst, a, b, c):
        for r in range(0, dst.shape[0], 16):
            rows = pl.ds(r, 16)
            dst[rows, :] = (a[rows, :].astype(F32) + b[rows, :].astype(F32) + c[rows, :].astype(F32)).astype(BF16)

    def forward_encoded():
        arrived(half_rows(m_left, 0), ENC_R)
        send(half_rows(m_left, 0), half_rows(m_left, 0), EFWD_R, y_right)
        arrived(half_rows(m_right, 1), ENC_L + 1)
        send(half_rows(m_right, 1), half_rows(m_right, 1), EFWD_L, y_left)

    def encoded_complete():
        arrived(half_rows(m_left, 1), ENC_R + 1)
        arrived(half_rows(m_right, 0), ENC_L)
        arrived(half_rows(m_far, 0), EFWD_R)
        arrived(half_rows(m_far, 1), EFWD_L)
        gain_load.wait()
        for d in (1, 2, 3):
            arrived(gain.at[(mp + 4 - d) % 4], GAIN + d)
        qw_load.wait()

    def heads(part):
        def normalize(i, carry):
            rows = pl.ds(pl.multiple_of(part * 128 + i * 32, 32), 32)
            values = [enc[m, rows, :].astype(F32) for m in range(4)]
            total = jnp.sum(values[0] + values[1] + values[2] + values[3], axis=1, keepdims=True)
            square = jnp.sum(sum(v * v for v in values), axis=1, keepdims=True)
            mean = total / (4 * O)
            scale = lax.rsqrt(square / (4 * O) - mean * mean + 1e-05)
            for m in range(4):
                norm[rows, m * O : (m + 1) * O] = ((values[m] - mean) * scale * gain[m]).astype(BF16)
            return carry

        lax.fori_loop(0, 4, normalize, 0)
        rows = pl.ds(part * 128, 128)
        qout[rows, :] = jnp.dot(norm[rows, :], qw[...], preferred_element_type=F32).astype(BF16)

    top, bottom = pl.ds(0, XB // 2), pl.ds(XB // 2, XB // 2)
    xf, xr, xl = (x + 2) % 4, (x + 1) % 4, (x + 3) % 4
    gf, gr, gl = (zl + 2) % 4, (zl + 1) % 4, (zl + 3) % 4

    lower, upper = (z + 6) % 8 // 4, (z + 2) % 8 // 4

    def z_chain(step, part, base, received, staged):
        for sign, ids, peer in ((1, (ZUA, ZUB), z_up), (-1, (ZDA, ZDB), z_down)):
            z_hop(sign, step, part, base, received, staged, ids[part] + step - 1, peer)

    def z_hop(sign, step, part, base, received, staged, i, peer):
        src = base(sign, step, part)
        if step > 1 + part:
            arrived(received(sign, step - 1, part), i - 1)
            dst = staged(sign, step, part)
            add_to(dst, src, received(sign, step - 1, part))
            src = dst
        send(src, received(sign, step, part), i, peer)

    def z_last(received):
        for sign, ids in ((1, (ZUA, ZUB)), (-1, (ZDA, ZDB))):
            for part in (0, 1):
                arrived(received(sign, 4, part), ids[part] + 3)

    shared = len(sent)

    @pl.when(core == 0)
    def _():
        theirs(1, 0, gf)
        ours(0, 0, xf, 0)
        send(gown.at[xf, top], x1l, X1R, x_right)
        ours(0, 4, xf, 1)
        send(gown.at[xf, bottom], x1r, X1L, x_left)
        theirs(1, 1, gr)
        ours(0, 1, xr, 1)
        send(gown.at[xr, bottom], x2l.at[bottom], X2R + 1, x_right)
        ours(0, 1, xr, 0, waits=False)
        theirs(1, 2, gl)
        forward_encoded()
        theirs(1, 3, zl)
        ours(0, 2, xl)
        send(gown.at[xl, top], x2r.at[top], X2L, x_left)
        arrived(x1l, X1R)
        add(gown.at[xr, top], x1l)
        send(gown.at[xr, top], x2l.at[top], X2R, x_right)
        arrived(x1r, X1L)
        add(gown.at[xl, bottom], x1r)
        send(gown.at[xl, bottom], x2r.at[bottom], X2L + 1, x_left)
        ours(0, 3, x)
        encoded_complete()
        for part in range(4):
            heads(part)
        for half, rows in ((0, top), (1, bottom)):
            arrived(x2l.at[rows], X2R + half)
            arrived(x2r.at[rows], X2L + half)
        for g in range(4):
            rows = pl.ds(g * ZB, ZB)
            add3(zb.at[g], gown.at[x, rows], x2l.at[rows], x2r.at[rows])

        spans = (pl.ds(0, 640), pl.ds(640, 512))

        def cols(sign, part):
            return spans[part if sign == 1 else 1 - part]

        def way(sign):
            return 0 if sign == 1 else 1

        def base(sign, step, part):
            return zb.at[(zl + 5 - step if sign == 1 else zl + 3 + step) % 4, :, cols(sign, part)]

        def received(sign, step, part):
            return zr.at[way(sign), step - 1, :, cols(sign, part)]

        def staged(sign, step, part):
            return zs.at[way(sign), step - 2, :, cols(sign, part)]

        z_chain(1, 0, base, received, staged)
        z_chain(2, 1, base, received, staged)
        z_chain(2, 0, base, received, staged)
        z_chain(3, 1, base, received, staged)
        z_chain(3, 0, base, received, staged)
        z_chain(4, 1, base, received, staged)
        z_chain(4, 0, base, received, staged)
        z_last(received)
        add3(fin0, zb.at[zl], zr.at[0, 3], zr.at[1, 3])
        send(fin0, fin0, DSW, partner)
        arrived(fin1.at[lower], DSW)
        arrived(fin1.at[upper], DSW + 1)
        for copy in sent:
            copy.wait_send()

    @pl.when(core == 1)
    def _():
        del sent[shared:]
        theirs(0, 0, xf, 0)
        theirs(0, 4, xf, 1)
        theirs(0, 1, xr)
        ours(1, 0, gf)

        def piece(zo):
            return gown.at[(zo + 2) % 4, :, pl.ds(pl.multiple_of(zo // 4 * PIECE, 128), PIECE)]

        def half(ref, sign, part):
            return ref.at[top if (part == 0) == (sign == 1) else bottom]

        def base(sign, step, part):
            return half(piece((z + 5 - step if sign == 1 else z + 3 + step) % 8), sign, part)

        def received(sign, step, part):
            return half(zr1.at[0 if sign == 1 else 1, step - 1], sign, part)

        def hop(sign, step, part):
            i, peer = ((ZUA, ZUB)[part], z_up) if sign == 1 else ((ZDA, ZDB)[part], z_down)
            z_hop(sign, step, part, base, received, base, i + step - 1, peer)

        z_chain(1, 0, base, received, base)
        theirs(0, 2, xl)
        ours(1, 1, gr)
        hop(1, 2, 1)
        hop(1, 2, 0)
        ours(1, 2, gl)
        hop(-1, 2, 1)
        hop(-1, 2, 0)
        theirs(0, 3, x)
        ours(1, 3, zl)
        z_chain(3, 1, base, received, base)
        z_chain(3, 0, base, received, base)
        forward_encoded()
        z_chain(4, 1, base, received, base)
        z_chain(4, 0, base, received, base)
        encoded_complete()
        heads(0)
        z_last(received)
        add3(zs1, piece(z), zr1.at[0, 3], zr1.at[1, 3])

        def rows_at(xb, first, rows):
            return zs1.at[pl.ds(pl.multiple_of(xb * ZB + first, 16), rows)]

        send(rows_at(xf, 0, 48), u1l, X1R, x_right)
        send(rows_at(xf, 48, 32), u1r, X1L, x_left)
        heads(1)
        arrived(u1l, X1R)
        add(rows_at(xr, 0, 48), u1l)
        send(rows_at(xr, 0, ZB), u2l, X2R, x_right)
        arrived(u1r, X1L)
        add(rows_at(xl, 48, 32), u1r)
        send(rows_at(xl, 0, ZB), u2r, X2L, x_left)
        heads(2)
        arrived(u2l, X2R)
        arrived(u2r, X2L)
        mine = rows_at(x, 0, ZB)
        add3(mine, mine, u2l, u2r)
        send(mine, fin1.at[zh], DUP, z_up2)
        send(mine, fin1.at[zh], DDN, z_down2)
        heads(3)
        arrived(fin1.at[lower], DUP)
        send(fin1.at[lower], fin1.at[lower], DSW, partner)
        arrived(fin1.at[upper], DDN)
        send(fin1.at[upper], fin1.at[upper], DSW + 1, partner)
        arrived(fin0, DSW)
        for copy in sent:
            copy.wait_send()

    for i in range(N // 128):
        if i < 9:
            src = fin0.at[:, pl.ds(i * 128, 128)]
        else:
            src = fin1.at[(i - 9) // 3, :, pl.ds((i - 9) % 3 * 128, 128)]
        cgo[i // OT, :, pl.ds((i % OT) * 128, 128)] = src[...].astype(F32)


def finish(qkv_in, grad_in, qkv_out, grad_out, sem):
    copies = [
        pltpu.make_async_copy(grad_in, grad_out, sem.at[0]),
        pltpu.make_async_copy(qkv_in, qkv_out, sem.at[1]),
    ]
    for copy in copies:
        copy.start()
    for copy in copies:
        copy.wait()


def on_device(block_input, conv_weight, norm_gain, qkv_weight, encoder_grad):
    xin, eg = block_input[0], encoder_grad[0]
    any_ = pl.BlockSpec(memory_space=pl.ANY)
    v = pltpu.VMEM
    qkv, grad = pl.pallas_call(
        kernel,
        name="block",
        out_shape=(jax.ShapeDtypeStruct((R, Q), BF16), jax.ShapeDtypeStruct((KW, ZB, O), F32)),
        in_specs=[pl.BlockSpec(memory_space=pltpu.HBM)] * 5,
        out_specs=(pl.BlockSpec(memory_space=pltpu.VMEM),) * 2,
        scratch_shapes=[
            v((C, T), BF16), v((2, O, 128), BF16), v((2, 16, O), BF16), v((4, 32, O), BF16), v((2, 16, O), BF16),
            v((C, N), BF16), v((4, O), F32), v((4 * O, Q), BF16), v((R, O), BF16),
            v((TC, C), BF16), v((N // 128, T + 16, 128), F32), v((OT, T + 16, 128), F32), v((T, N), BF16),
            v((4, R, O), BF16), v((R, 4 * O), BF16),
            v((4, XB, COLS[0]), BF16), v((4, XB, COLS[0]), BF16), v((4, XB, COLS[0]), BF16),
            v((XB // 2, COLS[0]), BF16), v((XB // 2, COLS[0]), BF16), v((XB, COLS[0]), BF16), v((XB, COLS[0]), BF16),
            v((4, ZB, COLS[0]), BF16), v((2, 4, ZB, COLS[0]), BF16), v((2, 3, ZB, COLS[0]), BF16),
            v((2, 4, XB, PIECE), BF16), v((XB, PIECE), BF16),
            v((48, PIECE), BF16), v((32, PIECE), BF16), v((ZB, PIECE), BF16), v((ZB, PIECE), BF16),
            v((ZB, COLS[0]), BF16), v((2, ZB, PIECE), BF16),
            pltpu.SemaphoreType.DMA((16,)), pltpu.SemaphoreType.DMA((COPIES,)), pltpu.SemaphoreType.DMA((COPIES,)),
        ],
        compiler_params=pltpu.CompilerParams(collective_id=0, has_side_effects=True, vmem_limit_bytes=50 * 2**20),
    )(*(pltpu.with_memory_space_constraint(a, pltpu.HBM) for a in (xin.T, conv_weight, norm_gain, qkv_weight, eg)))
    qkv, grad = pl.pallas_call(
        finish,
        name="finish",
        out_shape=(jax.ShapeDtypeStruct((R, Q), BF16), jax.ShapeDtypeStruct((KW, ZB, O), F32)),
        in_specs=[any_] * 2,
        out_specs=(any_, any_),
        scratch_shapes=[pltpu.SemaphoreType.DMA((2,))],
        compiler_params=pltpu.CompilerParams(vmem_limit_bytes=4 * 2**20),
    )(qkv, grad)
    return qkv[None], grad.transpose(1, 0, 2)


def solution(mesh):
    return jax.shard_map(
        on_device,
        mesh=mesh,
        in_specs=(
            P("dp", "seq", "mp"),
            P(None, None, "mp"),
            P("mp"),
            P(None, "mp"),
            P("dp", "seq", "mp"),
        ),
        out_specs=(P("dp", "seq", "mp"), P("seq", None, "mp")),
        check_vma=False,
    )
```

```python
import jax
import jax.numpy as jnp
from jax import lax
from jax.experimental import pallas as pl
from jax.experimental.pallas import tpu as pltpu
from jax.sharding import PartitionSpec as P

MESH = pl.DeviceIdType.MESH
BF16, F32 = jnp.bfloat16, jnp.float32
KW = 5
T = 1024
R = 512
CB = 320
O = 384
OT = O // 128
C = 4 * CB
N = KW * O
Q = 640
TB = 128
TC = 256
XB = 320
ZB = 80
COLS = (7 * 128, 8 * 128)
PIECE = 4 * 128
Y0 = 8

OWN_R, OWN_L, FWD_R, FWD_L = 0, 8, 16, 24
EDGE_UP, EDGE_DOWN, GRAD_UP, GRAD_DOWN, RIM, GAIN = 32, 33, 34, 35, 35, 38
ENC_R, ENC_L, EFWD_R, EFWD_L = 42, 44, 46, 47
SWAP = 48
SPLIT = (0, 4)
X1R, X1L, X2R, X2L = 53, 54, 55, 57
ZUA, ZUB, ZDA, ZDB = 59, 63, 67, 71
DUP, DDN, DSW = 75, 76, 77
COPIES = 79


def kernel(
    xt_hbm, w_hbm, gain_hbm, qw_hbm, eg_hbm, qout, cgo,
    xt, ends, edge, rim, egrim, wcat, gain, qw, eg, xrow, yb, pgb, pgcat, enc, norm,
    psend, precv, gown, x1l, x1r, x2l, x2r, zb, zr, zs, zr1, zs1, u1l, u1r, u2l, u2r, fin0, fin1,
    lsem, ssem, rsem,
):
    seq, mp, dp = lax.axis_index("seq"), lax.axis_index("mp"), lax.axis_index("dp")
    x, zl = seq // 4, seq % 4
    zh, core = dp // 2, dp % 2
    z = zh * 4 + zl

    def at(s=None, m=None, d=None):
        return {"seq": seq if s is None else s, "mp": mp if m is None else m, "dp": dp if d is None else d}

    def z_at(zn):
        return at(s=x * 4 + zn % 4, d=(zn // 4) * 2 + core)

    y_right, y_left = at(m=(mp + 1) % 4), at(m=(mp + 3) % 4)
    s_up, s_down = at(s=(seq + 1) % 16), at(s=(seq + 15) % 16)
    x_right, x_left = at(s=(seq + 4) % 16), at(s=(seq + 12) % 16)
    z_up, z_down = z_at((z + 1) % 8), z_at((z + 7) % 8)
    partner = at(d=zh * 2 + 1 - core)
    z_up2, z_down2 = z_at((z + 2) % 8), z_at((z + 6) % 8)

    local = []

    def load(src, dst):
        copy = pltpu.make_async_copy(src, dst, lsem.at[len(local)])
        copy.start()
        local.append(copy)
        return copy

    own_rows = pl.ds(pl.multiple_of(mp * CB, CB), CB)
    end_loads = [load(xt_hbm.at[:, pl.ds(e * (T - 128), 128)], ends.at[e, pl.ds(0, CB)]) for e in (0, 1)]
    own_x = load(xt_hbm, xt.at[own_rows])
    loads = [load(w_hbm.at[k], wcat.at[:, pl.ds(k * O, O)]) for k in range(KW)]
    eg_load = load(eg_hbm, eg)
    gain_load = load(gain_hbm, gain.at[mp])
    qw_load = load(qw_hbm, qw)

    barrier = pltpu.get_barrier_semaphore()
    peers = [y_right, y_left, at(m=(mp + 2) % 4), s_up, s_down, x_right, x_left, z_up, z_down, z_up2, z_down2, partner]
    for peer in peers:
        pl.semaphore_signal(barrier, inc=1, device_id=peer, device_id_type=MESH)
    pl.semaphore_wait(barrier, len(peers))

    sent = []

    def remote(src, dst, i, peer):
        return pltpu.make_async_remote_copy(
            src_ref=src, dst_ref=dst, send_sem=ssem.at[i], recv_sem=rsem.at[i], device_id=peer, device_id_type=MESH
        )

    def send(src, dst, i, peer):
        copy = remote(src, dst, i, peer)
        copy.start()
        sent.append(copy)

    def arrived(dst, i):
        remote(dst, dst, i, y_right).wait_recv()

    def block(owner, half, tb):
        first = owner * CB + (0 if half is None else half * (CB // 2))
        size = CB if half is None else CB // 2
        return xt.at[pl.ds(pl.multiple_of(first, CB // 2), size), pl.ds(tb * TB, TB)]

    m_left, m_right, m_far = (mp + 3) % 4, (mp + 1) % 4, (mp + 2) % 4

    def send_own(tb):
        src = xt_hbm.at[:, pl.ds(tb * TB, TB)]
        send(src, block(mp, None, tb), OWN_R + tb, y_right)
        send(src, block(mp, None, tb), OWN_L + tb, y_left)

    def forward(tb):
        arrived(block(m_left, None, tb), OWN_R + tb)
        send(block(m_left, 0, tb), block(m_left, 0, tb), FWD_R + tb, y_right)
        arrived(block(m_right, None, tb), OWN_L + tb)
        send(block(m_right, 1, tb), block(m_right, 1, tb), FWD_L + tb, y_left)

    def complete(tb):
        arrived(block(m_far, 0, tb), FWD_R + tb)
        arrived(block(m_far, 1, tb), FWD_L + tb)

    send_own(0)
    send_own(1)
    for d in (1, 2, 3):
        send(gain_hbm, gain.at[mp], GAIN + d, at(m=(mp + d) % 4))
    send(eg_hbm.at[pl.ds(R - 16, 16)], egrim.at[0], GRAD_UP, s_up)
    send(eg_hbm.at[pl.ds(0, 16)], egrim.at[1], GRAD_DOWN, s_down)
    for copy in end_loads:
        copy.wait()
    for e in (0, 1):
        ends[e, CB:, :] = jnp.zeros((O - CB, 128), BF16)
        edge[e] = ends[e].T[112 * e : 112 * e + 16, :]
    send(edge.at[1], rim.at[mp, pl.ds(0, 16)], EDGE_UP, s_up)
    send(edge.at[0], rim.at[mp, pl.ds(16, 16)], EDGE_DOWN, s_down)
    own_x.wait()

    def tap_products(g, half):
        if half == 0:
            xrow[...] = xt[:, g * TC : (g + 1) * TC].T

        def tile(n, carry):
            cols = pl.ds(pl.multiple_of(n * 256, 256), 256)
            y = jnp.dot(xrow[...], wcat[:, cols], preferred_element_type=F32)
            yb[2 * n, pl.ds(Y0 + g * TC, TC), :] = y[:, :128]
            yb[2 * n + 1, pl.ds(Y0 + g * TC, TC), :] = y[:, 128:]
            return carry

        if half == 0:
            lax.fori_loop(0, 4, tile, 0)
        else:
            lax.fori_loop(4, N // 256, tile, 0)
            y = jnp.dot(xrow[...], wcat[:, N - 128 :], preferred_element_type=F32)
            yb[N // 128 - 1, pl.ds(Y0 + g * TC, TC), :] = y

    def rim_products():
        for d in (1, 2, 3):
            owner = (mp + 4 - d) % 4
            arrived(rim.at[owner], RIM + d)
        before = jnp.where(seq > 0, 1.0, 0.0).astype(F32)
        after = jnp.where(seq < 15, 1.0, 0.0).astype(F32)

        def tile(n, carry):
            cols = pl.ds(pl.multiple_of(n * 128, 128), 128)
            y = jnp.zeros((32, 128), F32)
            for m in range(4):
                y += jnp.dot(rim[m][:, :CB], wcat[m * CB : (m + 1) * CB, cols], preferred_element_type=F32)
            yb[n, pl.ds(0, 8), :] = y[8:16] * before
            yb[n, pl.ds(Y0 + T, 8), :] = y[16:24] * after
            return carry

        lax.fori_loop(0, N // 128, tile, 0)

    def gelu(v):
        v2 = v * v
        th = jnp.tanh(v * (0.7978845608 + (0.7978845608 * 0.044715) * v2))
        half = 0.5 + 0.5 * th
        slope = half + 0.5 * v * (1.0 - th * th) * (0.7978845608 + (0.7978845608 * 0.134145) * v2)
        return v * half, slope

    def pre(o, row, rows, stride):
        taps = [yb[k * OT + o, pl.ds(row + k - 2, rows, stride=stride), :] for k in range(KW)]
        return taps[0] + taps[1] + taps[2] + taps[3] + taps[4]

    STEP = 32

    def activations(first, count):
        def rows_of(i, carry):
            j = pl.multiple_of(first + i * STEP, STEP)
            for o in range(OT):
                lanes = pl.ds(o * 128, 128)
                act_e, slope_e = gelu(pre(o, Y0 + 2 * j, STEP, 2))
                act_o, slope_o = gelu(pre(o, Y0 + 2 * j + 1, STEP, 2))
                g = 0.5 * eg[pl.ds(j, STEP), lanes].astype(F32)
                enc[mp, pl.ds(j, STEP), lanes] = (0.5 * (act_e + act_o)).astype(BF16)
                pgb[o, pl.ds(Y0 + 2 * j, STEP, stride=2), :] = slope_e * g
                pgb[o, pl.ds(Y0 + 2 * j + 1, STEP, stride=2), :] = slope_o * g
            return carry

        lax.fori_loop(0, count // STEP, rows_of, 0)

    def rim_gradients(side):
        before = jnp.where(seq > 0, 0.5, 0.0).astype(F32)
        after = jnp.where(seq < 15, 0.5, 0.0).astype(F32)
        last, first = egrim[0, 8:16, :].astype(F32), egrim[1, 0:8, :].astype(F32)
        for o in range(OT):
            lanes = slice(o * 128, (o + 1) * 128)
            row, g = ((Y0 - 2, last[7:8, lanes] * before), (Y0 + T, first[0:1, lanes] * after))[side]
            for r in (row, row + 1):
                slope = gelu(pre(o, r, 1, 1))[1]
                pgb[o, pl.ds(r, 1), :] = slope * g

    PSTEP = 64

    def gradient_columns(first, count):
        def rows_of(i, carry):
            s = pl.multiple_of(first + i * PSTEP, PSTEP)
            for k in range(KW):
                for o in range(OT):
                    pgcat[pl.ds(s, PSTEP), (k * OT + o) * 128 : (k * OT + o + 1) * 128] = pgb[
                        o, pl.ds(Y0 + s + 2 - k, PSTEP), :
                    ].astype(BF16)
            return carry

        lax.fori_loop(0, count // PSTEP, rows_of, 0)

    def serve(i):
        forward(i)
        if i + 2 < T // TB:
            send_own(i + 2)

    def group(g):
        complete(2 * g)
        complete(2 * g + 1)

    serve(0)
    arrived(rim.at[mp, pl.ds(0, 16)], EDGE_UP)
    arrived(rim.at[mp, pl.ds(16, 16)], EDGE_DOWN)
    for d in (1, 2, 3):
        send(rim.at[mp], rim.at[mp], RIM + d, at(m=(mp + d) % 4))
    serve(1)
    for copy in loads:
        copy.wait()
    serve(2)
    group(0)
    tap_products(0, 0)
    serve(3)
    tap_products(0, 1)
    rim_products()
    serve(4)
    group(1)
    tap_products(1, 0)
    serve(5)
    tap_products(1, 1)
    eg_load.wait()
    activations(0, 224)
    arrived(egrim.at[0], GRAD_UP)
    arrived(egrim.at[1], GRAD_DOWN)
    rim_gradients(0)
    serve(6)
    gradient_columns(0, 384)
    group(2)
    tap_products(2, 0)
    serve(7)
    tap_products(2, 1)
    activations(224, 128)
    group(3)
    tap_products(3, 0)
    tap_products(3, 1)
    activations(352, 160)
    rim_gradients(1)

    def half_rows(owner, e):
        return enc.at[owner, pl.ds(e * (R // 2), R // 2)]

    send(half_rows(mp, 0), half_rows(mp, 0), ENC_R, y_right)
    send(half_rows(mp, 1), half_rows(mp, 1), ENC_L + 1, y_left)
    send(half_rows(mp, 1), half_rows(mp, 1), ENC_R + 1, y_right)
    send(half_rows(mp, 0), half_rows(mp, 0), ENC_L, y_left)
    gradient_columns(384, 640)

    def rows_of_z(g):
        return jnp.concatenate(
            [xt[pl.ds(pl.multiple_of(xb * XB + g * ZB, ZB), ZB), :] for xb in range(4)], axis=0
        )

    def products(left, owner, write):
        first, width = owner * COLS[0], COLS[owner]

        def tile(n, carry):
            lane = pl.multiple_of(n * 256, 256)
            write(lane, 256, jnp.dot(left, pgcat[:, pl.ds(first + lane, 256)], preferred_element_type=F32))
            return carry

        lax.fori_loop(0, width // 256, tile, 0)
        if width % 256:
            lane = width // 256 * 256
            write(lane, 128, jnp.dot(left, pgcat[:, pl.ds(first + lane, 128)], preferred_element_type=F32))

    def left_rows(kind, b, half):
        if kind:
            return rows_of_z(b)
        first, rows = (0, XB) if half is None else (half * (XB // 2), XB // 2)
        return xt[pl.ds(pl.multiple_of(b * XB + first, XB // 2), rows), :]

    def span(half):
        return pl.ds(0, XB) if half is None else pl.ds(half * (XB // 2), XB // 2)

    def theirs(other, step, b, half=None):
        rows = span(half)

        def write(lane, width, value):
            psend[b, rows, pl.ds(lane, width)] = value.astype(BF16)

        products(left_rows(other, b, half), other, write)
        cols = pl.ds(0, COLS[other])
        send(psend.at[b, rows, cols], precv.at[b, rows, cols], SWAP + step, partner)

    def ours(me, step, b, half=None, waits=True):
        rows = span(half)
        if waits:
            arrived(precv.at[b, span(half if me == 0 and step in SPLIT else None), pl.ds(0, COLS[me])], SWAP + step)

        def write(lane, width, value):
            cols = pl.ds(lane, width)
            gown[b, rows, cols] = (value + precv[b, rows, cols].astype(F32)).astype(BF16)

        products(left_rows(me, b, half), me, write)

    def add(dst, src):
        for r in range(0, dst.shape[0], 16):
            rows = pl.ds(r, 16)
            dst[rows, :] = (dst[rows, :].astype(F32) + src[rows, :].astype(F32)).astype(BF16)

    def add_to(dst, a, b):
        for r in range(0, dst.shape[0], 16):
            rows = pl.ds(r, 16)
            dst[rows, :] = (a[rows, :].astype(F32) + b[rows, :].astype(F32)).astype(BF16)

    def add3(dst, a, b, c):
        for r in range(0, dst.shape[0], 16):
            rows = pl.ds(r, 16)
            dst[rows, :] = (a[rows, :].astype(F32) + b[rows, :].astype(F32) + c[rows, :].astype(F32)).astype(BF16)

    def forward_encoded():
        arrived(half_rows(m_left, 0), ENC_R)
        send(half_rows(m_left, 0), half_rows(m_left, 0), EFWD_R, y_right)
        arrived(half_rows(m_right, 1), ENC_L + 1)
        send(half_rows(m_right, 1), half_rows(m_right, 1), EFWD_L, y_left)

    def encoded_complete():
        arrived(half_rows(m_left, 1), ENC_R + 1)
        arrived(half_rows(m_right, 0), ENC_L)
        arrived(half_rows(m_far, 0), EFWD_R)
        arrived(half_rows(m_far, 1), EFWD_L)
        gain_load.wait()
        for d in (1, 2, 3):
            arrived(gain.at[(mp + 4 - d) % 4], GAIN + d)
        qw_load.wait()

    def heads(part):
        def normalize(i, carry):
            rows = pl.ds(pl.multiple_of(part * 128 + i * 32, 32), 32)
            values = [enc[m, rows, :].astype(F32) for m in range(4)]
            total = jnp.sum(values[0] + values[1] + values[2] + values[3], axis=1, keepdims=True)
            square = jnp.sum(sum(v * v for v in values), axis=1, keepdims=True)
            mean = total / (4 * O)
            scale = lax.rsqrt(square / (4 * O) - mean * mean + 1e-05)
            for m in range(4):
                norm[rows, m * O : (m + 1) * O] = ((values[m] - mean) * scale * gain[m]).astype(BF16)
            return carry

        lax.fori_loop(0, 4, normalize, 0)
        rows = pl.ds(part * 128, 128)
        qout[rows, :] = jnp.dot(norm[rows, :], qw[...], preferred_element_type=F32).astype(BF16)

    top, bottom, own = pl.ds(0, XB // 2), pl.ds(XB // 2, XB // 2), pl.ds(0, COLS[0])
    xf, xr, xl = (x + 2) % 4, (x + 1) % 4, (x + 3) % 4
    gf, gr, gl = (zl + 2) % 4, (zl + 1) % 4, (zl + 3) % 4

    lower, upper = (z + 6) % 8 // 4, (z + 2) % 8 // 4

    def z_chain(step, part, base, received, staged):
        for sign, ids, peer in ((1, (ZUA, ZUB), z_up), (-1, (ZDA, ZDB), z_down)):
            z_hop(sign, step, part, base, received, staged, ids[part] + step - 1, peer)

    def z_hop(sign, step, part, base, received, staged, i, peer):
        src = base(sign, step, part)
        if step > 1 + part:
            arrived(received(sign, step - 1, part), i - 1)
            dst = staged(sign, step, part)
            add_to(dst, src, received(sign, step - 1, part))
            src = dst
        send(src, received(sign, step, part), i, peer)

    def z_last(received):
        for sign, ids in ((1, (ZUA, ZUB)), (-1, (ZDA, ZDB))):
            for part in (0, 1):
                arrived(received(sign, 4, part), ids[part] + 3)

    shared = len(sent)

    @pl.when(core == 0)
    def _():
        theirs(1, 0, gf)
        ours(0, 0, xf, 0)
        send(gown.at[xf, top, own], x1l, X1R, x_right)
        ours(0, 4, xf, 1)
        send(gown.at[xf, bottom, own], x1r, X1L, x_left)
        theirs(1, 1, gr)
        ours(0, 1, xr, 1)
        send(gown.at[xr, bottom, own], x2l.at[bottom], X2R + 1, x_right)
        ours(0, 1, xr, 0, waits=False)
        theirs(1, 2, gl)
        forward_encoded()
        theirs(1, 3, zl)
        ours(0, 2, xl)
        send(gown.at[xl, top, own], x2r.at[top], X2L, x_left)
        arrived(x1l, X1R)
        add(gown.at[xr, top, own], x1l)
        send(gown.at[xr, top, own], x2l.at[top], X2R, x_right)
        arrived(x1r, X1L)
        add(gown.at[xl, bottom, own], x1r)
        send(gown.at[xl, bottom, own], x2r.at[bottom], X2L + 1, x_left)
        ours(0, 3, x)
        encoded_complete()
        for part in range(4):
            heads(part)
        for half, rows in ((0, top), (1, bottom)):
            arrived(x2l.at[rows], X2R + half)
            arrived(x2r.at[rows], X2L + half)
        for g in range(4):
            rows = pl.ds(g * ZB, ZB)
            add3(zb.at[g], gown.at[x, rows, own], x2l.at[rows], x2r.at[rows])

        spans = (pl.ds(0, 512), pl.ds(512, 384))

        def cols(sign, part):
            return spans[part if sign == 1 else 1 - part]

        def way(sign):
            return 0 if sign == 1 else 1

        def base(sign, step, part):
            return zb.at[(zl + 5 - step if sign == 1 else zl + 3 + step) % 4, :, cols(sign, part)]

        def received(sign, step, part):
            return zr.at[way(sign), step - 1, :, cols(sign, part)]

        def staged(sign, step, part):
            return zs.at[way(sign), step - 2, :, cols(sign, part)]

        z_chain(1, 0, base, received, staged)
        z_chain(2, 1, base, received, staged)
        z_chain(2, 0, base, received, staged)
        z_chain(3, 1, base, received, staged)
        z_chain(3, 0, base, received, staged)
        z_chain(4, 1, base, received, staged)
        z_chain(4, 0, base, received, staged)
        z_last(received)
        add3(fin0, zb.at[zl], zr.at[0, 3], zr.at[1, 3])
        send(fin0, fin0, DSW, partner)
        arrived(fin1.at[lower], DSW)
        arrived(fin1.at[upper], DSW + 1)
        for copy in sent:
            copy.wait_send()

    @pl.when(core == 1)
    def _():
        del sent[shared:]
        theirs(0, 0, xf, 0)
        theirs(0, 4, xf, 1)
        theirs(0, 1, xr)
        ours(1, 0, gf)

        def piece(zo):
            return gown.at[(zo + 2) % 4, :, pl.ds(pl.multiple_of(zo // 4 * PIECE, 128), PIECE)]

        def half(ref, sign, part):
            return ref.at[top if (part == 0) == (sign == 1) else bottom]

        def base(sign, step, part):
            return half(piece((z + 5 - step if sign == 1 else z + 3 + step) % 8), sign, part)

        def received(sign, step, part):
            return half(zr1.at[0 if sign == 1 else 1, step - 1], sign, part)

        def hop(sign, step, part):
            i, peer = ((ZUA, ZUB)[part], z_up) if sign == 1 else ((ZDA, ZDB)[part], z_down)
            z_hop(sign, step, part, base, received, base, i + step - 1, peer)

        z_chain(1, 0, base, received, base)
        theirs(0, 2, xl)
        ours(1, 1, gr)
        hop(1, 2, 1)
        hop(1, 2, 0)
        ours(1, 2, gl)
        hop(-1, 2, 1)
        hop(-1, 2, 0)
        theirs(0, 3, x)
        ours(1, 3, zl)
        z_chain(3, 1, base, received, base)
        z_chain(3, 0, base, received, base)
        forward_encoded()
        z_chain(4, 1, base, received, base)
        z_chain(4, 0, base, received, base)
        encoded_complete()
        heads(0)
        z_last(received)
        add3(zs1, piece(z), zr1.at[0, 3], zr1.at[1, 3])

        def rows_at(xb, first, rows):
            return zs1.at[pl.ds(pl.multiple_of(xb * ZB + first, 16), rows)]

        send(rows_at(xf, 0, 48), u1l, X1R, x_right)
        send(rows_at(xf, 48, 32), u1r, X1L, x_left)
        heads(1)
        arrived(u1l, X1R)
        add(rows_at(xr, 0, 48), u1l)
        send(rows_at(xr, 0, ZB), u2l, X2R, x_right)
        arrived(u1r, X1L)
        add(rows_at(xl, 48, 32), u1r)
        send(rows_at(xl, 0, ZB), u2r, X2L, x_left)
        heads(2)
        arrived(u2l, X2R)
        arrived(u2r, X2L)
        mine = rows_at(x, 0, ZB)
        add3(mine, mine, u2l, u2r)
        send(mine, fin1.at[zh], DUP, z_up2)
        send(mine, fin1.at[zh], DDN, z_down2)
        heads(3)
        arrived(fin1.at[lower], DUP)
        send(fin1.at[lower], fin1.at[lower], DSW, partner)
        arrived(fin1.at[upper], DDN)
        send(fin1.at[upper], fin1.at[upper], DSW + 1, partner)
        arrived(fin0, DSW)
        for copy in sent:
            copy.wait_send()

    for i in range(N // 128):
        if i < 7:
            src = fin0.at[:, pl.ds(i * 128, 128)]
        else:
            src = fin1.at[(i - 7) // 4, :, pl.ds((i - 7) % 4 * 128, 128)]
        cgo[i // OT, :, pl.ds((i % OT) * 128, 128)] = src[...].astype(F32)


def finish(qkv_in, grad_in, qkv_out, grad_out, sem):
    copies = [
        pltpu.make_async_copy(grad_in, grad_out, sem.at[0]),
        pltpu.make_async_copy(qkv_in, qkv_out, sem.at[1]),
    ]
    for copy in copies:
        copy.start()
    for copy in copies:
        copy.wait()


def on_device(block_input, conv_weight, norm_gain, qkv_weight, encoder_grad):
    xin, eg = block_input[0], encoder_grad[0]
    any_ = pl.BlockSpec(memory_space=pl.ANY)
    v = pltpu.VMEM
    qkv, grad = pl.pallas_call(
        kernel,
        name="block",
        out_shape=(jax.ShapeDtypeStruct((R, Q), BF16), jax.ShapeDtypeStruct((KW, ZB, O), F32)),
        in_specs=[pl.BlockSpec(memory_space=pltpu.HBM)] * 5,
        out_specs=(pl.BlockSpec(memory_space=pltpu.VMEM),) * 2,
        scratch_shapes=[
            v((C, T), BF16), v((2, O, 128), BF16), v((2, 16, O), BF16), v((4, 32, O), BF16), v((2, 16, O), BF16),
            v((C, N), BF16), v((4, O), F32), v((4 * O, Q), BF16), v((R, O), BF16),
            v((TC, C), BF16), v((N // 128, T + 16, 128), F32), v((OT, T + 16, 128), F32), v((T, N), BF16),
            v((4, R, O), BF16), v((R, 4 * O), BF16),
            v((4, XB, COLS[1]), BF16), v((4, XB, COLS[1]), BF16), v((4, XB, COLS[1]), BF16),
            v((XB // 2, COLS[0]), BF16), v((XB // 2, COLS[0]), BF16), v((XB, COLS[0]), BF16), v((XB, COLS[0]), BF16),
            v((4, ZB, COLS[0]), BF16), v((2, 4, ZB, COLS[0]), BF16), v((2, 3, ZB, COLS[0]), BF16),
            v((2, 4, XB, PIECE), BF16), v((XB, PIECE), BF16),
            v((48, PIECE), BF16), v((32, PIECE), BF16), v((ZB, PIECE), BF16), v((ZB, PIECE), BF16),
            v((ZB, COLS[0]), BF16), v((2, ZB, PIECE), BF16),
            pltpu.SemaphoreType.DMA((16,)), pltpu.SemaphoreType.DMA((COPIES,)), pltpu.SemaphoreType.DMA((COPIES,)),
        ],
        compiler_params=pltpu.CompilerParams(collective_id=0, has_side_effects=True, vmem_limit_bytes=50 * 2**20),
    )(*(pltpu.with_memory_space_constraint(a, pltpu.HBM) for a in (xin.T, conv_weight, norm_gain, qkv_weight, eg)))
    qkv, grad = pl.pallas_call(
        finish,
        name="finish",
        out_shape=(jax.ShapeDtypeStruct((R, Q), BF16), jax.ShapeDtypeStruct((KW, ZB, O), F32)),
        in_specs=[any_] * 2,
        out_specs=(any_, any_),
        scratch_shapes=[pltpu.SemaphoreType.DMA((2,))],
        compiler_params=pltpu.CompilerParams(vmem_limit_bytes=4 * 2**20),
    )(qkv, grad)
    return qkv[None], grad.transpose(1, 0, 2)


def solution(mesh):
    return jax.shard_map(
        on_device,
        mesh=mesh,
        in_specs=(
            P("dp", "seq", "mp"),
            P(None, None, "mp"),
            P("mp"),
            P(None, "mp"),
            P("dp", "seq", "mp"),
        ),
        out_specs=(P("dp", "seq", "mp"), P("seq", None, "mp")),
        check_vma=False,
    )
```

```python
import jax
import jax.numpy as jnp
from jax import lax
from jax.experimental import pallas as pl
from jax.experimental.pallas import tpu as pltpu
from jax.sharding import PartitionSpec as P

MESH = pl.DeviceIdType.MESH
BF16, F32 = jnp.bfloat16, jnp.float32
KW = 5
T = 1024
R = 512
CB = 320
O = 384
OT = O // 128
C = 4 * CB
N = KW * O
Q = 640
TB = 128
TC = 256
XB = 320
ZB = 80
COLS = (7 * 128, 8 * 128)
PIECE = 4 * 128
Y0 = 8

OWN_R, OWN_L, FWD_R, FWD_L = 0, 8, 16, 24
EDGE_UP, EDGE_DOWN, GRAD_UP, GRAD_DOWN, RIM, GAIN = 32, 33, 34, 35, 35, 38
ENC_R, ENC_L, EFWD_R, EFWD_L = 42, 44, 46, 47
SWAP = 48
SPLIT = (0, 4)
X1R, X1L, X2R, X2L = 53, 54, 55, 57
ZUA, ZUB, ZDA, ZDB = 59, 63, 67, 71
DUP, DDN, DSW = 75, 76, 77
COPIES = 79


def kernel(
    xt_hbm, w_hbm, gain_hbm, qw_hbm, eg_hbm, qout, cgo,
    xt, ends, edge, rim, egrim, wcat, gain, qw, eg, xrow, yb, pgb, pgcat, enc, norm,
    psend, precv, gown, x1l, x1r, x2l, x2r, zb, zr, zs, zr1, zs1, u1l, u1r, u2l, u2r, fin0, fin1,
    lsem, ssem, rsem,
):
    seq, mp, dp = lax.axis_index("seq"), lax.axis_index("mp"), lax.axis_index("dp")
    x, zl = seq // 4, seq % 4
    zh, core = dp // 2, dp % 2
    z = zh * 4 + zl

    def at(s=None, m=None, d=None):
        return {"seq": seq if s is None else s, "mp": mp if m is None else m, "dp": dp if d is None else d}

    def z_at(zn):
        return at(s=x * 4 + zn % 4, d=(zn // 4) * 2 + core)

    y_right, y_left = at(m=(mp + 1) % 4), at(m=(mp + 3) % 4)
    s_up, s_down = at(s=(seq + 1) % 16), at(s=(seq + 15) % 16)
    x_right, x_left = at(s=(seq + 4) % 16), at(s=(seq + 12) % 16)
    z_up, z_down = z_at((z + 1) % 8), z_at((z + 7) % 8)
    partner = at(d=zh * 2 + 1 - core)
    z_up2, z_down2 = z_at((z + 2) % 8), z_at((z + 6) % 8)

    local = []

    def load(src, dst):
        copy = pltpu.make_async_copy(src, dst, lsem.at[len(local)])
        copy.start()
        local.append(copy)
        return copy

    own_rows = pl.ds(pl.multiple_of(mp * CB, CB), CB)
    end_loads = [load(xt_hbm.at[:, pl.ds(e * (T - 128), 128)], ends.at[e, pl.ds(0, CB)]) for e in (0, 1)]
    own_x = load(xt_hbm, xt.at[own_rows])
    loads = [load(w_hbm.at[k], wcat.at[:, pl.ds(k * O, O)]) for k in range(KW)]
    eg_load = load(eg_hbm, eg)
    gain_load = load(gain_hbm, gain.at[mp])
    qw_load = load(qw_hbm, qw)

    barrier = pltpu.get_barrier_semaphore()
    peers = [y_right, y_left, at(m=(mp + 2) % 4), s_up, s_down, x_right, x_left, z_up, z_down, z_up2, z_down2, partner]
    for peer in peers:
        pl.semaphore_signal(barrier, inc=1, device_id=peer, device_id_type=MESH)
    pl.semaphore_wait(barrier, len(peers))

    sent = []

    def remote(src, dst, i, peer):
        return pltpu.make_async_remote_copy(
            src_ref=src, dst_ref=dst, send_sem=ssem.at[i], recv_sem=rsem.at[i], device_id=peer, device_id_type=MESH
        )

    def send(src, dst, i, peer):
        copy = remote(src, dst, i, peer)
        copy.start()
        sent.append(copy)

    def arrived(dst, i):
        remote(dst, dst, i, y_right).wait_recv()

    def block(owner, half, tb):
        first = owner * CB + (0 if half is None else half * (CB // 2))
        size = CB if half is None else CB // 2
        return xt.at[pl.ds(pl.multiple_of(first, CB // 2), size), pl.ds(tb * TB, TB)]

    m_left, m_right, m_far = (mp + 3) % 4, (mp + 1) % 4, (mp + 2) % 4

    def send_own(tb):
        src = xt_hbm.at[:, pl.ds(tb * TB, TB)]
        send(src, block(mp, None, tb), OWN_R + tb, y_right)
        send(src, block(mp, None, tb), OWN_L + tb, y_left)

    def forward(tb):
        arrived(block(m_left, None, tb), OWN_R + tb)
        send(block(m_left, 0, tb), block(m_left, 0, tb), FWD_R + tb, y_right)
        arrived(block(m_right, None, tb), OWN_L + tb)
        send(block(m_right, 1, tb), block(m_right, 1, tb), FWD_L + tb, y_left)

    def complete(tb):
        arrived(block(m_far, 0, tb), FWD_R + tb)
        arrived(block(m_far, 1, tb), FWD_L + tb)

    send_own(0)
    send_own(1)
    for d in (1, 2, 3):
        send(gain_hbm, gain.at[mp], GAIN + d, at(m=(mp + d) % 4))
    send(eg_hbm.at[pl.ds(R - 16, 16)], egrim.at[0], GRAD_UP, s_up)
    send(eg_hbm.at[pl.ds(0, 16)], egrim.at[1], GRAD_DOWN, s_down)
    for copy in end_loads:
        copy.wait()
    for e in (0, 1):
        ends[e, CB:, :] = jnp.zeros((O - CB, 128), BF16)
        edge[e] = ends[e].T[112 * e : 112 * e + 16, :]
    send(edge.at[1], rim.at[mp, pl.ds(0, 16)], EDGE_UP, s_up)
    send(edge.at[0], rim.at[mp, pl.ds(16, 16)], EDGE_DOWN, s_down)
    send_own(2)
    own_x.wait()

    def tap_products(g, half):
        if half == 0:
            xrow[...] = xt[:, g * TC : (g + 1) * TC].T

        def tile(n, carry):
            cols = pl.ds(pl.multiple_of(n * 256, 256), 256)
            y = jnp.dot(xrow[...], wcat[:, cols], preferred_element_type=F32)
            yb[2 * n, pl.ds(Y0 + g * TC, TC), :] = y[:, :128]
            yb[2 * n + 1, pl.ds(Y0 + g * TC, TC), :] = y[:, 128:]
            return carry

        if half == 0:
            lax.fori_loop(0, 4, tile, 0)
        else:
            lax.fori_loop(4, N // 256, tile, 0)
            y = jnp.dot(xrow[...], wcat[:, N - 128 :], preferred_element_type=F32)
            yb[N // 128 - 1, pl.ds(Y0 + g * TC, TC), :] = y

    def rim_products():
        for d in (1, 2, 3):
            owner = (mp + 4 - d) % 4
            arrived(rim.at[owner], RIM + d)
        before = jnp.where(seq > 0, 1.0, 0.0).astype(F32)
        after = jnp.where(seq < 15, 1.0, 0.0).astype(F32)

        def tile(n, carry):
            cols = pl.ds(pl.multiple_of(n * 128, 128), 128)
            y = jnp.zeros((32, 128), F32)
            for m in range(4):
                y += jnp.dot(rim[m][:, :CB], wcat[m * CB : (m + 1) * CB, cols], preferred_element_type=F32)
            yb[n, pl.ds(0, 8), :] = y[8:16] * before
            yb[n, pl.ds(Y0 + T, 8), :] = y[16:24] * after
            return carry

        lax.fori_loop(0, N // 128, tile, 0)

    def gelu(v):
        v2 = v * v
        th = jnp.tanh(v * (0.7978845608 + (0.7978845608 * 0.044715) * v2))
        half = 0.5 + 0.5 * th
        slope = half + 0.5 * v * (1.0 - th * th) * (0.7978845608 + (0.7978845608 * 0.134145) * v2)
        return v * half, slope

    def pre(o, row, rows, stride):
        taps = [yb[k * OT + o, pl.ds(row + k - 2, rows, stride=stride), :] for k in range(KW)]
        return taps[0] + taps[1] + taps[2] + taps[3] + taps[4]

    STEP = 32

    def activations(first, count):
        def rows_of(i, carry):
            j = pl.multiple_of(first + i * STEP, STEP)
            for o in range(OT):
                lanes = pl.ds(o * 128, 128)
                act_e, slope_e = gelu(pre(o, Y0 + 2 * j, STEP, 2))
                act_o, slope_o = gelu(pre(o, Y0 + 2 * j + 1, STEP, 2))
                g = 0.5 * eg[pl.ds(j, STEP), lanes].astype(F32)
                enc[mp, pl.ds(j, STEP), lanes] = (0.5 * (act_e + act_o)).astype(BF16)
                pgb[o, pl.ds(Y0 + 2 * j, STEP, stride=2), :] = slope_e * g
                pgb[o, pl.ds(Y0 + 2 * j + 1, STEP, stride=2), :] = slope_o * g
            return carry

        lax.fori_loop(0, count // STEP, rows_of, 0)

    def rim_gradients(side):
        before = jnp.where(seq > 0, 0.5, 0.0).astype(F32)
        after = jnp.where(seq < 15, 0.5, 0.0).astype(F32)
        last, first = egrim[0, 8:16, :].astype(F32), egrim[1, 0:8, :].astype(F32)
        for o in range(OT):
            lanes = slice(o * 128, (o + 1) * 128)
            row, g = ((Y0 - 2, last[7:8, lanes] * before), (Y0 + T, first[0:1, lanes] * after))[side]
            for r in (row, row + 1):
                slope = gelu(pre(o, r, 1, 1))[1]
                pgb[o, pl.ds(r, 1), :] = slope * g

    PSTEP = 64

    def gradient_columns(first, count):
        def rows_of(i, carry):
            s = pl.multiple_of(first + i * PSTEP, PSTEP)
            for k in range(KW):
                for o in range(OT):
                    pgcat[pl.ds(s, PSTEP), (k * OT + o) * 128 : (k * OT + o + 1) * 128] = pgb[
                        o, pl.ds(Y0 + s + 2 - k, PSTEP), :
                    ].astype(BF16)
            return carry

        lax.fori_loop(0, count // PSTEP, rows_of, 0)

    def serve(i):
        forward(i)
        if i + 3 < T // TB:
            send_own(i + 3)

    def group(g):
        complete(2 * g)
        complete(2 * g + 1)

    serve(0)
    arrived(rim.at[mp, pl.ds(0, 16)], EDGE_UP)
    arrived(rim.at[mp, pl.ds(16, 16)], EDGE_DOWN)
    for d in (1, 2, 3):
        send(rim.at[mp], rim.at[mp], RIM + d, at(m=(mp + d) % 4))
    serve(1)
    for copy in loads:
        copy.wait()
    serve(2)
    group(0)
    tap_products(0, 0)
    serve(3)
    tap_products(0, 1)
    rim_products()
    serve(4)
    group(1)
    tap_products(1, 0)
    serve(5)
    tap_products(1, 1)
    eg_load.wait()
    activations(0, 224)
    arrived(egrim.at[0], GRAD_UP)
    arrived(egrim.at[1], GRAD_DOWN)
    rim_gradients(0)
    serve(6)
    gradient_columns(0, 384)
    group(2)
    tap_products(2, 0)
    serve(7)
    tap_products(2, 1)
    activations(224, 128)
    gradient_columns(384, 256)
    group(3)
    tap_products(3, 0)
    tap_products(3, 1)
    activations(352, 160)
    rim_gradients(1)

    def half_rows(owner, e):
        return enc.at[owner, pl.ds(e * (R // 2), R // 2)]

    send(half_rows(mp, 0), half_rows(mp, 0), ENC_R, y_right)
    send(half_rows(mp, 1), half_rows(mp, 1), ENC_L + 1, y_left)
    send(half_rows(mp, 1), half_rows(mp, 1), ENC_R + 1, y_right)
    send(half_rows(mp, 0), half_rows(mp, 0), ENC_L, y_left)
    gradient_columns(640, 384)

    def rows_of_z(g):
        return jnp.concatenate(
            [xt[pl.ds(pl.multiple_of(xb * XB + g * ZB, ZB), ZB), :] for xb in range(4)], axis=0
        )

    def products(left, owner, write):
        first, width = owner * COLS[0], COLS[owner]

        def tile(n, carry):
            lane = pl.multiple_of(n * 256, 256)
            write(lane, 256, jnp.dot(left, pgcat[:, pl.ds(first + lane, 256)], preferred_element_type=F32))
            return carry

        lax.fori_loop(0, width // 256, tile, 0)
        if width % 256:
            lane = width // 256 * 256
            write(lane, 128, jnp.dot(left, pgcat[:, pl.ds(first + lane, 128)], preferred_element_type=F32))

    def left_rows(kind, b, half):
        if kind:
            return rows_of_z(b)
        first, rows = (0, XB) if half is None else (half * (XB // 2), XB // 2)
        return xt[pl.ds(pl.multiple_of(b * XB + first, XB // 2), rows), :]

    def span(half):
        return pl.ds(0, XB) if half is None else pl.ds(half * (XB // 2), XB // 2)

    def theirs(other, step, b, half=None):
        rows = span(half)

        def write(lane, width, value):
            psend[b, rows, pl.ds(lane, width)] = value.astype(BF16)

        products(left_rows(other, b, half), other, write)
        cols = pl.ds(0, COLS[other])
        send(psend.at[b, rows, cols], precv.at[b, rows, cols], SWAP + step, partner)

    def ours(me, step, b, half=None, waits=True):
        rows = span(half)
        if waits:
            arrived(precv.at[b, span(half if me == 0 and step in SPLIT else None), pl.ds(0, COLS[me])], SWAP + step)

        def write(lane, width, value):
            cols = pl.ds(lane, width)
            gown[b, rows, cols] = (value + precv[b, rows, cols].astype(F32)).astype(BF16)

        products(left_rows(me, b, half), me, write)

    def add(dst, src):
        for r in range(0, dst.shape[0], 16):
            rows = pl.ds(r, 16)
            dst[rows, :] = (dst[rows, :].astype(F32) + src[rows, :].astype(F32)).astype(BF16)

    def add_to(dst, a, b):
        for r in range(0, dst.shape[0], 16):
            rows = pl.ds(r, 16)
            dst[rows, :] = (a[rows, :].astype(F32) + b[rows, :].astype(F32)).astype(BF16)

    def add3(dst, a, b, c):
        for r in range(0, dst.shape[0], 16):
            rows = pl.ds(r, 16)
            dst[rows, :] = (a[rows, :].astype(F32) + b[rows, :].astype(F32) + c[rows, :].astype(F32)).astype(BF16)

    def forward_encoded():
        arrived(half_rows(m_left, 0), ENC_R)
        send(half_rows(m_left, 0), half_rows(m_left, 0), EFWD_R, y_right)
        arrived(half_rows(m_right, 1), ENC_L + 1)
        send(half_rows(m_right, 1), half_rows(m_right, 1), EFWD_L, y_left)

    def encoded_complete():
        arrived(half_rows(m_left, 1), ENC_R + 1)
        arrived(half_rows(m_right, 0), ENC_L)
        arrived(half_rows(m_far, 0), EFWD_R)
        arrived(half_rows(m_far, 1), EFWD_L)
        gain_load.wait()
        for d in (1, 2, 3):
            arrived(gain.at[(mp + 4 - d) % 4], GAIN + d)
        qw_load.wait()

    def heads(part):
        def normalize(i, carry):
            rows = pl.ds(pl.multiple_of(part * 128 + i * 32, 32), 32)
            values = [enc[m, rows, :].astype(F32) for m in range(4)]
            total = jnp.sum(values[0] + values[1] + values[2] + values[3], axis=1, keepdims=True)
            square = jnp.sum(sum(v * v for v in values), axis=1, keepdims=True)
            mean = total / (4 * O)
            scale = lax.rsqrt(square / (4 * O) - mean * mean + 1e-05)
            for m in range(4):
                norm[rows, m * O : (m + 1) * O] = ((values[m] - mean) * scale * gain[m]).astype(BF16)
            return carry

        lax.fori_loop(0, 4, normalize, 0)
        rows = pl.ds(part * 128, 128)
        qout[rows, :] = jnp.dot(norm[rows, :], qw[...], preferred_element_type=F32).astype(BF16)

    top, bottom, own = pl.ds(0, XB // 2), pl.ds(XB // 2, XB // 2), pl.ds(0, COLS[0])
    xf, xr, xl = (x + 2) % 4, (x + 1) % 4, (x + 3) % 4
    gf, gr, gl = (zl + 2) % 4, (zl + 1) % 4, (zl + 3) % 4

    lower, upper = (z + 6) % 8 // 4, (z + 2) % 8 // 4

    def z_chain(step, part, base, received, staged):
        for sign, ids, peer in ((1, (ZUA, ZUB), z_up), (-1, (ZDA, ZDB), z_down)):
            z_hop(sign, step, part, base, received, staged, ids[part] + step - 1, peer)

    def z_hop(sign, step, part, base, received, staged, i, peer):
        src = base(sign, step, part)
        if step > 1 + part:
            arrived(received(sign, step - 1, part), i - 1)
            dst = staged(sign, step, part)
            add_to(dst, src, received(sign, step - 1, part))
            src = dst
        send(src, received(sign, step, part), i, peer)

    def z_last(received):
        for sign, ids in ((1, (ZUA, ZUB)), (-1, (ZDA, ZDB))):
            for part in (0, 1):
                arrived(received(sign, 4, part), ids[part] + 3)

    shared = len(sent)

    @pl.when(core == 0)
    def _():
        theirs(1, 0, gf)
        ours(0, 0, xf, 0)
        send(gown.at[xf, top, own], x1l, X1R, x_right)
        ours(0, 4, xf, 1)
        send(gown.at[xf, bottom, own], x1r, X1L, x_left)
        theirs(1, 1, gr)
        ours(0, 1, xr, 1)
        send(gown.at[xr, bottom, own], x2l.at[bottom], X2R + 1, x_right)
        ours(0, 1, xr, 0, waits=False)
        theirs(1, 2, gl)
        forward_encoded()
        theirs(1, 3, zl)
        arrived(x1l, X1R)
        add(gown.at[xr, top, own], x1l)
        send(gown.at[xr, top, own], x2l.at[top], X2R, x_right)
        ours(0, 2, xl)
        send(gown.at[xl, top, own], x2r.at[top], X2L, x_left)
        arrived(x1r, X1L)
        add(gown.at[xl, bottom, own], x1r)
        send(gown.at[xl, bottom, own], x2r.at[bottom], X2L + 1, x_left)
        ours(0, 3, x)
        encoded_complete()
        for part in range(4):
            heads(part)
        for half, rows in ((0, top), (1, bottom)):
            arrived(x2l.at[rows], X2R + half)
            arrived(x2r.at[rows], X2L + half)
        for g in range(4):
            rows = pl.ds(g * ZB, ZB)
            add3(zb.at[g], gown.at[x, rows, own], x2l.at[rows], x2r.at[rows])

        spans = (pl.ds(0, 512), pl.ds(512, 384))

        def cols(sign, part):
            return spans[part if sign == 1 else 1 - part]

        def way(sign):
            return 0 if sign == 1 else 1

        def base(sign, step, part):
            return zb.at[(zl + 5 - step if sign == 1 else zl + 3 + step) % 4, :, cols(sign, part)]

        def received(sign, step, part):
            return zr.at[way(sign), step - 1, :, cols(sign, part)]

        def staged(sign, step, part):
            return zs.at[way(sign), step - 2, :, cols(sign, part)]

        z_chain(1, 0, base, received, staged)
        z_chain(2, 1, base, received, staged)
        z_chain(2, 0, base, received, staged)
        z_chain(3, 1, base, received, staged)
        z_chain(3, 0, base, received, staged)
        z_chain(4, 1, base, received, staged)
        z_chain(4, 0, base, received, staged)
        z_last(received)
        add3(fin0, zb.at[zl], zr.at[0, 3], zr.at[1, 3])
        send(fin0, fin0, DSW, partner)
        arrived(fin1.at[lower], DSW)
        arrived(fin1.at[upper], DSW + 1)
        for copy in sent:
            copy.wait_send()

    @pl.when(core == 1)
    def _():
        del sent[shared:]
        theirs(0, 0, xf, 0)
        theirs(0, 4, xf, 1)
        theirs(0, 1, xr)
        ours(1, 0, gf)

        def piece(zo):
            return gown.at[(zo + 2) % 4, :, pl.ds(pl.multiple_of(zo // 4 * PIECE, 128), PIECE)]

        def half(ref, sign, part):
            return ref.at[top if (part == 0) == (sign == 1) else bottom]

        def base(sign, step, part):
            return half(piece((z + 5 - step if sign == 1 else z + 3 + step) % 8), sign, part)

        def received(sign, step, part):
            return half(zr1.at[0 if sign == 1 else 1, step - 1], sign, part)

        def hop(sign, step, part):
            i, peer = ((ZUA, ZUB)[part], z_up) if sign == 1 else ((ZDA, ZDB)[part], z_down)
            z_hop(sign, step, part, base, received, base, i + step - 1, peer)

        z_chain(1, 0, base, received, base)
        theirs(0, 2, xl)
        ours(1, 1, gr)
        hop(1, 2, 1)
        hop(1, 2, 0)
        theirs(0, 3, x)
        ours(1, 2, gl)
        hop(-1, 2, 1)
        hop(-1, 2, 0)
        ours(1, 3, zl)
        z_chain(3, 1, base, received, base)
        z_chain(3, 0, base, received, base)
        forward_encoded()
        z_chain(4, 1, base, received, base)
        z_chain(4, 0, base, received, base)
        encoded_complete()
        heads(0)
        z_last(received)
        add3(zs1, piece(z), zr1.at[0, 3], zr1.at[1, 3])

        def rows_at(xb, first, rows):
            return zs1.at[pl.ds(pl.multiple_of(xb * ZB + first, 16), rows)]

        send(rows_at(xf, 0, 48), u1l, X1R, x_right)
        send(rows_at(xf, 48, 32), u1r, X1L, x_left)
        heads(1)
        arrived(u1l, X1R)
        add(rows_at(xr, 0, 48), u1l)
        send(rows_at(xr, 0, ZB), u2l, X2R, x_right)
        arrived(u1r, X1L)
        add(rows_at(xl, 48, 32), u1r)
        send(rows_at(xl, 0, ZB), u2r, X2L, x_left)
        heads(2)
        arrived(u2l, X2R)
        arrived(u2r, X2L)
        mine = rows_at(x, 0, ZB)
        add3(mine, mine, u2l, u2r)
        send(mine, fin1.at[zh], DUP, z_up2)
        send(mine, fin1.at[zh], DDN, z_down2)
        heads(3)
        arrived(fin1.at[lower], DUP)
        send(fin1.at[lower], fin1.at[lower], DSW, partner)
        arrived(fin1.at[upper], DDN)
        send(fin1.at[upper], fin1.at[upper], DSW + 1, partner)
        arrived(fin0, DSW)
        for copy in sent:
            copy.wait_send()

    for i in range(N // 128):
        if i < 7:
            src = fin0.at[:, pl.ds(i * 128, 128)]
        else:
            src = fin1.at[(i - 7) // 4, :, pl.ds((i - 7) % 4 * 128, 128)]
        cgo[i // OT, :, pl.ds((i % OT) * 128, 128)] = src[...].astype(F32)


def finish(qkv_in, grad_in, qkv_out, grad_out, sem):
    copies = [
        pltpu.make_async_copy(grad_in, grad_out, sem.at[0]),
        pltpu.make_async_copy(qkv_in, qkv_out, sem.at[1]),
    ]
    for copy in copies:
        copy.start()
    for copy in copies:
        copy.wait()


def on_device(block_input, conv_weight, norm_gain, qkv_weight, encoder_grad):
    xin, eg = block_input[0], encoder_grad[0]
    any_ = pl.BlockSpec(memory_space=pl.ANY)
    v = pltpu.VMEM
    qkv, grad = pl.pallas_call(
        kernel,
        name="block",
        out_shape=(jax.ShapeDtypeStruct((R, Q), BF16), jax.ShapeDtypeStruct((KW, ZB, O), F32)),
        in_specs=[pl.BlockSpec(memory_space=pltpu.HBM)] * 5,
        out_specs=(pl.BlockSpec(memory_space=pltpu.VMEM),) * 2,
        scratch_shapes=[
            v((C, T), BF16), v((2, O, 128), BF16), v((2, 16, O), BF16), v((4, 32, O), BF16), v((2, 16, O), BF16),
            v((C, N), BF16), v((4, O), F32), v((4 * O, Q), BF16), v((R, O), BF16),
            v((TC, C), BF16), v((N // 128, T + 16, 128), F32), v((OT, T + 16, 128), F32), v((T, N), BF16),
            v((4, R, O), BF16), v((R, 4 * O), BF16),
            v((4, XB, COLS[1]), BF16), v((4, XB, COLS[1]), BF16), v((4, XB, COLS[1]), BF16),
            v((XB // 2, COLS[0]), BF16), v((XB // 2, COLS[0]), BF16), v((XB, COLS[0]), BF16), v((XB, COLS[0]), BF16),
            v((4, ZB, COLS[0]), BF16), v((2, 4, ZB, COLS[0]), BF16), v((2, 3, ZB, COLS[0]), BF16),
            v((2, 4, XB, PIECE), BF16), v((XB, PIECE), BF16),
            v((48, PIECE), BF16), v((32, PIECE), BF16), v((ZB, PIECE), BF16), v((ZB, PIECE), BF16),
            v((ZB, COLS[0]), BF16), v((2, ZB, PIECE), BF16),
            pltpu.SemaphoreType.DMA((16,)), pltpu.SemaphoreType.DMA((COPIES,)), pltpu.SemaphoreType.DMA((COPIES,)),
        ],
        compiler_params=pltpu.CompilerParams(collective_id=0, has_side_effects=True, vmem_limit_bytes=50 * 2**20),
    )(*(pltpu.with_memory_space_constraint(a, pltpu.HBM) for a in (xin.T, conv_weight, norm_gain, qkv_weight, eg)))
    qkv, grad = pl.pallas_call(
        finish,
        name="finish",
        out_shape=(jax.ShapeDtypeStruct((R, Q), BF16), jax.ShapeDtypeStruct((KW, ZB, O), F32)),
        in_specs=[any_] * 2,
        out_specs=(any_, any_),
        scratch_shapes=[pltpu.SemaphoreType.DMA((2,))],
        compiler_params=pltpu.CompilerParams(vmem_limit_bytes=4 * 2**20),
    )(qkv, grad)
    return qkv[None], grad.transpose(1, 0, 2)


def solution(mesh):
    return jax.shard_map(
        on_device,
        mesh=mesh,
        in_specs=(
            P("dp", "seq", "mp"),
            P(None, None, "mp"),
            P("mp"),
            P(None, "mp"),
            P("dp", "seq", "mp"),
        ),
        out_specs=(P("dp", "seq", "mp"), P("seq", None, "mp")),
        check_vma=False,
    )
```

```python
import jax
import jax.numpy as jnp
from jax import lax
from jax.experimental import pallas as pl
from jax.experimental.pallas import tpu as pltpu
from jax.sharding import PartitionSpec as P

MESH = pl.DeviceIdType.MESH
BF16, F32 = jnp.bfloat16, jnp.float32
KW = 5
T = 1024
R = 512
CB = 320
O = 384
OT = O // 128
C = 4 * CB
N = KW * O
Q = 640
TB = 128
TC = 256
XB = 320
ZB = 80
COLS = (7 * 128, 8 * 128)
PIECE = 4 * 128
REST = C - CB
Y0 = 8

OWN_R, OWN_L, FWD_R, FWD_L = 0, 8, 16, 24
EDGE_UP, EDGE_DOWN, GRAD_UP, GRAD_DOWN, RIM, GAIN = 32, 33, 34, 35, 35, 38
ENC_R, ENC_L, EFWD_R, EFWD_L = 42, 44, 46, 47
SWAP = 48
SPLIT = (0, 4)
X1R, X1L, X2R, X2L = 53, 54, 55, 57
ZUA, ZUB, ZDA, ZDB = 59, 63, 67, 71
DUP, DDN, DSW = 75, 76, 77
COPIES = 79


def kernel(
    xt_hbm, w_hbm, gain_hbm, qw_hbm, eg_hbm, qout, cgo,
    xt, xown, ends, edge, rim, egrim, wcat, gain, qw, eg, xrow, yb, pgb, pgcat, enc, norm,
    psend, precv, gown, x1l, x1r, x2l, x2r, zb, zr, zs, zr1, zs1, u1l, u1r, u2l, u2r, fin0, fin1,
    lsem, ssem, rsem,
):
    seq, mp, dp = lax.axis_index("seq"), lax.axis_index("mp"), lax.axis_index("dp")
    x, zl = seq // 4, seq % 4
    zh, core = dp // 2, dp % 2
    z = zh * 4 + zl

    def at(s=None, m=None, d=None):
        return {"seq": seq if s is None else s, "mp": mp if m is None else m, "dp": dp if d is None else d}

    def z_at(zn):
        return at(s=x * 4 + zn % 4, d=(zn // 4) * 2 + core)

    y_right, y_left = at(m=(mp + 1) % 4), at(m=(mp + 3) % 4)
    s_up, s_down = at(s=(seq + 1) % 16), at(s=(seq + 15) % 16)
    x_right, x_left = at(s=(seq + 4) % 16), at(s=(seq + 12) % 16)
    z_up, z_down = z_at((z + 1) % 8), z_at((z + 7) % 8)
    partner = at(d=zh * 2 + 1 - core)
    z_up2, z_down2 = z_at((z + 2) % 8), z_at((z + 6) % 8)

    local = []

    def load(src, dst):
        copy = pltpu.make_async_copy(src, dst, lsem.at[len(local)])
        copy.start()
        local.append(copy)
        return copy

    own_rows = pl.ds(REST, CB)
    end_loads = [load(xt_hbm.at[:, pl.ds(e * (T - 128), 128)], ends.at[e, pl.ds(0, CB)]) for e in (0, 1)]
    own_x = load(xt_hbm, xt.at[own_rows])
    own_again = load(xt_hbm, xown.at[pl.ds(0, CB)])
    loads = [
        load(
            w_hbm.at[k, pl.ds(pl.multiple_of((mp + slot + 1) % 4 * CB, CB), CB)],
            wcat.at[pl.ds(slot * CB, CB), pl.ds(k * O, O)],
        )
        for slot in (3, 0, 1, 2)
        for k in range(KW)
    ]
    eg_load = load(eg_hbm, eg)
    gain_load = load(gain_hbm, gain.at[mp])
    qw_load = load(qw_hbm, qw)

    barrier = pltpu.get_barrier_semaphore()
    peers = [y_right, y_left, at(m=(mp + 2) % 4), s_up, s_down, x_right, x_left, z_up, z_down, z_up2, z_down2, partner]
    for peer in peers:
        pl.semaphore_signal(barrier, inc=1, device_id=peer, device_id_type=MESH)
    pl.semaphore_wait(barrier, len(peers))

    sent = []

    def remote(src, dst, i, peer):
        return pltpu.make_async_remote_copy(
            src_ref=src, dst_ref=dst, send_sem=ssem.at[i], recv_sem=rsem.at[i], device_id=peer, device_id_type=MESH
        )

    def send(src, dst, i, peer):
        copy = remote(src, dst, i, peer)
        copy.start()
        sent.append(copy)

    def arrived(dst, i):
        remote(dst, dst, i, y_right).wait_recv()

    def block(slot, half, tb):
        first = slot * CB + (0 if half is None else half * (CB // 2))
        size = CB if half is None else CB // 2
        return xt.at[pl.ds(first, size), pl.ds(tb * TB, TB)]

    m_left, m_right, m_far = (mp + 3) % 4, (mp + 1) % 4, (mp + 2) % 4
    RIGHT, FAR, LEFT = 0, 1, 2

    def send_own(tb):
        src = xt_hbm.at[:, pl.ds(tb * TB, TB)]
        send(src, block(LEFT, None, tb), OWN_R + tb, y_right)
        send(src, block(RIGHT, None, tb), OWN_L + tb, y_left)

    def forward(tb):
        arrived(block(LEFT, None, tb), OWN_R + tb)
        send(block(LEFT, 0, tb), block(FAR, 0, tb), FWD_R + tb, y_right)
        arrived(block(RIGHT, None, tb), OWN_L + tb)
        send(block(RIGHT, 1, tb), block(FAR, 1, tb), FWD_L + tb, y_left)

    def complete(tb):
        arrived(block(FAR, 0, tb), FWD_R + tb)
        arrived(block(FAR, 1, tb), FWD_L + tb)

    send_own(0)
    send_own(1)
    for d in (1, 2, 3):
        send(gain_hbm, gain.at[mp], GAIN + d, at(m=(mp + d) % 4))
    send(eg_hbm.at[pl.ds(R - 16, 16)], egrim.at[0], GRAD_UP, s_up)
    send(eg_hbm.at[pl.ds(0, 16)], egrim.at[1], GRAD_DOWN, s_down)
    for copy in end_loads:
        copy.wait()
    for e in (0, 1):
        ends[e, CB:, :] = jnp.zeros((O - CB, 128), BF16)
        edge[e] = ends[e].T[112 * e : 112 * e + 16, :]
    send(edge.at[1], rim.at[mp, pl.ds(0, 16)], EDGE_UP, s_up)
    send(edge.at[0], rim.at[mp, pl.ds(16, 16)], EDGE_DOWN, s_down)
    send_own(2)
    own_x.wait()
    own_again.wait()
    xown[CB:, :] = jnp.zeros((O - CB, T), BF16)

    def own_products(g):
        xrow[:, :O] = xown[:, g * TC : (g + 1) * TC].T

        def tile(n, carry):
            cols = pl.ds(pl.multiple_of(n * 256, 256), 256)
            y = jnp.dot(xrow[:, :CB], wcat[REST:, cols], preferred_element_type=F32)
            yb[2 * n, pl.ds(Y0 + g * TC, TC), :] = y[:, :128]
            yb[2 * n + 1, pl.ds(Y0 + g * TC, TC), :] = y[:, 128:]
            return carry

        lax.fori_loop(0, N // 256, tile, 0)
        y = jnp.dot(xrow[:, :CB], wcat[REST:, N - 128 :], preferred_element_type=F32)
        yb[N // 128 - 1, pl.ds(Y0 + g * TC, TC), :] = y

    def tap_products(g, half):
        if half == 0:
            xrow[...] = xt[:1024, g * TC : (g + 1) * TC].T

        def tile(n, carry):
            cols = pl.ds(pl.multiple_of(n * 256, 256), 256)
            y = jnp.dot(xrow[:, :REST], wcat[:REST, cols], preferred_element_type=F32)
            yb[2 * n, pl.ds(Y0 + g * TC, TC), :] += y[:, :128]
            yb[2 * n + 1, pl.ds(Y0 + g * TC, TC), :] += y[:, 128:]
            return carry

        if half == 0:
            lax.fori_loop(0, 4, tile, 0)
        else:
            lax.fori_loop(4, N // 256, tile, 0)
            y = jnp.dot(xrow[:, :REST], wcat[:REST, N - 128 :], preferred_element_type=F32)
            yb[N // 128 - 1, pl.ds(Y0 + g * TC, TC), :] += y

    def rim_products():
        for d in (1, 2, 3):
            owner = (mp + 4 - d) % 4
            arrived(rim.at[owner], RIM + d)
        before = jnp.where(seq > 0, 1.0, 0.0).astype(F32)
        after = jnp.where(seq < 15, 1.0, 0.0).astype(F32)

        def rims(cols, width):
            y = jnp.zeros((32, width), F32)
            for slot in range(4):
                left = rim[(mp + slot + 1) % 4][:, :CB]
                y += jnp.dot(left, wcat[slot * CB : (slot + 1) * CB, cols], preferred_element_type=F32)
            return y[8:16] * before, y[16:24] * after

        def tile(n, carry):
            first, last = rims(pl.ds(pl.multiple_of(n * 256, 256), 256), 256)
            for i in range(2):
                yb[2 * n + i, pl.ds(0, 8), :] = first[:, i * 128 : (i + 1) * 128]
                yb[2 * n + i, pl.ds(Y0 + T, 8), :] = last[:, i * 128 : (i + 1) * 128]
            return carry

        lax.fori_loop(0, N // 256, tile, 0)
        first, last = rims(pl.ds(N - 128, 128), 128)
        yb[N // 128 - 1, pl.ds(0, 8), :] = first
        yb[N // 128 - 1, pl.ds(Y0 + T, 8), :] = last

    def gelu(v):
        v2 = v * v
        th = jnp.tanh(v * (0.7978845608 + (0.7978845608 * 0.044715) * v2))
        half = 0.5 + 0.5 * th
        slope = half + 0.5 * v * (1.0 - th * th) * (0.7978845608 + (0.7978845608 * 0.134145) * v2)
        return v * half, slope

    def pre(o, row, rows, stride):
        taps = [yb[k * OT + o, pl.ds(row + k - 2, rows, stride=stride), :] for k in range(KW)]
        return taps[0] + taps[1] + taps[2] + taps[3] + taps[4]

    STEP = 32

    def activations(first, count):
        def rows_of(i, carry):
            j = pl.multiple_of(first + i * STEP, STEP)
            for o in range(OT):
                lanes = pl.ds(o * 128, 128)
                act_e, slope_e = gelu(pre(o, Y0 + 2 * j, STEP, 2))
                act_o, slope_o = gelu(pre(o, Y0 + 2 * j + 1, STEP, 2))
                g = 0.5 * eg[pl.ds(j, STEP), lanes].astype(F32)
                enc[mp, pl.ds(j, STEP), lanes] = (0.5 * (act_e + act_o)).astype(BF16)
                pgb[o, pl.ds(Y0 + 2 * j, STEP, stride=2), :] = slope_e * g
                pgb[o, pl.ds(Y0 + 2 * j + 1, STEP, stride=2), :] = slope_o * g
            return carry

        lax.fori_loop(0, count // STEP, rows_of, 0)

    def rim_gradients(side):
        before = jnp.where(seq > 0, 0.5, 0.0).astype(F32)
        after = jnp.where(seq < 15, 0.5, 0.0).astype(F32)
        last, first = egrim[0, 8:16, :].astype(F32), egrim[1, 0:8, :].astype(F32)
        for o in range(OT):
            lanes = slice(o * 128, (o + 1) * 128)
            row, g = ((Y0 - 2, last[7:8, lanes] * before), (Y0 + T, first[0:1, lanes] * after))[side]
            for r in (row, row + 1):
                slope = gelu(pre(o, r, 1, 1))[1]
                pgb[o, pl.ds(r, 1), :] = slope * g

    PSTEP = 64

    def gradient_columns(first, count):
        def rows_of(i, carry):
            s = pl.multiple_of(first + i * PSTEP, PSTEP)
            for k in range(KW):
                for o in range(OT):
                    pgcat[pl.ds(s, PSTEP), (k * OT + o) * 128 : (k * OT + o + 1) * 128] = pgb[
                        o, pl.ds(Y0 + s + 2 - k, PSTEP), :
                    ].astype(BF16)
            return carry

        lax.fori_loop(0, count // PSTEP, rows_of, 0)

    def serve(i):
        forward(i)
        if i + 3 < T // TB:
            send_own(i + 3)

    def group(g):
        complete(2 * g)
        complete(2 * g + 1)

    serve(0)
    arrived(rim.at[mp, pl.ds(0, 16)], EDGE_UP)
    arrived(rim.at[mp, pl.ds(16, 16)], EDGE_DOWN)
    for d in (1, 2, 3):
        send(rim.at[mp], rim.at[mp], RIM + d, at(m=(mp + d) % 4))
    for copy in loads[:KW]:
        copy.wait()
    own_products(0)
    serve(1)
    own_products(1)
    serve(2)
    own_products(2)
    for copy in loads[KW:]:
        copy.wait()
    group(0)
    tap_products(0, 0)
    serve(3)
    tap_products(0, 1)
    own_products(3)
    serve(4)
    rim_products()
    group(1)
    tap_products(1, 0)
    serve(5)
    tap_products(1, 1)
    eg_load.wait()
    activations(0, 224)
    arrived(egrim.at[0], GRAD_UP)
    arrived(egrim.at[1], GRAD_DOWN)
    rim_gradients(0)
    serve(6)
    gradient_columns(0, 384)
    group(2)
    tap_products(2, 0)
    serve(7)
    tap_products(2, 1)
    activations(224, 128)
    gradient_columns(384, 256)
    group(3)
    tap_products(3, 0)
    tap_products(3, 1)
    activations(352, 160)
    rim_gradients(1)

    def half_rows(owner, e):
        return enc.at[owner, pl.ds(e * (R // 2), R // 2)]

    send(half_rows(mp, 0), half_rows(mp, 0), ENC_R, y_right)
    send(half_rows(mp, 1), half_rows(mp, 1), ENC_L + 1, y_left)
    send(half_rows(mp, 1), half_rows(mp, 1), ENC_R + 1, y_right)
    send(half_rows(mp, 0), half_rows(mp, 0), ENC_L, y_left)
    gradient_columns(640, 384)

    def rows_of_z(g):
        return jnp.concatenate(
            [xt[pl.ds(pl.multiple_of((xb - mp + 7) % 4 * XB + g * ZB, ZB), ZB), :] for xb in range(4)], axis=0
        )

    def products(left, owner, write):
        first, width = owner * COLS[0], COLS[owner]

        def tile(n, carry):
            lane = pl.multiple_of(n * 256, 256)
            write(lane, 256, jnp.dot(left, pgcat[:, pl.ds(first + lane, 256)], preferred_element_type=F32))
            return carry

        lax.fori_loop(0, width // 256, tile, 0)
        if width % 256:
            lane = width // 256 * 256
            write(lane, 128, jnp.dot(left, pgcat[:, pl.ds(first + lane, 128)], preferred_element_type=F32))

    def left_rows(kind, b, half):
        if kind:
            return rows_of_z(b)
        first, rows = (0, XB) if half is None else (half * (XB // 2), XB // 2)
        return xt[pl.ds(pl.multiple_of((b - mp + 7) % 4 * XB + first, XB // 2), rows), :]

    def span(half):
        return pl.ds(0, XB) if half is None else pl.ds(half * (XB // 2), XB // 2)

    def theirs(other, step, b, half=None):
        rows = span(half)

        def write(lane, width, value):
            psend[b, rows, pl.ds(lane, width)] = value.astype(BF16)

        products(left_rows(other, b, half), other, write)
        cols = pl.ds(0, COLS[other])
        send(psend.at[b, rows, cols], precv.at[b, rows, cols], SWAP + step, partner)

    def ours(me, step, b, half=None, waits=True):
        rows = span(half)
        if waits:
            arrived(precv.at[b, span(half if me == 0 and step in SPLIT else None), pl.ds(0, COLS[me])], SWAP + step)

        def write(lane, width, value):
            cols = pl.ds(lane, width)
            gown[b, rows, cols] = (value + precv[b, rows, cols].astype(F32)).astype(BF16)

        products(left_rows(me, b, half), me, write)

    def add(dst, src):
        for r in range(0, dst.shape[0], 16):
            rows = pl.ds(r, 16)
            dst[rows, :] = (dst[rows, :].astype(F32) + src[rows, :].astype(F32)).astype(BF16)

    def add_to(dst, a, b):
        for r in range(0, dst.shape[0], 16):
            rows = pl.ds(r, 16)
            dst[rows, :] = (a[rows, :].astype(F32) + b[rows, :].astype(F32)).astype(BF16)

    def add3(dst, a, b, c):
        for r in range(0, dst.shape[0], 16):
            rows = pl.ds(r, 16)
            dst[rows, :] = (a[rows, :].astype(F32) + b[rows, :].astype(F32) + c[rows, :].astype(F32)).astype(BF16)

    def forward_encoded():
        arrived(half_rows(m_left, 0), ENC_R)
        send(half_rows(m_left, 0), half_rows(m_left, 0), EFWD_R, y_right)
        arrived(half_rows(m_right, 1), ENC_L + 1)
        send(half_rows(m_right, 1), half_rows(m_right, 1), EFWD_L, y_left)

    def encoded_complete():
        arrived(half_rows(m_left, 1), ENC_R + 1)
        arrived(half_rows(m_right, 0), ENC_L)
        arrived(half_rows(m_far, 0), EFWD_R)
        arrived(half_rows(m_far, 1), EFWD_L)
        gain_load.wait()
        for d in (1, 2, 3):
            arrived(gain.at[(mp + 4 - d) % 4], GAIN + d)
        qw_load.wait()

    def heads(part):
        def normalize(i, carry):
            rows = pl.ds(pl.multiple_of(part * 128 + i * 32, 32), 32)
            values = [enc[m, rows, :].astype(F32) for m in range(4)]
            total = jnp.sum(values[0] + values[1] + values[2] + values[3], axis=1, keepdims=True)
            square = jnp.sum(sum(v * v for v in values), axis=1, keepdims=True)
            mean = total / (4 * O)
            scale = lax.rsqrt(square / (4 * O) - mean * mean + 1e-05)
            for m in range(4):
                norm[rows, m * O : (m + 1) * O] = ((values[m] - mean) * scale * gain[m]).astype(BF16)
            return carry

        lax.fori_loop(0, 4, normalize, 0)
        rows = pl.ds(part * 128, 128)
        qout[rows, :] = jnp.dot(norm[rows, :], qw[...], preferred_element_type=F32).astype(BF16)

    top, bottom, own = pl.ds(0, XB // 2), pl.ds(XB // 2, XB // 2), pl.ds(0, COLS[0])
    xf, xr, xl = (x + 2) % 4, (x + 1) % 4, (x + 3) % 4
    gf, gr, gl = (zl + 2) % 4, (zl + 1) % 4, (zl + 3) % 4

    lower, upper = (z + 6) % 8 // 4, (z + 2) % 8 // 4

    def z_chain(step, part, base, received, staged):
        for sign, ids, peer in ((1, (ZUA, ZUB), z_up), (-1, (ZDA, ZDB), z_down)):
            z_hop(sign, step, part, base, received, staged, ids[part] + step - 1, peer)

    def z_hop(sign, step, part, base, received, staged, i, peer):
        src = base(sign, step, part)
        if step > 1 + part:
            arrived(received(sign, step - 1, part), i - 1)
            dst = staged(sign, step, part)
            add_to(dst, src, received(sign, step - 1, part))
            src = dst
        send(src, received(sign, step, part), i, peer)

    def z_last(received):
        for sign, ids in ((1, (ZUA, ZUB)), (-1, (ZDA, ZDB))):
            for part in (0, 1):
                arrived(received(sign, 4, part), ids[part] + 3)

    shared = len(sent)

    @pl.when(core == 0)
    def _():
        theirs(1, 0, gf)
        ours(0, 0, xf, 0)
        send(gown.at[xf, top, own], x1l, X1R, x_right)
        ours(0, 4, xf, 1)
        send(gown.at[xf, bottom, own], x1r, X1L, x_left)
        theirs(1, 1, gr)
        ours(0, 1, xr, 1)
        send(gown.at[xr, bottom, own], x2l.at[bottom], X2R + 1, x_right)
        ours(0, 1, xr, 0, waits=False)
        theirs(1, 2, gl)
        forward_encoded()
        theirs(1, 3, zl)
        arrived(x1l, X1R)
        add(gown.at[xr, top, own], x1l)
        send(gown.at[xr, top, own], x2l.at[top], X2R, x_right)
        ours(0, 2, xl)
        send(gown.at[xl, top, own], x2r.at[top], X2L, x_left)
        arrived(x1r, X1L)
        add(gown.at[xl, bottom, own], x1r)
        send(gown.at[xl, bottom, own], x2r.at[bottom], X2L + 1, x_left)
        ours(0, 3, x)
        encoded_complete()
        for part in range(4):
            heads(part)
        for half, rows in ((0, top), (1, bottom)):
            arrived(x2l.at[rows], X2R + half)
            arrived(x2r.at[rows], X2L + half)
        for g in range(4):
            rows = pl.ds(g * ZB, ZB)
            add3(zb.at[g], gown.at[x, rows, own], x2l.at[rows], x2r.at[rows])

        spans = (pl.ds(0, 512), pl.ds(512, 384))

        def cols(sign, part):
            return spans[part if sign == 1 else 1 - part]

        def way(sign):
            return 0 if sign == 1 else 1

        def base(sign, step, part):
            return zb.at[(zl + 5 - step if sign == 1 else zl + 3 + step) % 4, :, cols(sign, part)]

        def received(sign, step, part):
            return zr.at[way(sign), step - 1, :, cols(sign, part)]

        def staged(sign, step, part):
            return zs.at[way(sign), step - 2, :, cols(sign, part)]

        z_chain(1, 0, base, received, staged)
        z_chain(2, 1, base, received, staged)
        z_chain(2, 0, base, received, staged)
        z_chain(3, 1, base, received, staged)
        z_chain(3, 0, base, received, staged)
        z_chain(4, 1, base, received, staged)
        z_chain(4, 0, base, received, staged)
        z_last(received)
        add3(fin0, zb.at[zl], zr.at[0, 3], zr.at[1, 3])
        send(fin0, fin0, DSW, partner)
        arrived(fin1.at[lower], DSW)
        arrived(fin1.at[upper], DSW + 1)
        for copy in sent:
            copy.wait_send()

    @pl.when(core == 1)
    def _():
        del sent[shared:]
        theirs(0, 0, xf, 0)
        theirs(0, 4, xf, 1)
        theirs(0, 1, xr)
        ours(1, 0, gf)

        def piece(zo):
            return gown.at[(zo + 2) % 4, :, pl.ds(pl.multiple_of(zo // 4 * PIECE, 128), PIECE)]

        def half(ref, sign, part):
            return ref.at[top if (part == 0) == (sign == 1) else bottom]

        def base(sign, step, part):
            return half(piece((z + 5 - step if sign == 1 else z + 3 + step) % 8), sign, part)

        def received(sign, step, part):
            return half(zr1.at[0 if sign == 1 else 1, step - 1], sign, part)

        def hop(sign, step, part):
            i, peer = ((ZUA, ZUB)[part], z_up) if sign == 1 else ((ZDA, ZDB)[part], z_down)
            z_hop(sign, step, part, base, received, base, i + step - 1, peer)

        z_chain(1, 0, base, received, base)
        theirs(0, 2, xl)
        ours(1, 1, gr)
        hop(1, 2, 1)
        hop(1, 2, 0)
        theirs(0, 3, x)
        ours(1, 2, gl)
        hop(-1, 2, 1)
        hop(-1, 2, 0)
        ours(1, 3, zl)
        z_chain(3, 1, base, received, base)
        z_chain(3, 0, base, received, base)
        forward_encoded()
        z_chain(4, 1, base, received, base)
        z_chain(4, 0, base, received, base)
        encoded_complete()
        heads(0)
        z_last(received)
        add3(zs1, piece(z), zr1.at[0, 3], zr1.at[1, 3])

        def rows_at(xb, first, rows):
            return zs1.at[pl.ds(pl.multiple_of(xb * ZB + first, 16), rows)]

        send(rows_at(xf, 0, 48), u1l, X1R, x_right)
        send(rows_at(xf, 48, 32), u1r, X1L, x_left)
        heads(1)
        arrived(u1l, X1R)
        add(rows_at(xr, 0, 48), u1l)
        send(rows_at(xr, 0, ZB), u2l, X2R, x_right)
        arrived(u1r, X1L)
        add(rows_at(xl, 48, 32), u1r)
        send(rows_at(xl, 0, ZB), u2r, X2L, x_left)
        heads(2)
        arrived(u2l, X2R)
        arrived(u2r, X2L)
        mine = rows_at(x, 0, ZB)
        add3(mine, mine, u2l, u2r)
        send(mine, fin1.at[zh], DUP, z_up2)
        send(mine, fin1.at[zh], DDN, z_down2)
        heads(3)
        arrived(fin1.at[lower], DUP)
        send(fin1.at[lower], fin1.at[lower], DSW, partner)
        arrived(fin1.at[upper], DDN)
        send(fin1.at[upper], fin1.at[upper], DSW + 1, partner)
        arrived(fin0, DSW)
        for copy in sent:
            copy.wait_send()

    for i in range(N // 128):
        if i < 7:
            src = fin0.at[:, pl.ds(i * 128, 128)]
        else:
            src = fin1.at[(i - 7) // 4, :, pl.ds((i - 7) % 4 * 128, 128)]
        cgo[i // OT, :, pl.ds((i % OT) * 128, 128)] = src[...].astype(F32)


def finish(qkv_in, grad_in, qkv_out, grad_out, sem):
    copies = [
        pltpu.make_async_copy(grad_in, grad_out, sem.at[0]),
        pltpu.make_async_copy(qkv_in, qkv_out, sem.at[1]),
    ]
    for copy in copies:
        copy.start()
    for copy in copies:
        copy.wait()


def on_device(block_input, conv_weight, norm_gain, qkv_weight, encoder_grad):
    xin, eg = block_input[0], encoder_grad[0]
    any_ = pl.BlockSpec(memory_space=pl.ANY)
    v = pltpu.VMEM
    qkv, grad = pl.pallas_call(
        kernel,
        name="block",
        out_shape=(jax.ShapeDtypeStruct((R, Q), BF16), jax.ShapeDtypeStruct((KW, ZB, O), F32)),
        in_specs=[pl.BlockSpec(memory_space=pltpu.HBM)] * 5,
        out_specs=(pl.BlockSpec(memory_space=pltpu.VMEM),) * 2,
        scratch_shapes=[
            v((C, T), BF16), v((O, T), BF16), v((2, O, 128), BF16), v((2, 16, O), BF16), v((4, 32, O), BF16), v((2, 16, O), BF16),
            v((C, N), BF16), v((4, O), F32), v((4 * O, Q), BF16), v((R, O), BF16),
            v((TC, 1024), BF16), v((N // 128, T + 16, 128), F32), v((OT, T + 16, 128), F32), v((T, N), BF16),
            v((4, R, O), BF16), v((R, 4 * O), BF16),
            v((4, XB, COLS[1]), BF16), v((4, XB, COLS[1]), BF16), v((4, XB, COLS[1]), BF16),
            v((XB // 2, COLS[0]), BF16), v((XB // 2, COLS[0]), BF16), v((XB, COLS[0]), BF16), v((XB, COLS[0]), BF16),
            v((4, ZB, COLS[0]), BF16), v((2, 4, ZB, COLS[0]), BF16), v((2, 3, ZB, COLS[0]), BF16),
            v((2, 4, XB, PIECE), BF16), v((XB, PIECE), BF16),
            v((48, PIECE), BF16), v((32, PIECE), BF16), v((ZB, PIECE), BF16), v((ZB, PIECE), BF16),
            v((ZB, COLS[0]), BF16), v((2, ZB, PIECE), BF16),
            pltpu.SemaphoreType.DMA((32,)), pltpu.SemaphoreType.DMA((COPIES,)), pltpu.SemaphoreType.DMA((COPIES,)),
        ],
        compiler_params=pltpu.CompilerParams(collective_id=0, has_side_effects=True, vmem_limit_bytes=50 * 2**20),
    )(*(pltpu.with_memory_space_constraint(a, pltpu.HBM) for a in (xin.T, conv_weight, norm_gain, qkv_weight, eg)))
    qkv, grad = pl.pallas_call(
        finish,
        name="finish",
        out_shape=(jax.ShapeDtypeStruct((R, Q), BF16), jax.ShapeDtypeStruct((KW, ZB, O), F32)),
        in_specs=[any_] * 2,
        out_specs=(any_, any_),
        scratch_shapes=[pltpu.SemaphoreType.DMA((2,))],
        compiler_params=pltpu.CompilerParams(vmem_limit_bytes=4 * 2**20),
    )(qkv, grad)
    return qkv[None], grad.transpose(1, 0, 2)


def solution(mesh):
    return jax.shard_map(
        on_device,
        mesh=mesh,
        in_specs=(
            P("dp", "seq", "mp"),
            P(None, None, "mp"),
            P("mp"),
            P(None, "mp"),
            P("dp", "seq", "mp"),
        ),
        out_specs=(P("dp", "seq", "mp"), P("seq", None, "mp")),
        check_vma=False,
    )
```

```python
import jax
import jax.numpy as jnp
from jax import lax
from jax.experimental import pallas as pl
from jax.experimental.pallas import tpu as pltpu
from jax.sharding import PartitionSpec as P

MESH = pl.DeviceIdType.MESH
BF16, F32 = jnp.bfloat16, jnp.float32
KW = 5
T = 1024
R = 512
CB = 320
O = 384
OT = O // 128
C = 4 * CB
N = KW * O
Q = 640
TB = 128
TC = 256
XB = 320
ZB = 80
COLS = (7 * 128, 8 * 128)
PIECE = 4 * 128
Y0 = 8

OWN_R, OWN_L, FWD_R, FWD_L = 0, 8, 16, 24
EDGE_UP, EDGE_DOWN, GRAD_UP, GRAD_DOWN, RIM, GAIN = 32, 33, 34, 35, 35, 38
ENC_R, ENC_L, EFWD_R, EFWD_L = 42, 44, 46, 47
SWAP = 48
SPLIT = (0, 4)
X1R, X1L, X2R, X2L = 53, 54, 55, 57
ZUA, ZUB, ZDA, ZDB = 59, 63, 67, 71
DUP, DDN, DSW = 75, 76, 77
COPIES = 79


def kernel(
    xt_hbm, w_hbm, gain_hbm, qw_hbm, eg_hbm, qout, cgo,
    xt, ends, edge, rim, egrim, wcat, gain, qw, eg, xrow, yb, pgb, pgcat, enc, norm,
    psend, precv, gown, x1l, x1r, x2l, x2r, zb, zr, zs, zr1, zs1, uf, u2l, u2r, fin0, fin1,
    lsem, ssem, rsem,
):
    seq, mp, dp = lax.axis_index("seq"), lax.axis_index("mp"), lax.axis_index("dp")
    x, zl = seq // 4, seq % 4
    zh, core = dp // 2, dp % 2
    z = zh * 4 + zl

    def at(s=None, m=None, d=None):
        return {"seq": seq if s is None else s, "mp": mp if m is None else m, "dp": dp if d is None else d}

    def z_at(zn):
        return at(s=x * 4 + zn % 4, d=(zn // 4) * 2 + core)

    y_right, y_left = at(m=(mp + 1) % 4), at(m=(mp + 3) % 4)
    s_up, s_down = at(s=(seq + 1) % 16), at(s=(seq + 15) % 16)
    x_right, x_left = at(s=(seq + 4) % 16), at(s=(seq + 12) % 16)
    x_far = at(s=(seq + 8) % 16)
    z_up, z_down = z_at((z + 1) % 8), z_at((z + 7) % 8)
    partner = at(d=zh * 2 + 1 - core)
    z_up2, z_down2 = z_at((z + 2) % 8), z_at((z + 6) % 8)

    local = []

    def load(src, dst):
        copy = pltpu.make_async_copy(src, dst, lsem.at[len(local)])
        copy.start()
        local.append(copy)
        return copy

    own_rows = pl.ds(pl.multiple_of(mp * CB, CB), CB)
    end_loads = [load(xt_hbm.at[:, pl.ds(e * (T - 128), 128)], ends.at[e, pl.ds(0, CB)]) for e in (0, 1)]
    own_x = load(xt_hbm, xt.at[own_rows])
    loads = [load(w_hbm.at[k], wcat.at[:, pl.ds(k * O, O)]) for k in range(KW)]
    eg_load = load(eg_hbm, eg)
    gain_load = load(gain_hbm, gain.at[mp])
    qw_load = load(qw_hbm, qw)

    barrier = pltpu.get_barrier_semaphore()
    peers = [y_right, y_left, at(m=(mp + 2) % 4), s_up, s_down, x_right, x_left, x_far, z_up, z_down, z_up2, z_down2, partner]
    for peer in peers:
        pl.semaphore_signal(barrier, inc=1, device_id=peer, device_id_type=MESH)
    pl.semaphore_wait(barrier, len(peers))

    sent = []

    def remote(src, dst, i, peer):
        return pltpu.make_async_remote_copy(
            src_ref=src, dst_ref=dst, send_sem=ssem.at[i], recv_sem=rsem.at[i], device_id=peer, device_id_type=MESH
        )

    def send(src, dst, i, peer):
        copy = remote(src, dst, i, peer)
        copy.start()
        sent.append(copy)

    def arrived(dst, i):
        remote(dst, dst, i, y_right).wait_recv()

    def block(owner, half, tb):
        first = owner * CB + (0 if half is None else half * (CB // 2))
        size = CB if half is None else CB // 2
        return xt.at[pl.ds(pl.multiple_of(first, CB // 2), size), pl.ds(tb * TB, TB)]

    m_left, m_right, m_far = (mp + 3) % 4, (mp + 1) % 4, (mp + 2) % 4

    def send_own(tb):
        src = xt_hbm.at[:, pl.ds(tb * TB, TB)]
        send(src, block(mp, None, tb), OWN_R + tb, y_right)
        send(src, block(mp, None, tb), OWN_L + tb, y_left)

    def forward(tb):
        arrived(block(m_left, None, tb), OWN_R + tb)
        send(block(m_left, 0, tb), block(m_left, 0, tb), FWD_R + tb, y_right)
        arrived(block(m_right, None, tb), OWN_L + tb)
        send(block(m_right, 1, tb), block(m_right, 1, tb), FWD_L + tb, y_left)

    def complete(tb):
        arrived(block(m_far, 0, tb), FWD_R + tb)
        arrived(block(m_far, 1, tb), FWD_L + tb)

    send_own(0)
    send_own(1)
    for d in (1, 2, 3):
        send(gain_hbm, gain.at[mp], GAIN + d, at(m=(mp + d) % 4))
    send(eg_hbm.at[pl.ds(R - 16, 16)], egrim.at[0], GRAD_UP, s_up)
    send(eg_hbm.at[pl.ds(0, 16)], egrim.at[1], GRAD_DOWN, s_down)
    for copy in end_loads:
        copy.wait()
    for e in (0, 1):
        ends[e, CB:, :] = jnp.zeros((O - CB, 128), BF16)
        edge[e] = ends[e].T[112 * e : 112 * e + 16, :]
    send(edge.at[1], rim.at[mp, pl.ds(0, 16)], EDGE_UP, s_up)
    send(edge.at[0], rim.at[mp, pl.ds(16, 16)], EDGE_DOWN, s_down)
    send_own(2)
    own_x.wait()

    def tap_products(g, half):
        if half == 0:
            xrow[...] = xt[:, g * TC : (g + 1) * TC].T

        def tile(n, carry):
            cols = pl.ds(pl.multiple_of(n * 256, 256), 256)
            y = jnp.dot(xrow[...], wcat[:, cols], preferred_element_type=F32)
            yb[2 * n, pl.ds(Y0 + g * TC, TC), :] = y[:, :128]
            yb[2 * n + 1, pl.ds(Y0 + g * TC, TC), :] = y[:, 128:]
            return carry

        if half == 0:
            lax.fori_loop(0, 4, tile, 0)
        else:
            lax.fori_loop(4, N // 256, tile, 0)
            y = jnp.dot(xrow[...], wcat[:, N - 128 :], preferred_element_type=F32)
            yb[N // 128 - 1, pl.ds(Y0 + g * TC, TC), :] = y

    def rim_products():
        for d in (1, 2, 3):
            owner = (mp + 4 - d) % 4
            arrived(rim.at[owner], RIM + d)
        before = jnp.where(seq > 0, 1.0, 0.0).astype(F32)
        after = jnp.where(seq < 15, 1.0, 0.0).astype(F32)

        def tile(n, carry):
            cols = pl.ds(pl.multiple_of(n * 128, 128), 128)
            y = jnp.zeros((32, 128), F32)
            for m in range(4):
                y += jnp.dot(rim[m][:, :CB], wcat[m * CB : (m + 1) * CB, cols], preferred_element_type=F32)
            yb[n, pl.ds(0, 8), :] = y[8:16] * before
            yb[n, pl.ds(Y0 + T, 8), :] = y[16:24] * after
            return carry

        lax.fori_loop(0, N // 128, tile, 0)

    def gelu(v):
        v2 = v * v
        th = jnp.tanh(v * (0.7978845608 + (0.7978845608 * 0.044715) * v2))
        half = 0.5 + 0.5 * th
        slope = half + 0.5 * v * (1.0 - th * th) * (0.7978845608 + (0.7978845608 * 0.134145) * v2)
        return v * half, slope

    def pre(o, row, rows, stride):
        taps = [yb[k * OT + o, pl.ds(row + k - 2, rows, stride=stride), :] for k in range(KW)]
        return taps[0] + taps[1] + taps[2] + taps[3] + taps[4]

    STEP = 32

    def activations(first, count):
        def rows_of(i, carry):
            j = pl.multiple_of(first + i * STEP, STEP)
            for o in range(OT):
                lanes = pl.ds(o * 128, 128)
                act_e, slope_e = gelu(pre(o, Y0 + 2 * j, STEP, 2))
                act_o, slope_o = gelu(pre(o, Y0 + 2 * j + 1, STEP, 2))
                g = 0.5 * eg[pl.ds(j, STEP), lanes].astype(F32)
                enc[mp, pl.ds(j, STEP), lanes] = (0.5 * (act_e + act_o)).astype(BF16)
                pgb[o, pl.ds(Y0 + 2 * j, STEP, stride=2), :] = slope_e * g
                pgb[o, pl.ds(Y0 + 2 * j + 1, STEP, stride=2), :] = slope_o * g
            return carry

        lax.fori_loop(0, count // STEP, rows_of, 0)

    def rim_gradients(side):
        before = jnp.where(seq > 0, 0.5, 0.0).astype(F32)
        after = jnp.where(seq < 15, 0.5, 0.0).astype(F32)
        last, first = egrim[0, 8:16, :].astype(F32), egrim[1, 0:8, :].astype(F32)
        for o in range(OT):
            lanes = slice(o * 128, (o + 1) * 128)
            row, g = ((Y0 - 2, last[7:8, lanes] * before), (Y0 + T, first[0:1, lanes] * after))[side]
            for r in (row, row + 1):
                slope = gelu(pre(o, r, 1, 1))[1]
                pgb[o, pl.ds(r, 1), :] = slope * g

    PSTEP = 64

    def gradient_columns(first, count):
        def rows_of(i, carry):
            s = pl.multiple_of(first + i * PSTEP, PSTEP)
            for k in range(KW):
                for o in range(OT):
                    pgcat[pl.ds(s, PSTEP), (k * OT + o) * 128 : (k * OT + o + 1) * 128] = pgb[
                        o, pl.ds(Y0 + s + 2 - k, PSTEP), :
                    ].astype(BF16)
            return carry

        lax.fori_loop(0, count // PSTEP, rows_of, 0)

    def serve(i):
        forward(i)
        if i + 3 < T // TB:
            send_own(i + 3)

    def group(g):
        complete(2 * g)
        complete(2 * g + 1)

    serve(0)
    arrived(rim.at[mp, pl.ds(0, 16)], EDGE_UP)
    arrived(rim.at[mp, pl.ds(16, 16)], EDGE_DOWN)
    for d in (1, 2, 3):
        send(rim.at[mp], rim.at[mp], RIM + d, at(m=(mp + d) % 4))
    serve(1)
    for copy in loads:
        copy.wait()
    serve(2)
    group(0)
    tap_products(0, 0)
    serve(3)
    tap_products(0, 1)
    rim_products()
    serve(4)
    group(1)
    tap_products(1, 0)
    serve(5)
    tap_products(1, 1)
    eg_load.wait()
    activations(0, 224)
    arrived(egrim.at[0], GRAD_UP)
    arrived(egrim.at[1], GRAD_DOWN)
    rim_gradients(0)
    serve(6)
    gradient_columns(0, 384)
    group(2)
    tap_products(2, 0)
    serve(7)
    tap_products(2, 1)
    activations(224, 128)
    gradient_columns(384, 256)
    group(3)
    tap_products(3, 0)
    tap_products(3, 1)
    activations(352, 160)
    rim_gradients(1)

    def half_rows(owner, e):
        return enc.at[owner, pl.ds(e * (R // 2), R // 2)]

    send(half_rows(mp, 0), half_rows(mp, 0), ENC_R, y_right)
    send(half_rows(mp, 1), half_rows(mp, 1), ENC_L + 1, y_left)
    send(half_rows(mp, 1), half_rows(mp, 1), ENC_R + 1, y_right)
    send(half_rows(mp, 0), half_rows(mp, 0), ENC_L, y_left)
    gradient_columns(640, 384)

    def rows_of_z(g):
        return jnp.concatenate(
            [xt[pl.ds(pl.multiple_of(xb * XB + g * ZB, ZB), ZB), :] for xb in range(4)], axis=0
        )

    def products(left, owner, write):
        first, width = owner * COLS[0], COLS[owner]

        def tile(n, carry):
            lane = pl.multiple_of(n * 256, 256)
            write(lane, 256, jnp.dot(left, pgcat[:, pl.ds(first + lane, 256)], preferred_element_type=F32))
            return carry

        lax.fori_loop(0, width // 256, tile, 0)
        if width % 256:
            lane = width // 256 * 256
            write(lane, 128, jnp.dot(left, pgcat[:, pl.ds(first + lane, 128)], preferred_element_type=F32))

    def left_rows(kind, b, half):
        if kind:
            return rows_of_z(b)
        first, rows = (0, XB) if half is None else (half * (XB // 2), XB // 2)
        return xt[pl.ds(pl.multiple_of(b * XB + first, XB // 2), rows), :]

    def span(half):
        return pl.ds(0, XB) if half is None else pl.ds(half * (XB // 2), XB // 2)

    def theirs(other, step, b, half=None):
        rows = span(half)

        def write(lane, width, value):
            psend[b, rows, pl.ds(lane, width)] = value.astype(BF16)

        products(left_rows(other, b, half), other, write)
        cols = pl.ds(0, COLS[other])
        send(psend.at[b, rows, cols], precv.at[b, rows, cols], SWAP + step, partner)

    def ours(me, step, b, half=None, waits=True):
        rows = span(half)
        if waits:
            arrived(precv.at[b, span(half if me == 0 and step in SPLIT else None), pl.ds(0, COLS[me])], SWAP + step)

        def write(lane, width, value):
            cols = pl.ds(lane, width)
            gown[b, rows, cols] = (value + precv[b, rows, cols].astype(F32)).astype(BF16)

        products(left_rows(me, b, half), me, write)

    def add(dst, src):
        for r in range(0, dst.shape[0], 16):
            rows = pl.ds(r, 16)
            dst[rows, :] = (dst[rows, :].astype(F32) + src[rows, :].astype(F32)).astype(BF16)

    def add_to(dst, a, b):
        for r in range(0, dst.shape[0], 16):
            rows = pl.ds(r, 16)
            dst[rows, :] = (a[rows, :].astype(F32) + b[rows, :].astype(F32)).astype(BF16)

    def add3(dst, a, b, c):
        for r in range(0, dst.shape[0], 16):
            rows = pl.ds(r, 16)
            dst[rows, :] = (a[rows, :].astype(F32) + b[rows, :].astype(F32) + c[rows, :].astype(F32)).astype(BF16)

    def forward_encoded():
        arrived(half_rows(m_left, 0), ENC_R)
        send(half_rows(m_left, 0), half_rows(m_left, 0), EFWD_R, y_right)
        arrived(half_rows(m_right, 1), ENC_L + 1)
        send(half_rows(m_right, 1), half_rows(m_right, 1), EFWD_L, y_left)

    def encoded_complete():
        arrived(half_rows(m_left, 1), ENC_R + 1)
        arrived(half_rows(m_right, 0), ENC_L)
        arrived(half_rows(m_far, 0), EFWD_R)
        arrived(half_rows(m_far, 1), EFWD_L)
        gain_load.wait()
        for d in (1, 2, 3):
            arrived(gain.at[(mp + 4 - d) % 4], GAIN + d)
        qw_load.wait()

    def heads(part):
        def normalize(i, carry):
            rows = pl.ds(pl.multiple_of(part * 128 + i * 32, 32), 32)
            values = [enc[m, rows, :].astype(F32) for m in range(4)]
            total = jnp.sum(values[0] + values[1] + values[2] + values[3], axis=1, keepdims=True)
            square = jnp.sum(sum(v * v for v in values), axis=1, keepdims=True)
            mean = total / (4 * O)
            scale = lax.rsqrt(square / (4 * O) - mean * mean + 1e-05)
            for m in range(4):
                norm[rows, m * O : (m + 1) * O] = ((values[m] - mean) * scale * gain[m]).astype(BF16)
            return carry

        lax.fori_loop(0, 4, normalize, 0)
        rows = pl.ds(part * 128, 128)
        qout[rows, :] = jnp.dot(norm[rows, :], qw[...], preferred_element_type=F32).astype(BF16)

    top, bottom, own = pl.ds(0, XB // 2), pl.ds(XB // 2, XB // 2), pl.ds(0, COLS[0])
    xf, xr, xl = (x + 2) % 4, (x + 1) % 4, (x + 3) % 4
    gf, gr, gl = (zl + 2) % 4, (zl + 1) % 4, (zl + 3) % 4

    lower, upper = (z + 6) % 8 // 4, (z + 2) % 8 // 4

    def z_chain(step, part, base, received, staged):
        for sign, ids, peer in ((1, (ZUA, ZUB), z_up), (-1, (ZDA, ZDB), z_down)):
            z_hop(sign, step, part, base, received, staged, ids[part] + step - 1, peer)

    def z_hop(sign, step, part, base, received, staged, i, peer):
        src = base(sign, step, part)
        if step > 1 + part:
            arrived(received(sign, step - 1, part), i - 1)
            dst = staged(sign, step, part)
            add_to(dst, src, received(sign, step - 1, part))
            src = dst
        send(src, received(sign, step, part), i, peer)

    def z_last(received):
        for sign, ids in ((1, (ZUA, ZUB)), (-1, (ZDA, ZDB))):
            for part in (0, 1):
                arrived(received(sign, 4, part), ids[part] + 3)

    shared = len(sent)

    @pl.when(core == 0)
    def _():
        theirs(1, 0, gf)
        ours(0, 0, xf, 0)
        send(gown.at[xf, top, own], x1l, X1R, x_right)
        ours(0, 4, xf, 1)
        send(gown.at[xf, bottom, own], x1r, X1L, x_left)
        theirs(1, 1, gr)
        ours(0, 1, xr, 1)
        send(gown.at[xr, bottom, own], x2l.at[bottom], X2R + 1, x_right)
        ours(0, 1, xr, 0, waits=False)
        theirs(1, 2, gl)
        forward_encoded()
        theirs(1, 3, zl)
        arrived(x1l, X1R)
        add(gown.at[xr, top, own], x1l)
        send(gown.at[xr, top, own], x2l.at[top], X2R, x_right)
        ours(0, 2, xl)
        send(gown.at[xl, top, own], x2r.at[top], X2L, x_left)
        arrived(x1r, X1L)
        add(gown.at[xl, bottom, own], x1r)
        send(gown.at[xl, bottom, own], x2r.at[bottom], X2L + 1, x_left)
        ours(0, 3, x)
        encoded_complete()
        for part in range(4):
            heads(part)
        for half, rows in ((0, top), (1, bottom)):
            arrived(x2l.at[rows], X2R + half)
            arrived(x2r.at[rows], X2L + half)
        for g in range(4):
            rows = pl.ds(g * ZB, ZB)
            add3(zb.at[g], gown.at[x, rows, own], x2l.at[rows], x2r.at[rows])

        spans = (pl.ds(0, 512), pl.ds(512, 384))

        def cols(sign, part):
            return spans[part if sign == 1 else 1 - part]

        def way(sign):
            return 0 if sign == 1 else 1

        def base(sign, step, part):
            return zb.at[(zl + 5 - step if sign == 1 else zl + 3 + step) % 4, :, cols(sign, part)]

        def received(sign, step, part):
            return zr.at[way(sign), step - 1, :, cols(sign, part)]

        def staged(sign, step, part):
            return zs.at[way(sign), step - 2, :, cols(sign, part)]

        z_chain(1, 0, base, received, staged)
        z_chain(2, 1, base, received, staged)
        z_chain(2, 0, base, received, staged)
        z_chain(3, 1, base, received, staged)
        z_chain(3, 0, base, received, staged)
        z_chain(4, 1, base, received, staged)
        z_chain(4, 0, base, received, staged)
        z_last(received)
        add3(fin0, zb.at[zl], zr.at[0, 3], zr.at[1, 3])
        send(fin0, fin0, DSW, partner)
        arrived(fin1.at[lower], DSW)
        arrived(fin1.at[upper], DSW + 1)
        for copy in sent:
            copy.wait_send()

    @pl.when(core == 1)
    def _():
        del sent[shared:]
        theirs(0, 0, xf, 0)
        theirs(0, 4, xf, 1)
        theirs(0, 1, xr)
        ours(1, 0, gf)

        def piece(zo):
            return gown.at[(zo + 2) % 4, :, pl.ds(pl.multiple_of(zo // 4 * PIECE, 128), PIECE)]

        def half(ref, sign, part):
            return ref.at[top if (part == 0) == (sign == 1) else bottom]

        def base(sign, step, part):
            return half(piece((z + 5 - step if sign == 1 else z + 3 + step) % 8), sign, part)

        def received(sign, step, part):
            return half(zr1.at[0 if sign == 1 else 1, step - 1], sign, part)

        def hop(sign, step, part):
            i, peer = ((ZUA, ZUB)[part], z_up) if sign == 1 else ((ZDA, ZDB)[part], z_down)
            z_hop(sign, step, part, base, received, base, i + step - 1, peer)

        z_chain(1, 0, base, received, base)
        theirs(0, 2, xl)
        ours(1, 1, gr)
        hop(1, 2, 1)
        hop(1, 2, 0)
        theirs(0, 3, x)
        ours(1, 2, gl)
        hop(-1, 2, 1)
        hop(-1, 2, 0)
        forward_encoded()
        ours(1, 3, zl)
        z_chain(3, 1, base, received, base)
        z_chain(3, 0, base, received, base)
        z_chain(4, 1, base, received, base)
        z_chain(4, 0, base, received, base)
        encoded_complete()
        heads(0)
        heads(1)
        z_last(received)
        add3(zs1, piece(z), zr1.at[0, 3], zr1.at[1, 3])

        def rows_at(xb):
            return zs1.at[pl.ds(pl.multiple_of(xb * ZB, ZB), ZB)]

        send(rows_at(xf), uf, X1R, x_far)
        send(rows_at(xr), u2l, X2R, x_right)
        send(rows_at(xl), u2r, X2L, x_left)
        heads(2)
        arrived(u2l, X2R)
        arrived(u2r, X2L)
        arrived(uf, X1R)
        mine = rows_at(x)
        for r in range(0, ZB, 16):
            rows = pl.ds(r, 16)
            parts = [ref[rows, :].astype(F32) for ref in (mine, u2l, u2r, uf)]
            mine[rows, :] = (parts[0] + parts[1] + parts[2] + parts[3]).astype(BF16)
        send(mine, fin1.at[zh], DUP, z_up2)
        send(mine, fin1.at[zh], DDN, z_down2)
        heads(3)
        arrived(fin1.at[lower], DUP)
        send(fin1.at[lower], fin1.at[lower], DSW, partner)
        arrived(fin1.at[upper], DDN)
        send(fin1.at[upper], fin1.at[upper], DSW + 1, partner)
        arrived(fin0, DSW)
        for copy in sent:
            copy.wait_send()

    for i in range(N // 128):
        if i < 7:
            src = fin0.at[:, pl.ds(i * 128, 128)]
        else:
            src = fin1.at[(i - 7) // 4, :, pl.ds((i - 7) % 4 * 128, 128)]
        cgo[i // OT, :, pl.ds((i % OT) * 128, 128)] = src[...].astype(F32)


def finish(qkv_in, grad_in, qkv_out, grad_out, sem):
    copies = [
        pltpu.make_async_copy(grad_in, grad_out, sem.at[0]),
        pltpu.make_async_copy(qkv_in, qkv_out, sem.at[1]),
    ]
    for copy in copies:
        copy.start()
    for copy in copies:
        copy.wait()


def on_device(block_input, conv_weight, norm_gain, qkv_weight, encoder_grad):
    xin, eg = block_input[0], encoder_grad[0]
    any_ = pl.BlockSpec(memory_space=pl.ANY)
    v = pltpu.VMEM
    qkv, grad = pl.pallas_call(
        kernel,
        name="block",
        out_shape=(jax.ShapeDtypeStruct((R, Q), BF16), jax.ShapeDtypeStruct((KW, ZB, O), F32)),
        in_specs=[pl.BlockSpec(memory_space=pltpu.HBM)] * 5,
        out_specs=(pl.BlockSpec(memory_space=pltpu.VMEM),) * 2,
        scratch_shapes=[
            v((C, T), BF16), v((2, O, 128), BF16), v((2, 16, O), BF16), v((4, 32, O), BF16), v((2, 16, O), BF16),
            v((C, N), BF16), v((4, O), F32), v((4 * O, Q), BF16), v((R, O), BF16),
            v((TC, C), BF16), v((N // 128, T + 16, 128), F32), v((OT, T + 16, 128), F32), v((T, N), BF16),
            v((4, R, O), BF16), v((R, 4 * O), BF16),
            v((4, XB, COLS[1]), BF16), v((4, XB, COLS[1]), BF16), v((4, XB, COLS[1]), BF16),
            v((XB // 2, COLS[0]), BF16), v((XB // 2, COLS[0]), BF16), v((XB, COLS[0]), BF16), v((XB, COLS[0]), BF16),
            v((4, ZB, COLS[0]), BF16), v((2, 4, ZB, COLS[0]), BF16), v((2, 3, ZB, COLS[0]), BF16),
            v((2, 4, XB, PIECE), BF16), v((XB, PIECE), BF16),
            v((ZB, PIECE), BF16), v((ZB, PIECE), BF16), v((ZB, PIECE), BF16),
            v((ZB, COLS[0]), BF16), v((2, ZB, PIECE), BF16),
            pltpu.SemaphoreType.DMA((16,)), pltpu.SemaphoreType.DMA((COPIES,)), pltpu.SemaphoreType.DMA((COPIES,)),
        ],
        compiler_params=pltpu.CompilerParams(collective_id=0, has_side_effects=True, vmem_limit_bytes=50 * 2**20),
    )(*(pltpu.with_memory_space_constraint(a, pltpu.HBM) for a in (xin.T, conv_weight, norm_gain, qkv_weight, eg)))
    qkv, grad = pl.pallas_call(
        finish,
        name="finish",
        out_shape=(jax.ShapeDtypeStruct((R, Q), BF16), jax.ShapeDtypeStruct((KW, ZB, O), F32)),
        in_specs=[any_] * 2,
        out_specs=(any_, any_),
        scratch_shapes=[pltpu.SemaphoreType.DMA((2,))],
        compiler_params=pltpu.CompilerParams(vmem_limit_bytes=4 * 2**20),
    )(qkv, grad)
    return qkv[None], grad.transpose(1, 0, 2)


def solution(mesh):
    return jax.shard_map(
        on_device,
        mesh=mesh,
        in_specs=(
            P("dp", "seq", "mp"),
            P(None, None, "mp"),
            P("mp"),
            P(None, "mp"),
            P("dp", "seq", "mp"),
        ),
        out_specs=(P("dp", "seq", "mp"), P("seq", None, "mp")),
        check_vma=False,
    )
```

```python
import jax
import jax.numpy as jnp
from jax import lax
from jax.experimental import pallas as pl
from jax.experimental.pallas import tpu as pltpu
from jax.sharding import PartitionSpec as P

MESH = pl.DeviceIdType.MESH
BF16, F32 = jnp.bfloat16, jnp.float32
KW = 5
T = 1024
R = 512
CB = 320
O = 384
OT = O // 128
C = 4 * CB
N = KW * O
Q = 640
TB = 128
TC = 256
XB = 320
ZB = 80
COLS = (7 * 128, 8 * 128)
PIECE = 4 * 128
Y0 = 8

OWN_R, OWN_L, FWD_R, FWD_L = 0, 8, 16, 24
EDGE_UP, EDGE_DOWN, GRAD_UP, GRAD_DOWN, RIM, GAIN = 32, 33, 34, 35, 35, 38
ENC_R, ENC_L, EFWD_R, EFWD_L = 42, 44, 46, 47
SWAP = 48
SPLIT = (0, 4)
X1R, X1L, X2R, X2L = 53, 54, 55, 57
ZUA, ZUB, ZDA, ZDB = 59, 63, 67, 71
DUP, DDN, DSW = 75, 76, 77
COPIES = 79


def kernel(
    xt_hbm, w_hbm, gain_hbm, qw_hbm, eg_hbm, qout, cgo,
    xt, ends, edge, rim, egrim, wcat, gain, qw, eg, xrow, yb, pgb, pgcat, enc, norm,
    psend, precv, gown, x1l, x1r, x2l, x2r, zb, zr, zs, zr1, zs1, uf, u2l, u2r, fin0, fin1,
    lsem, ssem, rsem,
):
    seq, mp, dp = lax.axis_index("seq"), lax.axis_index("mp"), lax.axis_index("dp")
    x, zl = seq // 4, seq % 4
    zh, core = dp // 2, dp % 2
    z = zh * 4 + zl

    def at(s=None, m=None, d=None):
        return {"seq": seq if s is None else s, "mp": mp if m is None else m, "dp": dp if d is None else d}

    def z_at(zn):
        return at(s=x * 4 + zn % 4, d=(zn // 4) * 2 + core)

    y_right, y_left = at(m=(mp + 1) % 4), at(m=(mp + 3) % 4)
    s_up, s_down = at(s=(seq + 1) % 16), at(s=(seq + 15) % 16)
    x_right, x_left = at(s=(seq + 4) % 16), at(s=(seq + 12) % 16)
    x_far = at(s=(seq + 8) % 16)
    z_up, z_down = z_at((z + 1) % 8), z_at((z + 7) % 8)
    partner = at(d=zh * 2 + 1 - core)
    z_up2, z_down2 = z_at((z + 2) % 8), z_at((z + 6) % 8)

    local = []

    def load(src, dst):
        copy = pltpu.make_async_copy(src, dst, lsem.at[len(local)])
        copy.start()
        local.append(copy)
        return copy

    own_rows = pl.ds(pl.multiple_of(mp * CB, CB), CB)
    end_loads = [load(xt_hbm.at[:, pl.ds(e * (T - 128), 128)], ends.at[e, pl.ds(0, CB)]) for e in (0, 1)]
    own_x = load(xt_hbm, xt.at[own_rows])
    loads = [load(w_hbm.at[k], wcat.at[:, pl.ds(k * O, O)]) for k in range(KW)]
    eg_load = load(eg_hbm, eg)
    gain_load = load(gain_hbm, gain.at[mp])
    qw_load = load(qw_hbm, qw)

    barrier = pltpu.get_barrier_semaphore()
    peers = [y_right, y_left, at(m=(mp + 2) % 4), s_up, s_down, x_right, x_left, x_far, z_up, z_down, z_up2, z_down2, partner]
    for peer in peers:
        pl.semaphore_signal(barrier, inc=1, device_id=peer, device_id_type=MESH)
    pl.semaphore_wait(barrier, len(peers))

    sent = []

    def remote(src, dst, i, peer):
        return pltpu.make_async_remote_copy(
            src_ref=src, dst_ref=dst, send_sem=ssem.at[i], recv_sem=rsem.at[i], device_id=peer, device_id_type=MESH
        )

    def send(src, dst, i, peer):
        copy = remote(src, dst, i, peer)
        copy.start()
        sent.append(copy)

    def arrived(dst, i):
        remote(dst, dst, i, y_right).wait_recv()

    def block(owner, half, tb):
        first = owner * CB + (0 if half is None else half * (CB // 2))
        size = CB if half is None else CB // 2
        return xt.at[pl.ds(pl.multiple_of(first, CB // 2), size), pl.ds(tb * TB, TB)]

    m_left, m_right, m_far = (mp + 3) % 4, (mp + 1) % 4, (mp + 2) % 4

    def send_own(tb):
        src = xt_hbm.at[:, pl.ds(tb * TB, TB)]
        send(src, block(mp, None, tb), OWN_R + tb, y_right)
        send(src, block(mp, None, tb), OWN_L + tb, y_left)

    def forward(tb):
        arrived(block(m_left, None, tb), OWN_R + tb)
        send(block(m_left, 0, tb), block(m_left, 0, tb), FWD_R + tb, y_right)
        arrived(block(m_right, None, tb), OWN_L + tb)
        send(block(m_right, 1, tb), block(m_right, 1, tb), FWD_L + tb, y_left)

    def complete(tb):
        arrived(block(m_far, 0, tb), FWD_R + tb)
        arrived(block(m_far, 1, tb), FWD_L + tb)

    send_own(0)
    send_own(1)
    for d in (1, 2, 3):
        send(gain_hbm, gain.at[mp], GAIN + d, at(m=(mp + d) % 4))
    send(eg_hbm.at[pl.ds(R - 16, 16)], egrim.at[0], GRAD_UP, s_up)
    send(eg_hbm.at[pl.ds(0, 16)], egrim.at[1], GRAD_DOWN, s_down)
    for copy in end_loads:
        copy.wait()
    for e in (0, 1):
        ends[e, CB:, :] = jnp.zeros((O - CB, 128), BF16)
        edge[e] = ends[e].T[112 * e : 112 * e + 16, :]
    send(edge.at[1], rim.at[mp, pl.ds(0, 16)], EDGE_UP, s_up)
    send(edge.at[0], rim.at[mp, pl.ds(16, 16)], EDGE_DOWN, s_down)
    send_own(2)
    own_x.wait()

    def tap_products(g, half):
        if half == 0:
            xrow[...] = xt[:, g * TC : (g + 1) * TC].T

        def tile(n, carry):
            cols = pl.ds(pl.multiple_of(n * 256, 256), 256)
            y = jnp.dot(xrow[...], wcat[:, cols], preferred_element_type=F32)
            yb[2 * n, pl.ds(Y0 + g * TC, TC), :] = y[:, :128]
            yb[2 * n + 1, pl.ds(Y0 + g * TC, TC), :] = y[:, 128:]
            return carry

        if half == 0:
            lax.fori_loop(0, 4, tile, 0)
        else:
            lax.fori_loop(4, N // 256, tile, 0)
            y = jnp.dot(xrow[...], wcat[:, N - 128 :], preferred_element_type=F32)
            yb[N // 128 - 1, pl.ds(Y0 + g * TC, TC), :] = y

    def rim_products():
        for d in (1, 2, 3):
            owner = (mp + 4 - d) % 4
            arrived(rim.at[owner], RIM + d)
        before = jnp.where(seq > 0, 1.0, 0.0).astype(F32)
        after = jnp.where(seq < 15, 1.0, 0.0).astype(F32)

        def tile(n, carry):
            cols = pl.ds(pl.multiple_of(n * 128, 128), 128)
            y = jnp.zeros((32, 128), F32)
            for m in range(4):
                y += jnp.dot(rim[m][:, :CB], wcat[m * CB : (m + 1) * CB, cols], preferred_element_type=F32)
            yb[n, pl.ds(0, 8), :] = y[8:16] * before
            yb[n, pl.ds(Y0 + T, 8), :] = y[16:24] * after
            return carry

        lax.fori_loop(0, N // 128, tile, 0)

    def gelu(v):
        v2 = v * v
        th = jnp.tanh(v * (0.7978845608 + (0.7978845608 * 0.044715) * v2))
        half = 0.5 + 0.5 * th
        slope = half + 0.5 * v * (1.0 - th * th) * (0.7978845608 + (0.7978845608 * 0.134145) * v2)
        return v * half, slope

    def pre(o, row, rows, stride):
        taps = [yb[k * OT + o, pl.ds(row + k - 2, rows, stride=stride), :] for k in range(KW)]
        return taps[0] + taps[1] + taps[2] + taps[3] + taps[4]

    STEP = 32

    def activations(first, count):
        def rows_of(i, carry):
            j = pl.multiple_of(first + i * STEP, STEP)
            for o in range(OT):
                lanes = pl.ds(o * 128, 128)
                act_e, slope_e = gelu(pre(o, Y0 + 2 * j, STEP, 2))
                act_o, slope_o = gelu(pre(o, Y0 + 2 * j + 1, STEP, 2))
                g = 0.5 * eg[pl.ds(j, STEP), lanes].astype(F32)
                enc[mp, pl.ds(j, STEP), lanes] = (0.5 * (act_e + act_o)).astype(BF16)
                pgb[o, pl.ds(Y0 + 2 * j, STEP, stride=2), :] = slope_e * g
                pgb[o, pl.ds(Y0 + 2 * j + 1, STEP, stride=2), :] = slope_o * g
            return carry

        lax.fori_loop(0, count // STEP, rows_of, 0)

    def rim_gradients(side):
        before = jnp.where(seq > 0, 0.5, 0.0).astype(F32)
        after = jnp.where(seq < 15, 0.5, 0.0).astype(F32)
        last, first = egrim[0, 8:16, :].astype(F32), egrim[1, 0:8, :].astype(F32)
        for o in range(OT):
            lanes = slice(o * 128, (o + 1) * 128)
            row, g = ((Y0 - 2, last[7:8, lanes] * before), (Y0 + T, first[0:1, lanes] * after))[side]
            for r in (row, row + 1):
                slope = gelu(pre(o, r, 1, 1))[1]
                pgb[o, pl.ds(r, 1), :] = slope * g

    PSTEP = 64

    def gradient_columns(first, count):
        def rows_of(i, carry):
            s = pl.multiple_of(first + i * PSTEP, PSTEP)
            for k in range(KW):
                for o in range(OT):
                    pgcat[pl.ds(s, PSTEP), (k * OT + o) * 128 : (k * OT + o + 1) * 128] = pgb[
                        o, pl.ds(Y0 + s + 2 - k, PSTEP), :
                    ].astype(BF16)
            return carry

        lax.fori_loop(0, count // PSTEP, rows_of, 0)

    def serve(i):
        forward(i)
        if i + 3 < T // TB:
            send_own(i + 3)

    def group(g):
        complete(2 * g)
        complete(2 * g + 1)

    serve(0)
    arrived(rim.at[mp, pl.ds(0, 16)], EDGE_UP)
    arrived(rim.at[mp, pl.ds(16, 16)], EDGE_DOWN)
    for d in (1, 2, 3):
        send(rim.at[mp], rim.at[mp], RIM + d, at(m=(mp + d) % 4))
    serve(1)
    for copy in loads:
        copy.wait()
    serve(2)
    group(0)
    tap_products(0, 0)
    serve(3)
    tap_products(0, 1)
    rim_products()
    serve(4)
    group(1)
    tap_products(1, 0)
    serve(5)
    tap_products(1, 1)
    eg_load.wait()
    activations(0, 224)
    arrived(egrim.at[0], GRAD_UP)
    arrived(egrim.at[1], GRAD_DOWN)
    rim_gradients(0)
    serve(6)
    gradient_columns(0, 384)
    group(2)
    tap_products(2, 0)
    serve(7)
    tap_products(2, 1)
    activations(224, 128)
    gradient_columns(384, 256)
    group(3)
    tap_products(3, 0)
    tap_products(3, 1)
    activations(352, 160)
    rim_gradients(1)

    def half_rows(owner, e):
        return enc.at[owner, pl.ds(e * (R // 2), R // 2)]

    send(half_rows(mp, 0), half_rows(mp, 0), ENC_R, y_right)
    send(half_rows(mp, 1), half_rows(mp, 1), ENC_L + 1, y_left)
    send(half_rows(mp, 1), half_rows(mp, 1), ENC_R + 1, y_right)
    send(half_rows(mp, 0), half_rows(mp, 0), ENC_L, y_left)
    gradient_columns(640, 384)

    def rows_of_z(g):
        return jnp.concatenate(
            [xt[pl.ds(pl.multiple_of(xb * XB + g * ZB, ZB), ZB), :] for xb in range(4)], axis=0
        )

    def products(left, owner, write):
        first, width = owner * COLS[0], COLS[owner]

        def tile(n, carry):
            lane = pl.multiple_of(n * 256, 256)
            write(lane, 256, jnp.dot(left, pgcat[:, pl.ds(first + lane, 256)], preferred_element_type=F32))
            return carry

        lax.fori_loop(0, width // 256, tile, 0)
        if width % 256:
            lane = width // 256 * 256
            write(lane, 128, jnp.dot(left, pgcat[:, pl.ds(first + lane, 128)], preferred_element_type=F32))

    def left_rows(kind, b, half):
        if kind:
            return rows_of_z(b)
        first, rows = (0, XB) if half is None else (half * (XB // 2), XB // 2)
        return xt[pl.ds(pl.multiple_of(b * XB + first, XB // 2), rows), :]

    def span(half):
        return pl.ds(0, XB) if half is None else pl.ds(half * (XB // 2), XB // 2)

    def theirs(other, step, b, half=None):
        rows = span(half)

        def write(lane, width, value):
            psend[b, rows, pl.ds(lane, width)] = value.astype(BF16)

        products(left_rows(other, b, half), other, write)
        cols = pl.ds(0, COLS[other])
        send(psend.at[b, rows, cols], precv.at[b, rows, cols], SWAP + step, partner)

    def ours(me, step, b, half=None, waits=True):
        rows = span(half)
        if waits:
            arrived(precv.at[b, span(half if me == 0 and step in SPLIT else None), pl.ds(0, COLS[me])], SWAP + step)

        def write(lane, width, value):
            cols = pl.ds(lane, width)
            gown[b, rows, cols] = (value + precv[b, rows, cols].astype(F32)).astype(BF16)

        products(left_rows(me, b, half), me, write)

    def add(dst, src):
        for r in range(0, dst.shape[0], 16):
            rows = pl.ds(r, 16)
            dst[rows, :] = (dst[rows, :].astype(F32) + src[rows, :].astype(F32)).astype(BF16)

    def add_to(dst, a, b):
        for r in range(0, dst.shape[0], 16):
            rows = pl.ds(r, 16)
            dst[rows, :] = (a[rows, :].astype(F32) + b[rows, :].astype(F32)).astype(BF16)

    def add3(dst, a, b, c):
        for r in range(0, dst.shape[0], 16):
            rows = pl.ds(r, 16)
            dst[rows, :] = (a[rows, :].astype(F32) + b[rows, :].astype(F32) + c[rows, :].astype(F32)).astype(BF16)

    def forward_encoded():
        arrived(half_rows(m_left, 0), ENC_R)
        send(half_rows(m_left, 0), half_rows(m_left, 0), EFWD_R, y_right)
        arrived(half_rows(m_right, 1), ENC_L + 1)
        send(half_rows(m_right, 1), half_rows(m_right, 1), EFWD_L, y_left)

    def encoded_complete():
        arrived(half_rows(m_left, 1), ENC_R + 1)
        arrived(half_rows(m_right, 0), ENC_L)
        arrived(half_rows(m_far, 0), EFWD_R)
        arrived(half_rows(m_far, 1), EFWD_L)
        gain_load.wait()
        for d in (1, 2, 3):
            arrived(gain.at[(mp + 4 - d) % 4], GAIN + d)
        qw_load.wait()

    def heads(part):
        def normalize(i, carry):
            rows = pl.ds(pl.multiple_of(part * 128 + i * 32, 32), 32)
            values = [enc[m, rows, :].astype(F32) for m in range(4)]
            total = jnp.sum(values[0] + values[1] + values[2] + values[3], axis=1, keepdims=True)
            square = jnp.sum(sum(v * v for v in values), axis=1, keepdims=True)
            mean = total / (4 * O)
            scale = lax.rsqrt(square / (4 * O) - mean * mean + 1e-05)
            for m in range(4):
                norm[rows, m * O : (m + 1) * O] = ((values[m] - mean) * scale * gain[m]).astype(BF16)
            return carry

        lax.fori_loop(0, 4, normalize, 0)
        rows = pl.ds(part * 128, 128)
        qout[rows, :] = jnp.dot(norm[rows, :], qw[...], preferred_element_type=F32).astype(BF16)

    top, bottom, own = pl.ds(0, XB // 2), pl.ds(XB // 2, XB // 2), pl.ds(0, COLS[0])
    xf, xr, xl = (x + 2) % 4, (x + 1) % 4, (x + 3) % 4
    gf, gr, gl = (zl + 2) % 4, (zl + 1) % 4, (zl + 3) % 4

    lower, upper = (z + 6) % 8 // 4, (z + 2) % 8 // 4

    def z_chain(step, part, base, received, staged):
        for sign, ids, peer in ((1, (ZUA, ZUB), z_up), (-1, (ZDA, ZDB), z_down)):
            z_hop(sign, step, part, base, received, staged, ids[part] + step - 1, peer)

    def z_hop(sign, step, part, base, received, staged, i, peer):
        src = base(sign, step, part)
        if step > 1 + part:
            arrived(received(sign, step - 1, part), i - 1)
            dst = staged(sign, step, part)
            add_to(dst, src, received(sign, step - 1, part))
            src = dst
        send(src, received(sign, step, part), i, peer)

    def z_last(received):
        for sign, ids in ((1, (ZUA, ZUB)), (-1, (ZDA, ZDB))):
            for part in (0, 1):
                arrived(received(sign, 4, part), ids[part] + 3)

    shared = len(sent)

    @pl.when(core == 0)
    def _():
        theirs(1, 0, gf)
        ours(0, 0, xf, 0)
        send(gown.at[xf, top, own], x1l, X1R, x_right)
        ours(0, 4, xf, 1)
        send(gown.at[xf, bottom, own], x1r, X1L, x_left)
        theirs(1, 1, gr)
        ours(0, 1, xr, 1)
        send(gown.at[xr, bottom, own], x2l.at[bottom], X2R + 1, x_right)
        ours(0, 1, xr, 0, waits=False)
        theirs(1, 2, gl)
        forward_encoded()
        theirs(1, 3, zl)
        arrived(x1l, X1R)
        add(gown.at[xr, top, own], x1l)
        send(gown.at[xr, top, own], x2l.at[top], X2R, x_right)
        ours(0, 2, xl)
        send(gown.at[xl, top, own], x2r.at[top], X2L, x_left)
        arrived(x1r, X1L)
        add(gown.at[xl, bottom, own], x1r)
        send(gown.at[xl, bottom, own], x2r.at[bottom], X2L + 1, x_left)
        ours(0, 3, x)
        for half, rows in ((0, top), (1, bottom)):
            arrived(x2l.at[rows], X2R + half)
            arrived(x2r.at[rows], X2L + half)
        for g in range(4):
            rows = pl.ds(g * ZB, ZB)
            add3(zb.at[g], gown.at[x, rows, own], x2l.at[rows], x2r.at[rows])

        spans = (pl.ds(0, 512), pl.ds(512, 384))

        def cols(sign, part):
            return spans[part if sign == 1 else 1 - part]

        def way(sign):
            return 0 if sign == 1 else 1

        def base(sign, step, part):
            return zb.at[(zl + 5 - step if sign == 1 else zl + 3 + step) % 4, :, cols(sign, part)]

        def received(sign, step, part):
            return zr.at[way(sign), step - 1, :, cols(sign, part)]

        def staged(sign, step, part):
            return zs.at[way(sign), step - 2, :, cols(sign, part)]

        z_chain(1, 0, base, received, staged)
        z_chain(2, 1, base, received, staged)
        encoded_complete()
        heads(0)
        z_chain(2, 0, base, received, staged)
        z_chain(3, 1, base, received, staged)
        heads(1)
        z_chain(3, 0, base, received, staged)
        z_chain(4, 1, base, received, staged)
        heads(2)
        z_chain(4, 0, base, received, staged)
        heads(3)
        z_last(received)
        add3(fin0, zb.at[zl], zr.at[0, 3], zr.at[1, 3])
        send(fin0, fin0, DSW, partner)
        arrived(fin1.at[lower], DSW)
        arrived(fin1.at[upper], DSW + 1)
        for copy in sent:
            copy.wait_send()

    @pl.when(core == 1)
    def _():
        del sent[shared:]
        theirs(0, 0, xf, 0)
        theirs(0, 4, xf, 1)
        theirs(0, 1, xr)
        ours(1, 0, gf)

        def piece(zo):
            return gown.at[(zo + 2) % 4, :, pl.ds(pl.multiple_of(zo // 4 * PIECE, 128), PIECE)]

        def half(ref, sign, part):
            return ref.at[top if (part == 0) == (sign == 1) else bottom]

        def base(sign, step, part):
            return half(piece((z + 5 - step if sign == 1 else z + 3 + step) % 8), sign, part)

        def received(sign, step, part):
            return half(zr1.at[0 if sign == 1 else 1, step - 1], sign, part)

        def hop(sign, step, part):
            i, peer = ((ZUA, ZUB)[part], z_up) if sign == 1 else ((ZDA, ZDB)[part], z_down)
            z_hop(sign, step, part, base, received, base, i + step - 1, peer)

        z_chain(1, 0, base, received, base)
        theirs(0, 2, xl)
        ours(1, 1, gr)
        hop(1, 2, 1)
        hop(1, 2, 0)
        theirs(0, 3, x)
        ours(1, 2, gl)
        hop(-1, 2, 1)
        hop(-1, 2, 0)
        forward_encoded()
        ours(1, 3, zl)
        z_chain(3, 1, base, received, base)
        z_chain(3, 0, base, received, base)
        z_chain(4, 1, base, received, base)
        z_chain(4, 0, base, received, base)
        encoded_complete()
        heads(0)
        heads(1)
        z_last(received)
        add3(zs1, piece(z), zr1.at[0, 3], zr1.at[1, 3])

        def rows_at(xb):
            return zs1.at[pl.ds(pl.multiple_of(xb * ZB, ZB), ZB)]

        send(rows_at(xf), uf, X1R, x_far)
        send(rows_at(xr), u2l, X2R, x_right)
        send(rows_at(xl), u2r, X2L, x_left)
        heads(2)
        arrived(u2l, X2R)
        arrived(u2r, X2L)
        arrived(uf, X1R)
        mine = rows_at(x)
        for r in range(0, ZB, 16):
            rows = pl.ds(r, 16)
            parts = [ref[rows, :].astype(F32) for ref in (mine, u2l, u2r, uf)]
            mine[rows, :] = (parts[0] + parts[1] + parts[2] + parts[3]).astype(BF16)
        send(mine, fin1.at[zh], DUP, z_up2)
        send(mine, fin1.at[zh], DDN, z_down2)
        heads(3)
        arrived(fin1.at[lower], DUP)
        send(fin1.at[lower], fin1.at[lower], DSW, partner)
        arrived(fin1.at[upper], DDN)
        send(fin1.at[upper], fin1.at[upper], DSW + 1, partner)
        arrived(fin0, DSW)
        for copy in sent:
            copy.wait_send()

    for i in range(N // 128):
        if i < 7:
            src = fin0.at[:, pl.ds(i * 128, 128)]
        else:
            src = fin1.at[(i - 7) // 4, :, pl.ds((i - 7) % 4 * 128, 128)]
        cgo[i // OT, :, pl.ds((i % OT) * 128, 128)] = src[...].astype(F32)


def finish(qkv_in, grad_in, qkv_out, grad_out, sem):
    copies = [
        pltpu.make_async_copy(grad_in, grad_out, sem.at[0]),
        pltpu.make_async_copy(qkv_in, qkv_out, sem.at[1]),
    ]
    for copy in copies:
        copy.start()
    for copy in copies:
        copy.wait()


def on_device(block_input, conv_weight, norm_gain, qkv_weight, encoder_grad):
    xin, eg = block_input[0], encoder_grad[0]
    any_ = pl.BlockSpec(memory_space=pl.ANY)
    v = pltpu.VMEM
    qkv, grad = pl.pallas_call(
        kernel,
        name="block",
        out_shape=(jax.ShapeDtypeStruct((R, Q), BF16), jax.ShapeDtypeStruct((KW, ZB, O), F32)),
        in_specs=[pl.BlockSpec(memory_space=pltpu.HBM)] * 5,
        out_specs=(pl.BlockSpec(memory_space=pltpu.VMEM),) * 2,
        scratch_shapes=[
            v((C, T), BF16), v((2, O, 128), BF16), v((2, 16, O), BF16), v((4, 32, O), BF16), v((2, 16, O), BF16),
            v((C, N), BF16), v((4, O), F32), v((4 * O, Q), BF16), v((R, O), BF16),
            v((TC, C), BF16), v((N // 128, T + 16, 128), F32), v((OT, T + 16, 128), F32), v((T, N), BF16),
            v((4, R, O), BF16), v((R, 4 * O), BF16),
            v((4, XB, COLS[1]), BF16), v((4, XB, COLS[1]), BF16), v((4, XB, COLS[1]), BF16),
            v((XB // 2, COLS[0]), BF16), v((XB // 2, COLS[0]), BF16), v((XB, COLS[0]), BF16), v((XB, COLS[0]), BF16),
            v((4, ZB, COLS[0]), BF16), v((2, 4, ZB, COLS[0]), BF16), v((2, 3, ZB, COLS[0]), BF16),
            v((2, 4, XB, PIECE), BF16), v((XB, PIECE), BF16),
            v((ZB, PIECE), BF16), v((ZB, PIECE), BF16), v((ZB, PIECE), BF16),
            v((ZB, COLS[0]), BF16), v((2, ZB, PIECE), BF16),
            pltpu.SemaphoreType.DMA((16,)), pltpu.SemaphoreType.DMA((COPIES,)), pltpu.SemaphoreType.DMA((COPIES,)),
        ],
        compiler_params=pltpu.CompilerParams(collective_id=0, has_side_effects=True, vmem_limit_bytes=50 * 2**20),
    )(*(pltpu.with_memory_space_constraint(a, pltpu.HBM) for a in (xin.T, conv_weight, norm_gain, qkv_weight, eg)))
    qkv, grad = pl.pallas_call(
        finish,
        name="finish",
        out_shape=(jax.ShapeDtypeStruct((R, Q), BF16), jax.ShapeDtypeStruct((KW, ZB, O), F32)),
        in_specs=[any_] * 2,
        out_specs=(any_, any_),
        scratch_shapes=[pltpu.SemaphoreType.DMA((2,))],
        compiler_params=pltpu.CompilerParams(vmem_limit_bytes=4 * 2**20),
    )(qkv, grad)
    return qkv[None], grad.transpose(1, 0, 2)


def solution(mesh):
    return jax.shard_map(
        on_device,
        mesh=mesh,
        in_specs=(
            P("dp", "seq", "mp"),
            P(None, None, "mp"),
            P("mp"),
            P(None, "mp"),
            P("dp", "seq", "mp"),
        ),
        out_specs=(P("dp", "seq", "mp"), P("seq", None, "mp")),
        check_vma=False,
    )
```

```python
import jax
import jax.numpy as jnp
from jax import lax
from jax.experimental import pallas as pl
from jax.experimental.pallas import tpu as pltpu
from jax.sharding import PartitionSpec as P

MESH = pl.DeviceIdType.MESH
BF16, F32 = jnp.bfloat16, jnp.float32
KW = 5
T = 1024
R = 512
CB = 320
O = 384
OT = O // 128
C = 4 * CB
N = KW * O
Q = 640
TB = 128
TC = 256
XB = 320
ZB = 80
COLS = (7 * 128, 8 * 128)
PIECE = 4 * 128
Y0 = 8

OWN_R, OWN_L, FWD_R, FWD_L = 0, 8, 16, 24
EDGE_UP, EDGE_DOWN, GRAD_UP, GRAD_DOWN, RIM, GAIN = 32, 33, 34, 35, 35, 38
ENC_R, ENC_L, EFWD_R, EFWD_L = 42, 44, 46, 47
SWAP = 48
SPLIT = (0, 4)
X1R, X1L, X2R, X2L = 53, 54, 55, 57
ZUA, ZUB, ZDA, ZDB = 59, 63, 67, 71
DUP, DDN, DSW = 75, 76, 77
COPIES = 79


def kernel(
    xt_hbm, w_hbm, gain_hbm, qw_hbm, eg_hbm, qout, cgo,
    xt, ends, edge, rim, egrim, wcat, gain, qw, eg, xrow, yb, pgb, pgcat, enc, norm,
    psend, precv, gown, x1l, x1r, x2l, x2r, zb, zr, zs, zr1, zs1, uf, u2l, u2r, fin0, fin1,
    lsem, ssem, rsem,
):
    seq, mp, dp = lax.axis_index("seq"), lax.axis_index("mp"), lax.axis_index("dp")
    x, zl = seq // 4, seq % 4
    zh, core = dp // 2, dp % 2
    z = zh * 4 + zl

    def at(s=None, m=None, d=None):
        return {"seq": seq if s is None else s, "mp": mp if m is None else m, "dp": dp if d is None else d}

    def z_at(zn):
        return at(s=x * 4 + zn % 4, d=(zn // 4) * 2 + core)

    y_right, y_left = at(m=(mp + 1) % 4), at(m=(mp + 3) % 4)
    s_up, s_down = at(s=(seq + 1) % 16), at(s=(seq + 15) % 16)
    x_right, x_left = at(s=(seq + 4) % 16), at(s=(seq + 12) % 16)
    x_far = at(s=(seq + 8) % 16)
    z_up, z_down = z_at((z + 1) % 8), z_at((z + 7) % 8)
    partner = at(d=zh * 2 + 1 - core)
    z_up2, z_down2 = z_at((z + 2) % 8), z_at((z + 6) % 8)

    local = []

    def load(src, dst):
        copy = pltpu.make_async_copy(src, dst, lsem.at[len(local)])
        copy.start()
        local.append(copy)
        return copy

    own_rows = pl.ds(pl.multiple_of(mp * CB, CB), CB)
    end_loads = [load(xt_hbm.at[:, pl.ds(e * (T - 128), 128)], ends.at[e, pl.ds(0, CB)]) for e in (0, 1)]
    own_x = load(xt_hbm, xt.at[own_rows])
    loads = [load(w_hbm.at[k], wcat.at[:, pl.ds(k * O, O)]) for k in range(KW)]
    eg_load = load(eg_hbm, eg)
    gain_load = load(gain_hbm, gain.at[mp])
    qw_load = load(qw_hbm, qw)

    barrier = pltpu.get_barrier_semaphore()
    peers = [y_right, y_left, at(m=(mp + 2) % 4), s_up, s_down, x_right, x_left, x_far, z_up, z_down, z_up2, z_down2, partner]
    for peer in peers:
        pl.semaphore_signal(barrier, inc=1, device_id=peer, device_id_type=MESH)
    pl.semaphore_wait(barrier, len(peers))

    sent = []

    def remote(src, dst, i, peer):
        return pltpu.make_async_remote_copy(
            src_ref=src, dst_ref=dst, send_sem=ssem.at[i], recv_sem=rsem.at[i], device_id=peer, device_id_type=MESH
        )

    def send(src, dst, i, peer):
        copy = remote(src, dst, i, peer)
        copy.start()
        sent.append(copy)

    def arrived(dst, i):
        remote(dst, dst, i, y_right).wait_recv()

    def block(owner, half, tb):
        first = owner * CB + (0 if half is None else half * (CB // 2))
        size = CB if half is None else CB // 2
        return xt.at[pl.ds(pl.multiple_of(first, CB // 2), size), pl.ds(tb * TB, TB)]

    m_left, m_right, m_far = (mp + 3) % 4, (mp + 1) % 4, (mp + 2) % 4

    def send_own(tb):
        src = xt_hbm.at[:, pl.ds(tb * TB, TB)]
        send(src, block(mp, None, tb), OWN_R + tb, y_right)
        send(src, block(mp, None, tb), OWN_L + tb, y_left)

    def forward(tb):
        arrived(block(m_left, None, tb), OWN_R + tb)
        send(block(m_left, 0, tb), block(m_left, 0, tb), FWD_R + tb, y_right)
        arrived(block(m_right, None, tb), OWN_L + tb)
        send(block(m_right, 1, tb), block(m_right, 1, tb), FWD_L + tb, y_left)

    def complete(tb):
        arrived(block(m_far, 0, tb), FWD_R + tb)
        arrived(block(m_far, 1, tb), FWD_L + tb)

    send_own(0)
    send_own(1)
    for d in (1, 2, 3):
        send(gain_hbm, gain.at[mp], GAIN + d, at(m=(mp + d) % 4))
    send(eg_hbm.at[pl.ds(R - 16, 16)], egrim.at[0], GRAD_UP, s_up)
    send(eg_hbm.at[pl.ds(0, 16)], egrim.at[1], GRAD_DOWN, s_down)
    for copy in end_loads:
        copy.wait()
    for e in (0, 1):
        ends[e, CB:, :] = jnp.zeros((O - CB, 128), BF16)
        edge[e] = ends[e].T[112 * e : 112 * e + 16, :]
    send(edge.at[1], rim.at[mp, pl.ds(0, 16)], EDGE_UP, s_up)
    send(edge.at[0], rim.at[mp, pl.ds(16, 16)], EDGE_DOWN, s_down)
    send_own(2)
    own_x.wait()

    def tap_products(g, half):
        if half == 0:
            xrow[...] = xt[:, g * TC : (g + 1) * TC].T

        def tile(n, carry):
            cols = pl.ds(pl.multiple_of(n * 256, 256), 256)
            y = jnp.dot(xrow[...], wcat[:, cols], preferred_element_type=F32)
            yb[2 * n, pl.ds(Y0 + g * TC, TC), :] = y[:, :128]
            yb[2 * n + 1, pl.ds(Y0 + g * TC, TC), :] = y[:, 128:]
            return carry

        if half == 0:
            lax.fori_loop(0, 4, tile, 0)
        else:
            lax.fori_loop(4, N // 256, tile, 0)
            y = jnp.dot(xrow[...], wcat[:, N - 128 :], preferred_element_type=F32)
            yb[N // 128 - 1, pl.ds(Y0 + g * TC, TC), :] = y

    def rim_products():
        for d in (1, 2, 3):
            owner = (mp + 4 - d) % 4
            arrived(rim.at[owner], RIM + d)
        before = jnp.where(seq > 0, 1.0, 0.0).astype(F32)
        after = jnp.where(seq < 15, 1.0, 0.0).astype(F32)

        def tile(n, carry):
            cols = pl.ds(pl.multiple_of(n * 128, 128), 128)
            y = jnp.zeros((32, 128), F32)
            for m in range(4):
                y += jnp.dot(rim[m][:, :CB], wcat[m * CB : (m + 1) * CB, cols], preferred_element_type=F32)
            yb[n, pl.ds(0, 8), :] = y[8:16] * before
            yb[n, pl.ds(Y0 + T, 8), :] = y[16:24] * after
            return carry

        lax.fori_loop(0, N // 128, tile, 0)

    def gelu(v):
        v2 = v * v
        th = jnp.tanh(v * (0.7978845608 + (0.7978845608 * 0.044715) * v2))
        half = 0.5 + 0.5 * th
        slope = half + 0.5 * v * (1.0 - th * th) * (0.7978845608 + (0.7978845608 * 0.134145) * v2)
        return v * half, slope

    def pre(o, row, rows, stride):
        taps = [yb[k * OT + o, pl.ds(row + k - 2, rows, stride=stride), :] for k in range(KW)]
        return taps[0] + taps[1] + taps[2] + taps[3] + taps[4]

    STEP = 32

    def activations(first, count):
        def rows_of(i, carry):
            j = pl.multiple_of(first + i * STEP, STEP)
            for o in range(OT):
                lanes = pl.ds(o * 128, 128)
                act_e, slope_e = gelu(pre(o, Y0 + 2 * j, STEP, 2))
                act_o, slope_o = gelu(pre(o, Y0 + 2 * j + 1, STEP, 2))
                g = 0.5 * eg[pl.ds(j, STEP), lanes].astype(F32)
                enc[mp, pl.ds(j, STEP), lanes] = (0.5 * (act_e + act_o)).astype(BF16)
                pgb[o, pl.ds(Y0 + 2 * j, STEP, stride=2), :] = slope_e * g
                pgb[o, pl.ds(Y0 + 2 * j + 1, STEP, stride=2), :] = slope_o * g
            return carry

        lax.fori_loop(0, count // STEP, rows_of, 0)

    def rim_gradients(side):
        before = jnp.where(seq > 0, 0.5, 0.0).astype(F32)
        after = jnp.where(seq < 15, 0.5, 0.0).astype(F32)
        last, first = egrim[0, 8:16, :].astype(F32), egrim[1, 0:8, :].astype(F32)
        for o in range(OT):
            lanes = slice(o * 128, (o + 1) * 128)
            row, g = ((Y0 - 2, last[7:8, lanes] * before), (Y0 + T, first[0:1, lanes] * after))[side]
            for r in (row, row + 1):
                slope = gelu(pre(o, r, 1, 1))[1]
                pgb[o, pl.ds(r, 1), :] = slope * g

    PSTEP = 64

    def gradient_columns(first, count):
        def rows_of(i, carry):
            s = pl.multiple_of(first + i * PSTEP, PSTEP)
            for k in range(KW):
                for o in range(OT):
                    pgcat[pl.ds(s, PSTEP), (k * OT + o) * 128 : (k * OT + o + 1) * 128] = pgb[
                        o, pl.ds(Y0 + s + 2 - k, PSTEP), :
                    ].astype(BF16)
            return carry

        lax.fori_loop(0, count // PSTEP, rows_of, 0)

    def serve(i):
        forward(i)
        if i + 3 < T // TB:
            send_own(i + 3)

    def group(g):
        complete(2 * g)
        complete(2 * g + 1)

    serve(0)
    arrived(rim.at[mp, pl.ds(0, 16)], EDGE_UP)
    arrived(rim.at[mp, pl.ds(16, 16)], EDGE_DOWN)
    for d in (1, 2, 3):
        send(rim.at[mp], rim.at[mp], RIM + d, at(m=(mp + d) % 4))
    serve(1)
    for copy in loads:
        copy.wait()
    serve(2)
    group(0)
    tap_products(0, 0)
    serve(3)
    tap_products(0, 1)
    rim_products()
    serve(4)
    group(1)
    tap_products(1, 0)
    serve(5)
    tap_products(1, 1)
    eg_load.wait()
    activations(0, 224)
    arrived(egrim.at[0], GRAD_UP)
    arrived(egrim.at[1], GRAD_DOWN)
    rim_gradients(0)
    serve(6)
    gradient_columns(0, 384)
    group(2)
    tap_products(2, 0)
    serve(7)
    tap_products(2, 1)
    activations(224, 128)
    gradient_columns(384, 256)
    group(3)
    tap_products(3, 0)
    tap_products(3, 1)
    activations(352, 160)
    rim_gradients(1)

    def half_rows(owner, e):
        return enc.at[owner, pl.ds(e * (R // 2), R // 2)]

    send(half_rows(mp, 0), half_rows(mp, 0), ENC_R, y_right)
    send(half_rows(mp, 1), half_rows(mp, 1), ENC_L + 1, y_left)
    send(half_rows(mp, 1), half_rows(mp, 1), ENC_R + 1, y_right)
    send(half_rows(mp, 0), half_rows(mp, 0), ENC_L, y_left)
    gradient_columns(640, 384)

    def rows_of_z(g):
        return jnp.concatenate(
            [xt[pl.ds(pl.multiple_of(xb * XB + g * ZB, ZB), ZB), :] for xb in range(4)], axis=0
        )

    def products(left, owner, write):
        first, width = owner * COLS[0], COLS[owner]

        def tile(n, carry):
            lane = pl.multiple_of(n * 256, 256)
            write(lane, 256, jnp.dot(left, pgcat[:, pl.ds(first + lane, 256)], preferred_element_type=F32))
            return carry

        lax.fori_loop(0, width // 256, tile, 0)
        if width % 256:
            lane = width // 256 * 256
            write(lane, 128, jnp.dot(left, pgcat[:, pl.ds(first + lane, 128)], preferred_element_type=F32))

    def left_rows(kind, b, half):
        if kind:
            return rows_of_z(b)
        first, rows = (0, XB) if half is None else (half * (XB // 2), XB // 2)
        return xt[pl.ds(pl.multiple_of(b * XB + first, XB // 2), rows), :]

    def span(half):
        return pl.ds(0, XB) if half is None else pl.ds(half * (XB // 2), XB // 2)

    def theirs(other, step, b, half=None):
        rows = span(half)

        def write(lane, width, value):
            psend[b, rows, pl.ds(lane, width)] = value.astype(BF16)

        products(left_rows(other, b, half), other, write)
        cols = pl.ds(0, COLS[other])
        send(psend.at[b, rows, cols], precv.at[b, rows, cols], SWAP + step, partner)

    def ours(me, step, b, half=None, waits=True):
        rows = span(half)
        if waits:
            arrived(precv.at[b, span(half if me == 0 and step in SPLIT else None), pl.ds(0, COLS[me])], SWAP + step)

        def write(lane, width, value):
            cols = pl.ds(lane, width)
            gown[b, rows, cols] = (value + precv[b, rows, cols].astype(F32)).astype(BF16)

        products(left_rows(me, b, half), me, write)

    def add(dst, src):
        for r in range(0, dst.shape[0], 16):
            rows = pl.ds(r, 16)
            dst[rows, :] = (dst[rows, :].astype(F32) + src[rows, :].astype(F32)).astype(BF16)

    def add_to(dst, a, b):
        for r in range(0, dst.shape[0], 16):
            rows = pl.ds(r, 16)
            dst[rows, :] = (a[rows, :].astype(F32) + b[rows, :].astype(F32)).astype(BF16)

    def add3(dst, a, b, c):
        for r in range(0, dst.shape[0], 16):
            rows = pl.ds(r, 16)
            dst[rows, :] = (a[rows, :].astype(F32) + b[rows, :].astype(F32) + c[rows, :].astype(F32)).astype(BF16)

    def forward_encoded():
        arrived(half_rows(m_left, 0), ENC_R)
        send(half_rows(m_left, 0), half_rows(m_left, 0), EFWD_R, y_right)
        arrived(half_rows(m_right, 1), ENC_L + 1)
        send(half_rows(m_right, 1), half_rows(m_right, 1), EFWD_L, y_left)

    def encoded_complete():
        arrived(half_rows(m_left, 1), ENC_R + 1)
        arrived(half_rows(m_right, 0), ENC_L)
        arrived(half_rows(m_far, 0), EFWD_R)
        arrived(half_rows(m_far, 1), EFWD_L)
        gain_load.wait()
        for d in (1, 2, 3):
            arrived(gain.at[(mp + 4 - d) % 4], GAIN + d)
        qw_load.wait()

    def heads(part):
        def normalize(i, carry):
            rows = pl.ds(pl.multiple_of(part * 128 + i * 32, 32), 32)
            values = [enc[m, rows, :].astype(F32) for m in range(4)]
            total = jnp.sum(values[0] + values[1] + values[2] + values[3], axis=1, keepdims=True)
            square = jnp.sum(sum(v * v for v in values), axis=1, keepdims=True)
            mean = total / (4 * O)
            scale = lax.rsqrt(square / (4 * O) - mean * mean + 1e-05)
            for m in range(4):
                norm[rows, m * O : (m + 1) * O] = ((values[m] - mean) * scale * gain[m]).astype(BF16)
            return carry

        lax.fori_loop(0, 4, normalize, 0)
        rows = pl.ds(part * 128, 128)
        qout[rows, :] = jnp.dot(norm[rows, :], qw[...], preferred_element_type=F32).astype(BF16)

    top, bottom, own = pl.ds(0, XB // 2), pl.ds(XB // 2, XB // 2), pl.ds(0, COLS[0])
    xf, xr, xl = (x + 2) % 4, (x + 1) % 4, (x + 3) % 4
    gf, gr, gl = (zl + 2) % 4, (zl + 1) % 4, (zl + 3) % 4

    lower, upper = (z + 6) % 8 // 4, (z + 2) % 8 // 4

    def z_chain(step, part, base, received, staged):
        for sign, ids, peer in ((1, (ZUA, ZUB), z_up), (-1, (ZDA, ZDB), z_down)):
            z_hop(sign, step, part, base, received, staged, ids[part] + step - 1, peer)

    def z_hop(sign, step, part, base, received, staged, i, peer):
        src = base(sign, step, part)
        if step > 1 + part:
            arrived(received(sign, step - 1, part), i - 1)
            dst = staged(sign, step, part)
            add_to(dst, src, received(sign, step - 1, part))
            src = dst
        send(src, received(sign, step, part), i, peer)

    def z_last(received):
        for sign, ids in ((1, (ZUA, ZUB)), (-1, (ZDA, ZDB))):
            for part in (0, 1):
                arrived(received(sign, 4, part), ids[part] + 3)

    shared = len(sent)

    @pl.when(core == 0)
    def _():
        theirs(1, 0, gf)
        ours(0, 0, xf, 0)
        send(gown.at[xf, top, own], x1l, X1R, x_right)
        ours(0, 4, xf, 1)
        send(gown.at[xf, bottom, own], x1r, X1L, x_left)
        theirs(1, 1, gr)
        ours(0, 1, xr, 1)
        send(gown.at[xr, bottom, own], x2l.at[bottom], X2R + 1, x_right)
        ours(0, 1, xr, 0, waits=False)
        theirs(1, 2, gl)
        forward_encoded()
        arrived(x1l, X1R)
        add(gown.at[xr, top, own], x1l)
        send(gown.at[xr, top, own], x2l.at[top], X2R, x_right)
        ours(0, 2, xl)
        send(gown.at[xl, top, own], x2r.at[top], X2L, x_left)
        arrived(x1r, X1L)
        add(gown.at[xl, bottom, own], x1r)
        send(gown.at[xl, bottom, own], x2r.at[bottom], X2L + 1, x_left)
        theirs(1, 3, zl)
        ours(0, 3, x)
        for half, rows in ((0, top), (1, bottom)):
            arrived(x2l.at[rows], X2R + half)
            arrived(x2r.at[rows], X2L + half)
        for g in range(4):
            rows = pl.ds(g * ZB, ZB)
            add3(zb.at[g], gown.at[x, rows, own], x2l.at[rows], x2r.at[rows])

        spans = (pl.ds(0, 512), pl.ds(512, 384))

        def cols(sign, part):
            return spans[part if sign == 1 else 1 - part]

        def way(sign):
            return 0 if sign == 1 else 1

        def base(sign, step, part):
            return zb.at[(zl + 5 - step if sign == 1 else zl + 3 + step) % 4, :, cols(sign, part)]

        def received(sign, step, part):
            return zr.at[way(sign), step - 1, :, cols(sign, part)]

        def staged(sign, step, part):
            return zs.at[way(sign), step - 2, :, cols(sign, part)]

        z_chain(1, 0, base, received, staged)
        z_chain(2, 1, base, received, staged)
        encoded_complete()
        heads(0)
        z_chain(2, 0, base, received, staged)
        z_chain(3, 1, base, received, staged)
        heads(1)
        z_chain(3, 0, base, received, staged)
        z_chain(4, 1, base, received, staged)
        heads(2)
        z_chain(4, 0, base, received, staged)
        heads(3)
        z_last(received)
        add3(fin0, zb.at[zl], zr.at[0, 3], zr.at[1, 3])
        send(fin0, fin0, DSW, partner)
        arrived(fin1.at[lower], DSW)
        arrived(fin1.at[upper], DSW + 1)
        for copy in sent:
            copy.wait_send()

    @pl.when(core == 1)
    def _():
        del sent[shared:]
        theirs(0, 0, xf, 0)
        theirs(0, 4, xf, 1)
        theirs(0, 1, xr)
        ours(1, 0, gf)

        def piece(zo):
            return gown.at[(zo + 2) % 4, :, pl.ds(pl.multiple_of(zo // 4 * PIECE, 128), PIECE)]

        def half(ref, sign, part):
            return ref.at[top if (part == 0) == (sign == 1) else bottom]

        def base(sign, step, part):
            return half(piece((z + 5 - step if sign == 1 else z + 3 + step) % 8), sign, part)

        def received(sign, step, part):
            return half(zr1.at[0 if sign == 1 else 1, step - 1], sign, part)

        def hop(sign, step, part):
            i, peer = ((ZUA, ZUB)[part], z_up) if sign == 1 else ((ZDA, ZDB)[part], z_down)
            z_hop(sign, step, part, base, received, base, i + step - 1, peer)

        z_chain(1, 0, base, received, base)
        theirs(0, 2, xl)
        ours(1, 1, gr)
        hop(1, 2, 1)
        hop(1, 2, 0)
        theirs(0, 3, x)
        ours(1, 2, gl)
        hop(-1, 2, 1)
        hop(-1, 2, 0)
        forward_encoded()
        ours(1, 3, zl)
        z_chain(3, 1, base, received, base)
        z_chain(3, 0, base, received, base)
        z_chain(4, 1, base, received, base)
        z_chain(4, 0, base, received, base)
        encoded_complete()
        heads(0)
        heads(1)
        z_last(received)
        add3(zs1, piece(z), zr1.at[0, 3], zr1.at[1, 3])

        def rows_at(xb):
            return zs1.at[pl.ds(pl.multiple_of(xb * ZB, ZB), ZB)]

        send(rows_at(xf), uf, X1R, x_far)
        send(rows_at(xr), u2l, X2R, x_right)
        send(rows_at(xl), u2r, X2L, x_left)
        heads(2)
        arrived(u2l, X2R)
        arrived(u2r, X2L)
        arrived(uf, X1R)
        mine = rows_at(x)
        for r in range(0, ZB, 16):
            rows = pl.ds(r, 16)
            parts = [ref[rows, :].astype(F32) for ref in (mine, u2l, u2r, uf)]
            mine[rows, :] = (parts[0] + parts[1] + parts[2] + parts[3]).astype(BF16)
        send(mine, fin1.at[zh], DUP, z_up2)
        send(mine, fin1.at[zh], DDN, z_down2)
        heads(3)
        arrived(fin1.at[lower], DUP)
        send(fin1.at[lower], fin1.at[lower], DSW, partner)
        arrived(fin1.at[upper], DDN)
        send(fin1.at[upper], fin1.at[upper], DSW + 1, partner)
        arrived(fin0, DSW)
        for copy in sent:
            copy.wait_send()

    for i in range(N // 128):
        if i < 7:
            src = fin0.at[:, pl.ds(i * 128, 128)]
        else:
            src = fin1.at[(i - 7) // 4, :, pl.ds((i - 7) % 4 * 128, 128)]
        cgo[i // OT, :, pl.ds((i % OT) * 128, 128)] = src[...].astype(F32)


def finish(qkv_in, grad_in, qkv_out, grad_out, sem):
    copies = [
        pltpu.make_async_copy(grad_in, grad_out, sem.at[0]),
        pltpu.make_async_copy(qkv_in, qkv_out, sem.at[1]),
    ]
    for copy in copies:
        copy.start()
    for copy in copies:
        copy.wait()


def on_device(block_input, conv_weight, norm_gain, qkv_weight, encoder_grad):
    xin, eg = block_input[0], encoder_grad[0]
    any_ = pl.BlockSpec(memory_space=pl.ANY)
    v = pltpu.VMEM
    qkv, grad = pl.pallas_call(
        kernel,
        name="block",
        out_shape=(jax.ShapeDtypeStruct((R, Q), BF16), jax.ShapeDtypeStruct((KW, ZB, O), F32)),
        in_specs=[pl.BlockSpec(memory_space=pltpu.HBM)] * 5,
        out_specs=(pl.BlockSpec(memory_space=pltpu.VMEM),) * 2,
        scratch_shapes=[
            v((C, T), BF16), v((2, O, 128), BF16), v((2, 16, O), BF16), v((4, 32, O), BF16), v((2, 16, O), BF16),
            v((C, N), BF16), v((4, O), F32), v((4 * O, Q), BF16), v((R, O), BF16),
            v((TC, C), BF16), v((N // 128, T + 16, 128), F32), v((OT, T + 16, 128), F32), v((T, N), BF16),
            v((4, R, O), BF16), v((R, 4 * O), BF16),
            v((4, XB, COLS[1]), BF16), v((4, XB, COLS[1]), BF16), v((4, XB, COLS[1]), BF16),
            v((XB // 2, COLS[0]), BF16), v((XB // 2, COLS[0]), BF16), v((XB, COLS[0]), BF16), v((XB, COLS[0]), BF16),
            v((4, ZB, COLS[0]), BF16), v((2, 4, ZB, COLS[0]), BF16), v((2, 3, ZB, COLS[0]), BF16),
            v((2, 4, XB, PIECE), BF16), v((XB, PIECE), BF16),
            v((ZB, PIECE), BF16), v((ZB, PIECE), BF16), v((ZB, PIECE), BF16),
            v((ZB, COLS[0]), BF16), v((2, ZB, PIECE), BF16),
            pltpu.SemaphoreType.DMA((16,)), pltpu.SemaphoreType.DMA((COPIES,)), pltpu.SemaphoreType.DMA((COPIES,)),
        ],
        compiler_params=pltpu.CompilerParams(collective_id=0, has_side_effects=True, vmem_limit_bytes=50 * 2**20),
    )(*(pltpu.with_memory_space_constraint(a, pltpu.HBM) for a in (xin.T, conv_weight, norm_gain, qkv_weight, eg)))
    qkv, grad = pl.pallas_call(
        finish,
        name="finish",
        out_shape=(jax.ShapeDtypeStruct((R, Q), BF16), jax.ShapeDtypeStruct((KW, ZB, O), F32)),
        in_specs=[any_] * 2,
        out_specs=(any_, any_),
        scratch_shapes=[pltpu.SemaphoreType.DMA((2,))],
        compiler_params=pltpu.CompilerParams(vmem_limit_bytes=4 * 2**20),
    )(qkv, grad)
    return qkv[None], grad.transpose(1, 0, 2)


def solution(mesh):
    return jax.shard_map(
        on_device,
        mesh=mesh,
        in_specs=(
            P("dp", "seq", "mp"),
            P(None, None, "mp"),
            P("mp"),
            P(None, "mp"),
            P("dp", "seq", "mp"),
        ),
        out_specs=(P("dp", "seq", "mp"), P("seq", None, "mp")),
        check_vma=False,
    )
```
